32 devices in a mesh: stripe: 2 (over x), row: 8 (over z, y), col: 2 (over core).
Axes of the slice: x: 2, y: 2, z: 4, core: 2. Of those that a mesh axis runs over, the one named last changes fastest.
Arguments:
- coverage: int32 [4096, 4096], P(('stripe', 'row'), 'col'), parts along dimension 0, may hold values from 0 to 255
- fog_rows: float32 [8, 8], replicated, may hold values from 0.02 to 50
- fog_cols: float32 [16, 16], replicated, may hold values from 0.02 to 50
Outputs:
- dose: float32 [4096, 4096], P(('stripe', 'row'), 'col'), parts along dimension 0
The draws below stay inside these ranges and needn't reach their ends.
There are 2 independent parts, one for each index of `stripe`. The reference program is written for one: setup_inputs(seed, part) draws one part's arguments, and reference() takes and returns one part's arrays. A program takes and returns all parts, laid end to end along the dimension named above; an argument that names none is the same for every part. Nothing has to cross between parts.
All inputs are finite; a program needn't handle non-finite values.
Results may differ from the reference program's by a relative error of at most 0.0001.
Values sent between devices are 32-bit elements; how exact they have to be, the bound alone decides.
No kernel may reach another device: no remote copies, remote signals or barrier semaphores. Data moves between devices by JAX's collectives and lax.ppermute only.
A program may use at most 64 MiB of HBM per device.

```python
import math
import jax
import jax.numpy as jnp
from jax import lax

BS = 32
FB = 256
HALO = 4
BSIG = 16
REACH = 40
PASSES = 2
NR = 2048
NC = 4096
FR = 8
FC = 16


def draw_coverage(key, part):
    first = jax.random.fold_in(key, 11)
    second = jax.random.fold_in(key, 12)
    third = jax.random.fold_in(key, 13)
    pixels = jax.random.randint(first, (NR, NC), 0, 256)
    levels = jax.random.randint(second, (NR // BS, NC // BS), 0, 5)
    regions = jax.random.randint(third, (NR // FB, NC // FB), 1, 4)
    levels_full = jnp.repeat(jnp.repeat(levels, BS, axis=0), BS, axis=1)
    regions_full = jnp.repeat(jnp.repeat(regions, FB, axis=0), FB, axis=1)
    return (pixels * levels_full * regions_full // 12).astype(jnp.int32)


def setup_inputs(seed: int = 0, part: int = 0) -> dict:
    streams_of = jax.random.split(jax.random.key(seed), 4)
    own_keys = jax.random.split(jax.random.fold_in(streams_of[3], part), 4)
    return {
        "coverage": draw_coverage(jax.random.fold_in(jax.random.fold_in(streams_of[3], part), 71), part),
        "fog_rows": jnp.clip(jnp.exp(jax.random.uniform(streams_of[1], (FR, FR), jnp.float32, math.log(0.02), math.log(50.0))), 0.02, 50.0),
        "fog_cols": jnp.clip(jnp.exp(jax.random.uniform(streams_of[2], (FC, FC), jnp.float32, math.log(0.02), math.log(50.0))), 0.02, 50.0),
    }


def fine_taps():
    offsets = jnp.arange(-HALO, HALO + 1).astype(jnp.float32)
    raw = jnp.exp(-0.5 * (offsets / 1.25) ** 2)
    return raw / jnp.sum(raw)

def blur_padded(padded, rows, cols):
    taps = fine_taps()
    across = taps[0] * padded[0:rows, :]
    for index in range(1, 2 * HALO + 1):
        across = across + taps[index] * padded[index:index + rows, :]
    result = taps[0] * across[:, 0:cols]
    for index in range(1, 2 * HALO + 1):
        result = result + taps[index] * across[:, index:index + cols]
    return result

def block_mean(field, size):
    rows, cols = field.shape
    return field.reshape(rows // size, size, cols // size, size).sum(axis=(1, 3)) / (size * size)

def spread_add(field, small, size, weight):
    rows, cols = field.shape
    return (field.reshape(rows // size, size, cols // size, size) + weight * small[:, None, :, None]).reshape(rows, cols)

def gauss_matrix(first, second):
    offsets = (first[:, None] - second[None, :]).astype(jnp.float32)
    values = jnp.exp(-0.5 * (offsets / BSIG) ** 2) / (BSIG * math.sqrt(2.0 * math.pi))
    return jnp.where(jnp.abs(offsets) <= REACH, values, jnp.zeros_like(values))

def reference(coverage, fog_rows, fog_cols):
    cover = coverage.astype(jnp.float32) / 255.0
    dose = jnp.ones((NR, NC), jnp.float32)
    row_norm = fog_rows / lax.optimization_barrier(jnp.sum(fog_rows, axis=1, keepdims=True))
    col_norm = fog_cols / lax.optimization_barrier(jnp.sum(fog_cols, axis=1, keepdims=True))
    coarse_cols = jnp.arange(NC // BS, dtype=jnp.int32)
    coarse_rows = jnp.arange(NR // BS, dtype=jnp.int32)
    across_gauss = gauss_matrix(coarse_cols, coarse_cols)
    down_gauss = gauss_matrix(coarse_rows, coarse_rows)
    high = lax.Precision.HIGHEST
    for step in range(PASSES):
        charge = dose * cover
        fine = blur_padded(jnp.pad(charge, HALO), NR, NC)
        back = block_mean(charge, BS)
        back_h = jnp.dot(back, across_gauss, precision=high)
        back_v = jnp.dot(down_gauss, back_h, precision=high)
        fogmean = block_mean(charge, FB)
        fog = jnp.dot(jnp.dot(row_norm, fogmean, precision=high), col_norm.T, precision=high)
        energy = spread_add(fine, back_v, BS, 0.6)
        energy = spread_add(energy, fog, FB, 0.4) / 2.0
        dose = dose + (0.5 - energy)
    return dose
```

```python
import math

import jax
import jax.numpy as jnp
import numpy as np
from jax import lax
from jax.experimental import pallas as pl
from jax.experimental.pallas import tpu as pltpu
from jax.sharding import PartitionSpec as P

BS = 32
FB = 256
HALO = 4
BSIG = 16
REACH = 40
LANES = 128
HALF = LANES // 2
EDGE = 2 * HALO
PAD = 8
HIGH = lax.Precision.HIGHEST
F32 = jnp.float32
BF16 = jnp.bfloat16
VMEM = pl.BlockSpec(memory_space=pltpu.VMEM)


def fine_taps():
    offsets = np.arange(-HALO, HALO + 1).astype(np.float32)
    raw = np.exp(np.float32(-0.5) * (offsets / np.float32(1.25)) ** 2).astype(np.float32)
    taps = (raw / raw.sum(dtype=np.float32)).astype(np.float32)
    return [float(taps[HALO + k]) for k in range(HALO + 1)]


TAPS = fine_taps()


def iota(shape, dim):
    return lax.broadcasted_iota(jnp.int32, shape, dim)


def tap_of(distance):
    value = jnp.zeros(distance.shape, F32)
    for k in range(HALO + 1):
        value = jnp.where(distance == k, F32(TAPS[k]), value)
    return value


def gauss(offsets):
    off = offsets.astype(F32)
    values = jnp.exp(-0.5 * (off / BSIG) ** 2) / (BSIG * math.sqrt(2.0 * math.pi))
    return jnp.where(jnp.abs(off) <= REACH, values, jnp.zeros_like(values))


def dot(a, b, precision=HIGH):
    return jnp.dot(a, b, precision=precision, preferred_element_type=F32)


def prep_kernel(cells, fog_rows_ref, fog_cols_ref, band_ref, left_ref, own_ref, right_ref):
    back_rows, n_rows, n_cols = cells
    place = lax.axis_index("row") * back_rows
    side = FB // BS
    row = iota((2 * LANES, LANES), 0)
    lane = iota((2 * LANES, LANES), 1)
    tap = tap_of(jnp.abs(row - HALF - lane))
    upper = tap.astype(BF16)
    band_ref[:, :LANES] = upper
    band_ref[:, LANES:] = (tap - upper.astype(F32)).astype(BF16)
    fog_rows = fog_rows_ref[...]
    fog_cols = fog_cols_ref[...]
    kr = fog_rows / jnp.sum(fog_rows, axis=1, keepdims=True)
    kc = fog_cols / jnp.sum(fog_cols, axis=1, keepdims=True)
    fr, fc = kr.shape[0], kc.shape[0]
    spread_r = (iota((fr, n_rows), 1) // side == iota((fr, n_rows), 0)).astype(F32)
    spread_c = (iota((fc, n_cols), 1) // side == iota((fc, n_cols), 0)).astype(F32)
    kr_cols = dot(kr, spread_r)

    def left(count, first):
        here = iota((count, n_rows), 0) + first
        weight = 0.3 * gauss(here - iota((count, n_rows), 1))
        pick = (jnp.clip(iota((count, fr), 0) + first, 0, n_rows - 1) // side == iota((count, fr), 1)).astype(F32)
        fog = dot(pick, kr_cols) * F32(0.2 / (side * side))
        return weight, fog

    left_ref[:, :n_rows], left_ref[:, n_rows:] = left(n_rows, 0)
    ring = own_ref.shape[0]
    own_ref[:, :n_rows], own_ref[:, n_rows:] = left(ring, place - 1)
    right_ref[:, :n_cols] = gauss(iota((n_cols, n_cols), 0) - iota((n_cols, n_cols), 1))
    cols = lax.dot_general(kc, spread_c, (((0,), (0,)), ((), ())), precision=HIGH, preferred_element_type=F32)
    right_ref[:, n_cols:] = lax.dot_general(
        spread_c, cols, (((0,), (0,)), ((), ())), precision=HIGH, preferred_element_type=F32
    )


def row_blur(load):
    acc = F32(TAPS[0]) * load(0)
    for k in range(1, HALO + 1):
        acc = acc + F32(TAPS[k]) * (load(-k) + load(k))
    return acc


def first_kernel(cov_ref, first_ref, second_ref, side_ref, band_ref, cover_ref, fine_ref, sums_ref, shifted, across):
    rows, cols = cov_ref.shape
    tiles = cols // LANES
    ext = rows + 2 * EDGE
    even = lax.rem(lax.axis_index("row"), 2) == 0
    lane = iota((1, LANES), 1)

    def gather(at, span, own):
        top = jnp.where(even, second_ref[:, span], first_ref[:, span])
        low = jnp.where(even, first_ref[:, span], second_ref[:, span])
        cover_ref[at, 0:EDGE, :] = top.astype(F32)
        cover_ref[at, EDGE : EDGE + rows, :] = own.astype(F32)
        cover_ref[at, EDGE + rows :, :] = low.astype(F32)

    for t in range(tiles):
        span = slice(t * LANES, (t + 1) * LANES)
        gather(t, span, cov_ref[:, span])
    gather(tiles, slice(cols, cols + LANES), side_ref[...])
    for t in range(tiles + 1):
        before = pltpu.roll(cover_ref[(t - 1) % (tiles + 1)], HALF, 1)
        here = pltpu.roll(cover_ref[t], HALF, 1)
        tile = jnp.where(lane < HALF, before, here).astype(BF16)
        shifted[t] = tile
        if t == 0:
            shifted[tiles + 1] = tile
    across[:, 0:PAD, :] = jnp.zeros((tiles + 1, PAD, LANES), F32)
    across[:, PAD + ext :, :] = jnp.zeros((tiles + 1, PAD, LANES), F32)

    def columns(t):
        window = jnp.concatenate([shifted[t], shifted[t + 1]], axis=1)
        both = jnp.dot(window, band_ref[...], preferred_element_type=F32)
        across[t, PAD : PAD + ext, :] = both[:, :LANES] + both[:, LANES:]

    cells = rows // BS
    per = LANES // BS
    spot = iota((cells, LANES), 1)
    pick = (spot % per) * BS

    def lanes(x):
        step = BS // 2
        while step:
            x = x + pltpu.roll(x, LANES - step, 1)
            step //= 2
        return jnp.take_along_axis(x, pick, axis=1)

    def down(t):
        fine = row_blur(lambda k: across[t, PAD + k : PAD + k + ext, :])
        fine_ref[t] = fine
        return fine

    sums_ref[...] = jnp.zeros((cells, LANES), F32)
    columns(0)
    for t in range(tiles + 1):
        if t < tiles:
            columns(t + 1)
        fine = down(t)
        if t < tiles:
            cover = cover_ref[t, EDGE : EDGE + rows, :]
            energy = cover * fine[EDGE : EDGE + rows, :]
            c = lanes(cover.reshape(cells, BS, LANES).sum(axis=1))
            f = lanes(energy.reshape(cells, BS, LANES).sum(axis=1))
            where_c = spot // per == t
            where_f = spot // per == t + tiles
            sums_ref[...] = jnp.where(where_c, c, jnp.where(where_f, f, sums_ref[...]))


def second_kernel(order, gathered_ref, left_ref, own_ref, right_ref, band_ref, cover_ref, fine_ref, out_ref, c_all, f_all, ring_ref, last_ref, charge, upper, lower):
    rows, cols = out_ref.shape
    tiles = cols // LANES
    ext = rows + 2 * EDGE
    n_rows, n_cols = c_all.shape
    back_rows = rows // BS
    col = lax.axis_index("col")
    row = lax.axis_index("row")
    lane8 = iota((back_rows, LANES), 1)
    lane = iota((1, LANES), 1)
    for j in range(n_rows // back_rows):
        a = gathered_ref[(2 * j) * back_rows : (2 * j + 1) * back_rows, :]
        b = gathered_ref[(2 * j + 1) * back_rows : (2 * j + 2) * back_rows, :]
        low = jnp.where(col == 0, a, b)
        high = jnp.where(col == 0, b, a)
        at = pl.ds(pl.multiple_of(order(row, j) * back_rows, back_rows), back_rows)
        c_all[at, :] = jnp.where(lane8 < HALF, low, pltpu.roll(high, HALF, 1)) * F32(1.0 / (255.0 * BS * BS))
        f_all[at, :] = jnp.where(lane8 < HALF, pltpu.roll(low, HALF, 1), high) * F32(1.0 / (255.0 * 255.0 * BS * BS))
    right = right_ref[...]

    def both(x):
        part = dot(x, right)
        return jnp.concatenate([part[:, :n_cols], part[:, n_cols:]], axis=0)

    c = c_all[...]
    spread = both(c)
    ring_ref[...] = dot(own_ref[...], spread)
    coarse = dot(left_ref[...], spread)
    back = (1.5 - coarse) * c - 0.5 * f_all[...]
    last_ref[...] = dot(own_ref[...], both(back))

    count = ring_ref.shape[0]
    scale = F32(-0.5 / 255.0)

    def expand(ref, t):
        if t < tiles:
            pick = iota((count, LANES), 1) // BS + (col * (cols // BS) + t * (LANES // BS))
        else:
            pick = jnp.where(iota((count, LANES), 1) < HALF, (col + 1) * (cols // BS), col * (cols // BS) - 1)
        pick = jnp.clip(pick, 0, n_cols - 1)
        parts = [
            jnp.take_along_axis(ref[i : i + 8, :], pick[i : i + 8], axis=1) for i in range(0, count, 8)
        ]
        return jnp.concatenate(parts, axis=0)

    def rows_of(value, first, length):
        return jnp.broadcast_to(value[first : first + 1, :], (length, LANES))

    def dose_of(t):
        ring = expand(ring_ref, t)
        spread = jnp.concatenate(
            [rows_of(ring, 0, EDGE)]
            + [rows_of(ring, 1 + i, BS) for i in range(back_rows)]
            + [rows_of(ring, 1 + back_rows, EDGE)],
            axis=0,
        )
        return 1.5 + scale * fine_ref[t] - spread

    for t in range(tiles + 1):
        charge[t] = dose_of(t) * (cover_ref[t] * F32(1.0 / 255.0))

    def down(t):
        blurred = row_blur(lambda k: charge[t, EDGE + k : EDGE + k + rows, :])
        return pltpu.roll(blurred, HALF, 1)

    before = down(tiles)
    for t in range(tiles + 1):
        here = down(t)
        tile = jnp.where(lane < HALF, before, here)
        top = tile.astype(BF16)
        upper[t] = top
        lower[t] = (tile - top.astype(F32)).astype(BF16)
        before = here
    for t in range(tiles):
        window = jnp.concatenate([upper[t], upper[t + 1]], axis=1)
        rest = jnp.concatenate([lower[t], lower[t + 1]], axis=1)
        twice = jnp.dot(window, band_ref[...], preferred_element_type=F32)
        once = jnp.dot(rest, band_ref[:, :LANES], preferred_element_type=F32)
        fine = twice[:, :LANES] + twice[:, LANES:] + once
        last = expand(last_ref, t)
        spread = jnp.concatenate([rows_of(last, 1 + i, BS) for i in range(back_rows)], axis=0)
        dose = dose_of(t)[EDGE : EDGE + rows, :]
        out_ref[:, t * LANES : (t + 1) * LANES] = dose + (0.5 - 0.5 * fine) - spread


def pairs(count):
    even = [(i, i + 1) for i in range(0, count - 1, 2)]
    odd = [(i, i + 1) for i in range(1, count - 1, 2)]
    return [[p for i, j in some for p in ((i, j), (j, i))] for some in (even, odd)]


def swap(value, axis, some):
    return lax.ppermute(value, axis, some) if some else jnp.zeros_like(value)


def shards(coverage, fog_rows, fog_cols):
    rows, cols = coverage.shape
    row = lax.axis_index("row")
    col = lax.axis_index("col")
    row_count = lax.axis_size("row")
    col_count = lax.axis_size("col")
    tiles = cols // LANES
    back_rows, back_cols = rows // BS, cols // BS
    n_rows, n_cols = back_rows * row_count, back_cols * col_count
    ext = rows + 2 * EDGE
    if col_count != 2 or n_cols != LANES or row_count & (row_count - 1):
        raise ValueError("unsupported mesh")

    band, left, own, right = pl.pallas_call(
        lambda *refs: prep_kernel((back_rows, n_rows, n_cols), *refs),
        out_shape=(
            jax.ShapeDtypeStruct((2 * LANES, 2 * LANES), BF16),
            jax.ShapeDtypeStruct((n_rows, 2 * n_rows), F32),
            jax.ShapeDtypeStruct((16, 2 * n_rows), F32),
            jax.ShapeDtypeStruct((n_cols, 2 * n_cols), F32),
        ),
        in_specs=[VMEM] * 2,
        out_specs=(VMEM,) * 4,
        name="prep",
    )(fog_rows, fog_cols)

    edge = lax.dynamic_slice(coverage, (0, (1 - col) * (cols - LANES)), (rows, LANES)).astype(F32)
    side = swap(edge, "col", pairs(col_count)[0])
    lane = jnp.arange(LANES, dtype=jnp.int32)[None, :]
    side = jnp.where((lane < HALF) == (col == 0), side, 0.0)
    wide = lambda first: jnp.concatenate(
        [
            lax.dynamic_slice(coverage, (first, 0), (EDGE, cols)).astype(F32),
            lax.dynamic_slice(side, (first, 0), (EDGE, LANES)),
        ],
        axis=1,
    )
    odd = row % 2
    even_pairs, odd_pairs = pairs(row_count)
    first = swap(wide((1 - odd) * (rows - EDGE)), "row", even_pairs)
    second = swap(wide(odd * (rows - EDGE)), "row", odd_pairs)

    cover, fine, sums = pl.pallas_call(
        first_kernel,
        out_shape=(
            jax.ShapeDtypeStruct((tiles + 1, ext, LANES), F32),
            jax.ShapeDtypeStruct((tiles + 1, ext, LANES), F32),
            jax.ShapeDtypeStruct((back_rows, LANES), F32),
        ),
        in_specs=[VMEM] * 5,
        out_specs=(VMEM,) * 3,
        scratch_shapes=[
            pltpu.VMEM((tiles + 2, ext, LANES), BF16),
            pltpu.VMEM((tiles + 1, ext + 2 * PAD, LANES), F32),
        ],
        name="first",
    )(coverage, first, second, side, band)

    gathered = jnp.concatenate([sums, lax.ppermute(sums, "col", [(0, 1), (1, 0)])], axis=0)
    bit = 1
    while bit < row_count:
        other = lax.ppermute(gathered, "row", [(i, i ^ bit) for i in range(row_count)])
        gathered = jnp.concatenate([gathered, other], axis=0)
        bit *= 2

    return pl.pallas_call(
        lambda *refs: second_kernel(lambda r, j: r ^ j, *refs),
        out_shape=jax.ShapeDtypeStruct((rows, cols), F32),
        in_specs=[VMEM] * 7,
        out_specs=VMEM,
        scratch_shapes=[
            pltpu.VMEM((n_rows, n_cols), F32),
            pltpu.VMEM((n_rows, n_cols), F32),
            pltpu.VMEM((16, n_cols), F32),
            pltpu.VMEM((16, n_cols), F32),
            pltpu.VMEM((tiles + 1, ext, LANES), F32),
            pltpu.VMEM((tiles + 1, rows, LANES), BF16),
            pltpu.VMEM((tiles + 1, rows, LANES), BF16),
        ],
        name="second",
    )(gathered, left, own, right, band, cover, fine)


def solution(mesh):
    in_specs = (P(("stripe", "row"), "col"), P(), P())
    out_specs = P(("stripe", "row"), "col")
    return jax.shard_map(shards, mesh=mesh, in_specs=in_specs, out_specs=out_specs, check_vma=False)
```

```python
import math

import jax
import jax.numpy as jnp
import numpy as np
from jax import lax
from jax.experimental import pallas as pl
from jax.experimental.pallas import tpu as pltpu
from jax.sharding import PartitionSpec as P

BS = 32
FB = 256
HALO = 4
BSIG = 16
REACH = 40
LANES = 128
HALF = LANES // 2
EDGE = 2 * HALO
PAD = 8
F32 = jnp.float32
BF16 = jnp.bfloat16
VMEM = pl.BlockSpec(memory_space=pltpu.VMEM)


def fine_taps():
    offsets = np.arange(-HALO, HALO + 1).astype(np.float32)
    raw = np.exp(np.float32(-0.5) * (offsets / np.float32(1.25)) ** 2).astype(np.float32)
    taps = (raw / raw.sum(dtype=np.float32)).astype(np.float32)
    return [float(taps[HALO + k]) for k in range(HALO + 1)]


TAPS = fine_taps()


def iota(shape, dim):
    return lax.broadcasted_iota(jnp.int32, shape, dim)


def tap_of(distance):
    value = jnp.zeros(distance.shape, F32)
    for k in range(HALO + 1):
        value = jnp.where(distance == k, F32(TAPS[k]), value)
    return value


def gauss(offsets):
    off = offsets.astype(F32)
    values = jnp.exp(-0.5 * (off / BSIG) ** 2) / (BSIG * math.sqrt(2.0 * math.pi))
    return jnp.where(jnp.abs(off) <= REACH, values, jnp.zeros_like(values))


def halves(x):
    upper = x.astype(BF16)
    return upper, (x - upper.astype(F32)).astype(BF16)


def dot(a, b):
    (ah, al), (bh, bl) = halves(a), halves(b)
    return jnp.dot(
        jnp.concatenate([ah, al, ah], axis=1),
        jnp.concatenate([bh, bh, bl], axis=0),
        preferred_element_type=F32,
    )


def full_dot(a, b, over=1):
    return lax.dot_general(
        a, b, (((over,), (0,)), ((), ())), precision=lax.Precision.HIGHEST, preferred_element_type=F32
    )


def prep(place, fog_rows, fog_cols, left_ref, own_ref, right_ref):
    n_rows = left_ref.shape[0]
    n_cols = right_ref.shape[0]
    side = FB // BS
    kr = fog_rows / jnp.sum(fog_rows, axis=1, keepdims=True)
    kc = fog_cols / jnp.sum(fog_cols, axis=1, keepdims=True)
    fr, fc = kr.shape[0], kc.shape[0]
    spread_r = (iota((fr, n_rows), 1) // side == iota((fr, n_rows), 0)).astype(F32)
    spread_c = (iota((fc, n_cols), 1) // side == iota((fc, n_cols), 0)).astype(F32)
    kr_cols = full_dot(kr, spread_r)

    def left(count, first):
        here = iota((count, n_rows), 0) + first
        weight = 0.3 * gauss(here - iota((count, n_rows), 1))
        cell = jnp.clip(iota((count, fr), 0) + first, 0, n_rows - 1) // side
        pick = (cell == iota((count, fr), 1)).astype(F32)
        return weight, full_dot(pick, kr_cols) * F32(0.2 / (side * side))

    left_ref[:, :n_rows], left_ref[:, n_rows:] = left(n_rows, 0)
    own_ref[:, :n_rows], own_ref[:, n_rows:] = left(own_ref.shape[0], place - 1)
    right_ref[:, :n_cols] = gauss(iota((n_cols, n_cols), 0) - iota((n_cols, n_cols), 1))
    right_ref[:, n_cols:] = full_dot(spread_c, full_dot(kc, spread_c, 0), 0)


def row_blur(load, scale=1.0):
    acc = F32(TAPS[0] * scale) * load(0)
    for k in range(1, HALO + 1):
        acc = acc + F32(TAPS[k] * scale) * (load(-k) + load(k))
    return acc


def fold(parts, pick):
    row = iota((8, LANES), 0)
    step = 4
    while step:
        keep = row % (2 * step) < step
        half = len(parts) // 2
        parts = [
            jnp.where(keep, a + pltpu.roll(a, 8 - step, 0), b + pltpu.roll(b, step, 0))
            for a, b in zip(parts[:half], parts[half:])
        ]
        step //= 2
    x = parts[0]
    step = BS // 2
    while step:
        x = x + pltpu.roll(x, LANES - step, 1)
        step //= 2
    return jnp.take_along_axis(x, pick, axis=1)


def chunks(start, stop, size=64):
    return [(a, min(size, stop - a)) for a in range(start, stop, size)]


def load_kernel(cov_ref, fog_rows_ref, fog_cols_ref, cover_ref, shifted, sums_ref, edge_ref, first_ref, second_ref, band_ref, left_ref, own_ref, right_ref, loaded, cells_of, fog_r, fog_c, sems):
    rows, cols = cov_ref.shape
    tiles = cols // LANES
    pieces = sems.shape[0] - 2
    part = rows // pieces
    copies = [
        pltpu.make_async_copy(
            cov_ref.at[p * part : (p + 1) * part], loaded.at[p * part : (p + 1) * part], sems.at[p]
        )
        for p in range(pieces)
    ]
    fogs = [
        pltpu.make_async_copy(fog_rows_ref, fog_r, sems.at[pieces]),
        pltpu.make_async_copy(fog_cols_ref, fog_c, sems.at[pieces + 1]),
    ]
    for copy in fogs + copies[:2]:
        copy.start()
    tap = tap_of(jnp.abs(iota((2 * LANES, LANES), 0) - HALF - iota((2 * LANES, LANES), 1)))
    band_ref[:, :LANES], band_ref[:, LANES:] = halves(tap)
    for copy in fogs:
        copy.wait()
    place = lax.axis_index("row") * (rows // BS)
    prep(place, fog_r[...], fog_c[...], left_ref, own_ref, right_ref)
    lane = iota((1, LANES), 1)
    per = LANES // BS
    for p, copy in enumerate(copies):
        copy.wait()
        if p + 2 < pieces:
            copies[p + 2].start()
        at = slice(EDGE + p * part, EDGE + (p + 1) * part)
        before = None
        for t in range(tiles):
            value = loaded[p * part : (p + 1) * part, t * LANES : (t + 1) * LANES].astype(F32)
            cover_ref[t, at, :] = value
            here = pltpu.roll(value, HALF, 1)
            if t:
                shifted[t, p * part : (p + 1) * part, :] = jnp.where(lane < HALF, before, here).astype(BF16)
            before = here
            for i in range(part // BS):
                cell = value[i * BS : (i + 1) * BS]
                cells_of[t, p * (part // BS) + i] = sum(cell[b : b + 8] for b in range(8, BS, 8)) + cell[:8]
    edge_ref[...] = cover_ref[(1 - lax.axis_index("col")) * (tiles - 1), EDGE : EDGE + rows, :]
    even = lax.rem(lax.axis_index("row"), 2) == 0
    spot = iota((8, LANES), 1)
    sums = jnp.zeros((8, LANES), F32)
    for t in range(tiles):
        top = cover_ref[t, EDGE : 2 * EDGE, :]
        low = cover_ref[t, rows : rows + EDGE, :]
        first_ref[t] = jnp.where(even, low, top)
        second_ref[t] = jnp.where(even, top, low)
        cell = fold([cells_of[t, i] for i in range(rows // BS)], (spot % per) * BS)
        sums = jnp.where(spot // per == t, cell, sums)
    sums_ref[...] = sums


def inner_kernel(side_ref, band_ref, c_ref, cover_in, shifted, cover_ref, fine_ref, across, sums_ref, ends):
    tiles = cover_ref.shape[0] - 1
    rows = side_ref.shape[0]
    lane = iota((1, LANES), 1)
    cells = rows // BS
    per = LANES // BS
    spot = iota((cells, LANES), 1)
    pick = (spot % per) * BS
    own = slice(EDGE, EDGE + rows)
    value = jnp.where((lane < HALF) == (lax.axis_index("col") == 0), side_ref[...], 0.0)
    cover_ref[tiles, own, :] = value
    side = pltpu.roll(value, HALF, 1)
    ends[0] = jnp.where(lane < HALF, side, pltpu.roll(cover_in[0, own, :], HALF, 1)).astype(BF16)
    ends[1] = jnp.where(lane < HALF, pltpu.roll(cover_in[tiles - 1, own, :], HALF, 1), side).astype(BF16)

    def tile(t):
        return ends.at[0] if t in (0, tiles + 1) else ends.at[1] if t == tiles else shifted.at[t]

    def columns(t):
        left, right = tile(t), tile(t + 1)
        for a, n in chunks(0, rows, 128):
            window = jnp.concatenate([left[a : a + n, :], right[a : a + n, :]], axis=1)
            both = jnp.dot(window, band_ref[...], preferred_element_type=F32)
            across[t, PAD + EDGE + a : PAD + EDGE + a + n, :] = both[:, :LANES] + both[:, LANES:]

    def down(t):
        parts = []
        for a, n in chunks(0, rows, BS):
            low, high = max(a, 8), min(a + n, rows - 8)
            base = PAD + EDGE + low
            fine = row_blur(lambda k: across[t, base + k : base + k + high - low, :])
            fine_ref[t, EDGE + low : EDGE + high, :] = fine
            energy = cover_in[t, EDGE + low : EDGE + high, :] * fine
            parts.append(sum(energy[b : b + 8] for b in range(8, high - low, 8)) + energy[:8])
        if t < tiles:
            f = fold(parts, pick)
            sums_ref[...] = jnp.where(spot // per == t + tiles, f, sums_ref[...])

    sums_ref[...] = c_ref[...]
    columns(0)
    for t in range(tiles + 1):
        if t < tiles:
            columns(t + 1)
        down(t)


def outer_kernel(first_ref, second_ref, band_ref, across_ref, part_ref, cover_in, fine_in, cover_ref, fine_ref, sums_ref, across, window):
    tiles = cover_ref.shape[0] - 1
    ext = cover_ref.shape[1]
    rows = ext - 2 * EDGE
    even = lax.rem(lax.axis_index("row"), 2) == 0
    lane = iota((1, LANES), 1)
    cells = rows // BS
    per = LANES // BS
    spot = iota((cells, LANES), 1)
    pick = (spot % per) * BS
    both = 2 * EDGE
    touches = (lane < HALF) == (lax.axis_index("col") == 0)
    place = lax.axis_index("row")
    alone = (place == 0) | (place == lax.axis_size("row") - 1)

    def halo(t):
        if t < tiles:
            a, b = first_ref[t], second_ref[t]
        else:
            a = jnp.where(even, first_ref[t], first_ref[t + 1])
            b = jnp.where(even, second_ref[t + 1], second_ref[t])
            a, b = jnp.where(touches, a, 0.0), jnp.where(touches, b, 0.0)
        b = jnp.where(alone, 0.0, b)
        top = jnp.where(even, b, a)
        low = jnp.where(even, a, b)
        cover_ref[t, 0:EDGE, :] = top
        cover_ref[t, EDGE + rows :, :] = low
        return pltpu.roll(jnp.concatenate([top, low], axis=0), HALF, 1)

    before = halo(tiles)
    first = before
    for t in range(tiles + 1):
        here = halo(t) if t < tiles else first
        tile = jnp.where(lane < HALF, before, here).astype(BF16)
        window[t * both : (t + 1) * both, :LANES] = tile
        at = t - 1 if t else tiles
        window[at * both : (at + 1) * both, LANES:] = tile
        before = here
    twice = jnp.dot(window[...], band_ref[...], preferred_element_type=F32)
    once = twice[:, :LANES] + twice[:, LANES:]
    reach = 2 * PAD + 2 * EDGE
    total = jnp.zeros((cells, LANES), F32)
    for t in range(tiles + 1):
        across[t, 0:PAD, :] = jnp.zeros((PAD, LANES), F32)
        across[t, PAD : PAD + EDGE, :] = once[t * both : t * both + EDGE]
        across[t, PAD + EDGE : reach, :] = across_ref[t, PAD + EDGE : reach, :]
        low = reach
        across[t, low : low + PAD + EDGE, :] = across_ref[t, ext - PAD - EDGE : ext, :]
        across[t, low + PAD + EDGE : low + PAD + 2 * EDGE, :] = once[t * both + EDGE : (t + 1) * both]
        across[t, low + PAD + 2 * EDGE :, :] = jnp.zeros((PAD, LANES), F32)
        top = row_blur(lambda k: across[t, PAD + k : PAD + k + EDGE + 8, :])
        base = low + 8
        bot = row_blur(lambda k: across[t, base + k : base + k + EDGE + 8, :])
        fine_ref[t, 0 : EDGE + 8, :] = top
        fine_ref[t, EDGE + rows - 8 :, :] = bot
        if t < tiles:
            zero = jnp.zeros((8, LANES), F32)
            a = top[EDGE:] * cover_ref[t, EDGE : EDGE + 8, :]
            b = bot[:8] * cover_ref[t, EDGE + rows - 8 : EDGE + rows, :]
            total = jnp.where(spot // per == t + tiles, fold([a] + [zero] * (cells - 2) + [b], pick), total)
    sums_ref[...] = part_ref[...] + total


def spread_kernel(cover_ref, blurred_ref, above_ref, below_ref):
    tiles, ext = cover_ref.shape[0] - 1, cover_ref.shape[1]
    rows = ext - 2 * EDGE
    scale = 0.5 / 255.0
    row = iota((8, LANES), 0)
    for t in range(tiles + 1):
        for a, n in chunks(0, rows):
            blurred_ref[t, a : a + n, :] = row_blur(lambda k: cover_ref[t, EDGE + a + k : EDGE + a + k + n, :], scale)
        for i in range(rows // BS):
            top = EDGE + i * BS
            low = top + BS - 8
            above = jnp.zeros((8, LANES), F32)
            below = jnp.zeros((8, LANES), F32)
            for k in range(1, HALO + 1):
                tap = F32(TAPS[k] * scale)
                above = above + jnp.where(row < k, tap * cover_ref[t, top - k : top - k + 8, :], 0.0)
                below = below + jnp.where(row >= 8 - k, tap * cover_ref[t, low + k : low + k + 8, :], 0.0)
            above_ref[t, i] = above
            below_ref[t, i] = below


def first_dose_kernel(cover_ref, fine_ref, after_ref, dose_ref, blurred_ref, charge):
    del after_ref
    tiles, ext = cover_ref.shape[0] - 1, cover_ref.shape[1]
    rows = ext - 2 * EDGE
    for t in range(tiles + 1):
        for a, n in [(0, EDGE)] + [(EDGE + a, n) for a, n in chunks(0, rows)] + [(EDGE + rows, EDGE)]:
            dose = 2.0 - F32(0.5 / 255.0) * fine_ref[t, a : a + n, :]
            if t < tiles and EDGE <= a < EDGE + rows:
                dose_ref[t, a - EDGE : a - EDGE + n, :] = dose
            charge[t, a : a + n, :] = (dose - 0.5) * cover_ref[t, a : a + n, :]
        for a, n in chunks(0, rows):
            blurred_ref[t, a : a + n, :] = row_blur(
                lambda k: charge[t, EDGE + a + k : EDGE + a + k + n, :], 0.5 / 255.0
            )


def last_kernel(gathered_ref, left_ref, own_ref, right_ref, band_ref, dose_ref, charge_ref, blurred_ref, above_ref, below_ref, out_ref, c_all, f_all, ring_ref, last_ref, upper, lower, turned, ends, staged, sems):
    rows, cols = out_ref.shape
    tiles = cols // LANES
    n_rows, n_cols = c_all.shape
    cells = rows // BS
    col = lax.axis_index("col")
    row = lax.axis_index("row")
    lane8 = iota((cells, LANES), 1)
    lane = iota((1, LANES), 1)
    count = n_rows // cells
    for j in range(count):
        mine = gathered_ref[j * cells : (j + 1) * cells, :]
        other = gathered_ref[(count + j) * cells : (count + j + 1) * cells, :]
        here = col == bin(j).count("1") % 2
        low = jnp.where(here, mine, other)
        high = jnp.where(here, other, mine)
        at = pl.ds(pl.multiple_of((row ^ j) * cells, cells), cells)
        c_all[at, :] = jnp.where(lane8 < HALF, low, pltpu.roll(high, HALF, 1)) * F32(1.0 / (255.0 * BS * BS))
        f_all[at, :] = jnp.where(lane8 < HALF, pltpu.roll(low, HALF, 1), high) * F32(1.0 / (255.0 * 255.0 * BS * BS))
    right = right_ref[...]

    def both(x):
        part = dot(x, right)
        return jnp.concatenate([part[:, :n_cols], part[:, n_cols:]], axis=0)

    c = c_all[...]
    spread = both(c)
    ring_ref[...] = dot(own_ref[...], spread)
    coarse = dot(left_ref[...], spread)
    back = (1.5 - coarse) * c - 0.5 * f_all[...]
    last_ref[...] = dot(own_ref[...], both(back))
    ring = ring_ref.shape[0]

    def expand(ref, t):
        if t < tiles:
            pick = iota((ring, LANES), 1) // BS + (col * (cols // BS) + t * (LANES // BS))
        else:
            pick = jnp.where(iota((ring, LANES), 1) < HALF, (col + 1) * (cols // BS), col * (cols // BS) - 1)
        pick = jnp.clip(pick, 0, n_cols - 1)
        parts = [jnp.take_along_axis(ref[i : i + 8, :], pick[i : i + 8], axis=1) for i in range(0, ring, 8)]
        return jnp.concatenate(parts, axis=0)

    def charge(t):
        value = expand(ring_ref, t)
        for i in range(cells):
            here = value[1 + i : 2 + i, :]
            up = value[i : 1 + i, :] - here
            down = value[2 + i : 3 + i, :] - here
            at = i * BS
            some = charge_ref[t, at : at + BS, :] - here * blurred_ref[t, at : at + BS, :]
            some = jnp.concatenate(
                [some[:8] - up * above_ref[t, i], some[8 : BS - 8], some[BS - 8 :] - down * below_ref[t, i]], axis=0
            )
            turned[t % 2, at : at + BS, :] = pltpu.roll(some, HALF, 1)

    def copy(g):
        span = slice(2 * g * LANES, 2 * (g + 1) * LANES)
        return pltpu.make_async_copy(staged.at[:, span], out_ref.at[:, span], sems.at[g])

    def finish(t):
        coarse = expand(ring_ref, t)[1 : 1 + cells] + expand(last_ref, t)[1 : 1 + cells]
        for a, n in chunks(0, rows, 128):
            at = slice(a, a + n)
            window = jnp.concatenate([upper[t, at, :], upper[t + 1, at, :]], axis=1)
            rest = jnp.concatenate([lower[t, at, :], lower[t + 1, at, :]], axis=1)
            twice = jnp.dot(window, band_ref[...], preferred_element_type=F32)
            once = jnp.dot(rest, band_ref[:, :LANES], preferred_element_type=F32)
            fine = twice[:, :LANES] + twice[:, LANES:] + once
            for i in range(n // BS):
                cell = slice(a + i * BS, a + (i + 1) * BS)
                value = dose_ref[t, cell, :] - fine[i * BS : (i + 1) * BS] - coarse[a // BS + i : a // BS + i + 1, :]
                staged[cell, t * LANES : (t + 1) * LANES] = value
        if t % 2:
            copy(t // 2).start()

    charge(tiles)
    first = tiles % 2
    for t in range(tiles + 1):
        if t == 0:
            ends[...] = turned[first]
        if t < tiles:
            charge(t)
        for a, n in chunks(0, rows):
            at = slice(a, a + n)
            before = turned[(t - 1) % 2, at, :] if t else ends[at, :]
            here = turned[t % 2, at, :] if t < tiles else ends[at, :]
            upper[t, at, :], lower[t, at, :] = halves(jnp.where(lane < HALF, before, here))
        if t:
            finish(t - 1)
    for g in range(tiles // 2):
        copy(g).wait()


def shards(coverage, fog_rows, fog_cols):
    rows, cols = coverage.shape
    row_count = lax.axis_size("row")
    col_count = lax.axis_size("col")
    tiles = cols // LANES
    back_rows, back_cols = rows // BS, cols // BS
    n_rows, n_cols = back_rows * row_count, back_cols * col_count
    ext = rows + 2 * EDGE
    if col_count != 2 or n_cols != LANES or row_count & (row_count - 1):
        raise ValueError("unsupported mesh")

    def move(value, target):
        both = [(r, c) for r in range(row_count) for c in range(col_count)]
        flat = [(r * col_count + c, target(r, c)) for r, c in both]
        return lax.ppermute(value, ("row", "col"), [(i, r * col_count + c) for i, (r, c) in flat])

    def shape(*dims, dtype=F32):
        return jax.ShapeDtypeStruct(dims, dtype)

    def call(kernel, outs, ins, *args, scratch=(), mib=16, name=None, aliases={}, ops=1):
        return pl.pallas_call(
            kernel,
            out_shape=outs,
            in_specs=ins,
            out_specs=(VMEM,) * len(outs),
            scratch_shapes=list(scratch),
            input_output_aliases=aliases,
            compiler_params=pltpu.CompilerParams(vmem_limit_bytes=mib << 20),
            cost_estimate=pl.CostEstimate(flops=ops * rows * cols, bytes_accessed=ops * rows * cols, transcendentals=0),
            name=name,
        )(*args)

    wide = shape(tiles + 1, ext, LANES)
    own_tiles = shape(tiles + 1, rows, LANES)
    hbm = pl.BlockSpec(memory_space=pltpu.HBM)
    in_hbm = [pltpu.with_memory_space_constraint(x, pltpu.HBM) for x in (coverage, fog_rows, fog_cols)]
    cover, shifted, c_sums, edge, first_rows, second_rows, band, left, own, right = call(
        load_kernel,
        (
            wide,
            shape(tiles, rows, LANES, dtype=BF16),
            shape(back_rows, LANES),
            shape(rows, LANES),
            shape(tiles, EDGE, LANES),
            shape(tiles, EDGE, LANES),
            shape(2 * LANES, 2 * LANES, dtype=BF16),
            shape(n_rows, 2 * n_rows),
            shape(16, 2 * n_rows),
            shape(n_cols, 2 * n_cols),
        ),
        [hbm] * 3,
        *in_hbm,
        scratch=[
            pltpu.VMEM((rows, cols), jnp.int32),
            pltpu.VMEM((tiles, back_rows, 8, LANES), F32),
            pltpu.VMEM(fog_rows.shape, F32),
            pltpu.VMEM(fog_cols.shape, F32),
            pltpu.SemaphoreType.DMA((4 + 2,)),
        ],
        name="load",
    )

    side = move(edge, lambda r, c: (r, 1 - c))
    corners = [side[None, :EDGE], side[None, rows - EDGE :]]

    first = move(jnp.concatenate([first_rows] + corners, axis=0), lambda r, c: (r ^ 1, c))
    second = move(
        jnp.concatenate([second_rows] + corners, axis=0),
        lambda r, c: (r, 1 - c) if r in (0, row_count - 1) else ((r + 1, c) if r % 2 else (r - 1, c)),
    )
    cover, fine, across, part = call(
        inner_kernel,
        (wide, wide, shape(tiles + 1, ext + 2 * PAD, LANES), shape(back_rows, LANES)),
        [VMEM] * 5,
        side,
        band,
        c_sums,
        cover,
        shifted,
        scratch=[pltpu.VMEM((2, rows, LANES), BF16)],
        aliases={3: 0},
        ops=64,
        name="inner",
    )
    cover, fine, sums = call(
        outer_kernel,
        (wide, wide, shape(back_rows, LANES)),
        [VMEM] * 7,
        first,
        second,
        band,
        across,
        part,
        cover,
        fine,
        scratch=[
            pltpu.VMEM((tiles + 1, 4 * PAD + 4 * EDGE, LANES), F32),
            pltpu.VMEM(((tiles + 1) * 2 * EDGE, 2 * LANES), BF16),
        ],
        aliases={5: 0, 6: 1},
        name="outer",
    )

    few = shape(tiles + 1, back_rows, 8, LANES)
    blurred, above, below = call(
        spread_kernel, (own_tiles, few, few), [VMEM], cover, mib=4, ops=32, name="spread"
    )
    gathered = sums
    bit = 1
    while bit < row_count:
        other = move(gathered, lambda r, c: (r ^ bit, 1 - c))
        gathered = jnp.concatenate([gathered, other], axis=0)
        if bit == 1:
            dose, charge = call(
                first_dose_kernel,
                (shape(tiles, rows, LANES), own_tiles),
                [VMEM] * 3,
                cover,
                fine,
                gathered,
                scratch=[pltpu.VMEM((tiles + 1, ext, LANES), F32)],
                mib=8,
                ops=32,
                name="dose",
            )
        bit *= 2
    gathered = jnp.concatenate([gathered, move(gathered, lambda r, c: (r, 1 - c))], axis=0)

    return pl.pallas_call(
        last_kernel,
        out_shape=shape(rows, cols),
        in_specs=[VMEM] * 10,
        out_specs=pl.BlockSpec(memory_space=pltpu.HBM),
        scratch_shapes=[
            pltpu.VMEM((n_rows, n_cols), F32),
            pltpu.VMEM((n_rows, n_cols), F32),
            pltpu.VMEM((16, n_cols), F32),
            pltpu.VMEM((16, n_cols), F32),
            pltpu.VMEM((tiles + 1, rows, LANES), BF16),
            pltpu.VMEM((tiles + 1, rows, LANES), BF16),
            pltpu.VMEM((2, rows, LANES), F32),
            pltpu.VMEM((rows, LANES), F32),
            pltpu.VMEM((rows, cols), F32),
            pltpu.SemaphoreType.DMA((tiles // 2,)),
        ],
        compiler_params=pltpu.CompilerParams(vmem_limit_bytes=16 << 20),
        name="last",
    )(gathered, left, own, right, band, dose, charge, blurred, above, below)


def solution(mesh):
    in_specs = (P(("stripe", "row"), "col"), P(), P())
    out_specs = P(("stripe", "row"), "col")
    return jax.shard_map(shards, mesh=mesh, in_specs=in_specs, out_specs=out_specs, check_vma=False)
```

```python
import math

import jax
import jax.numpy as jnp
import numpy as np
from jax import lax
from jax.experimental import pallas as pl
from jax.experimental.pallas import tpu as pltpu
from jax.sharding import PartitionSpec as P

BS = 32
FB = 256
HALO = 4
BSIG = 16
REACH = 40
LANES = 128
HALF = LANES // 2
EDGE = 2 * HALO
PAD = 8
F32 = jnp.float32
BF16 = jnp.bfloat16
VMEM = pl.BlockSpec(memory_space=pltpu.VMEM)


def fine_taps():
    offsets = np.arange(-HALO, HALO + 1).astype(np.float32)
    raw = np.exp(np.float32(-0.5) * (offsets / np.float32(1.25)) ** 2).astype(np.float32)
    taps = (raw / raw.sum(dtype=np.float32)).astype(np.float32)
    return [float(taps[HALO + k]) for k in range(HALO + 1)]


TAPS = fine_taps()


def iota(shape, dim):
    return lax.broadcasted_iota(jnp.int32, shape, dim)


def tap_of(distance):
    value = jnp.zeros(distance.shape, F32)
    for k in range(HALO + 1):
        value = jnp.where(distance == k, F32(TAPS[k]), value)
    return value


def gauss(offsets):
    off = offsets.astype(F32)
    values = jnp.exp(-0.5 * (off / BSIG) ** 2) / (BSIG * math.sqrt(2.0 * math.pi))
    return jnp.where(jnp.abs(off) <= REACH, values, jnp.zeros_like(values))


def halves(x):
    upper = x.astype(BF16)
    return upper, (x - upper.astype(F32)).astype(BF16)


def dot(a, b):
    (ah, al), (bh, bl) = halves(a), halves(b)
    return jnp.dot(
        jnp.concatenate([ah, al, ah], axis=1),
        jnp.concatenate([bh, bh, bl], axis=0),
        preferred_element_type=F32,
    )


def full_dot(a, b, over=1):
    return lax.dot_general(
        a, b, (((over,), (0,)), ((), ())), precision=lax.Precision.HIGHEST, preferred_element_type=F32
    )


def prep(place, fog_rows, fog_cols, left_ref, own_ref, right_ref):
    n_rows = left_ref.shape[0]
    n_cols = right_ref.shape[0]
    side = FB // BS
    kr = fog_rows / jnp.sum(fog_rows, axis=1, keepdims=True)
    kc = fog_cols / jnp.sum(fog_cols, axis=1, keepdims=True)
    fr, fc = kr.shape[0], kc.shape[0]
    spread_r = (iota((fr, n_rows), 1) // side == iota((fr, n_rows), 0)).astype(F32)
    spread_c = (iota((fc, n_cols), 1) // side == iota((fc, n_cols), 0)).astype(F32)
    kr_cols = full_dot(kr, spread_r)

    def left(count, first):
        here = iota((count, n_rows), 0) + first
        weight = 0.3 * gauss(here - iota((count, n_rows), 1))
        cell = jnp.clip(iota((count, fr), 0) + first, 0, n_rows - 1) // side
        pick = (cell == iota((count, fr), 1)).astype(F32)
        return weight, full_dot(pick, kr_cols) * F32(0.2 / (side * side))

    left_ref[:, :n_rows], left_ref[:, n_rows:] = left(n_rows, 0)
    own_ref[:, :n_rows], own_ref[:, n_rows:] = left(own_ref.shape[0], place - 1)
    right_ref[:, :n_cols] = gauss(iota((n_cols, n_cols), 0) - iota((n_cols, n_cols), 1))
    right_ref[:, n_cols:] = full_dot(spread_c, full_dot(kc, spread_c, 0), 0)


def row_blur(load, scale=1.0):
    acc = F32(TAPS[0] * scale) * load(0)
    for k in range(1, HALO + 1):
        acc = acc + F32(TAPS[k] * scale) * (load(-k) + load(k))
    return acc


def fold(parts, pick):
    row = iota((8, LANES), 0)
    step = 4
    while step:
        keep = row % (2 * step) < step
        half = len(parts) // 2
        parts = [
            jnp.where(keep, a + pltpu.roll(a, 8 - step, 0), b + pltpu.roll(b, step, 0))
            for a, b in zip(parts[:half], parts[half:])
        ]
        step //= 2
    x = parts[0]
    step = BS // 2
    while step:
        x = x + pltpu.roll(x, LANES - step, 1)
        step //= 2
    return jnp.take_along_axis(x, pick, axis=1)


def chunks(start, stop, size=64):
    return [(a, min(size, stop - a)) for a in range(start, stop, size)]


def edges_kernel(cov_ref, edge_ref, first_ref, second_ref, tile, strips, sems):
    rows, cols = cov_ref.shape
    tiles = cols // LANES
    odd = lax.rem(lax.axis_index("row"), 2)
    over = pl.ds(pl.multiple_of((1 - lax.axis_index("col")) * (cols - LANES), LANES), LANES)
    copies = [pltpu.make_async_copy(cov_ref.at[:, over], tile, sems.at[0])]
    for i, start in enumerate((1 - odd, odd)):
        span = pl.ds(pl.multiple_of(start * (rows - EDGE), EDGE), EDGE)
        copies.append(pltpu.make_async_copy(cov_ref.at[span], strips.at[i], sems.at[1 + i]))
    for copy in copies:
        copy.start()
    for copy in copies:
        copy.wait()
    edge_ref[...] = tile[...].astype(F32)
    for t in range(tiles):
        first_ref[t] = strips[0, :, t * LANES : (t + 1) * LANES].astype(F32)
        second_ref[t] = strips[1, :, t * LANES : (t + 1) * LANES].astype(F32)


def load_kernel(cov_ref, fog_rows_ref, fog_cols_ref, side_ref, cover_ref, window, sums_ref, band_ref, left_ref, own_ref, right_ref, loaded, cells_of, fog_r, fog_c, sems):
    rows, cols = cov_ref.shape
    tiles = cols // LANES
    pieces = sems.shape[0] - 2
    part = rows // pieces
    copies = [
        pltpu.make_async_copy(
            cov_ref.at[p * part : (p + 1) * part], loaded.at[p * part : (p + 1) * part], sems.at[p]
        )
        for p in range(pieces)
    ]
    fogs = [
        pltpu.make_async_copy(fog_rows_ref, fog_r, sems.at[pieces]),
        pltpu.make_async_copy(fog_cols_ref, fog_c, sems.at[pieces + 1]),
    ]
    ahead = 3
    for copy in fogs + copies[:ahead]:
        copy.start()
    tap = tap_of(jnp.abs(iota((2 * LANES, LANES), 0) - HALF - iota((2 * LANES, LANES), 1)))
    band_ref[:, :LANES], band_ref[:, LANES:] = halves(tap)
    for copy in fogs:
        copy.wait()
    place = lax.axis_index("row") * (rows // BS)
    prep(place, fog_r[...], fog_c[...], left_ref, own_ref, right_ref)
    lane = iota((1, LANES), 1)
    per = LANES // BS
    touches = (lane < HALF) == (lax.axis_index("col") == 0)

    def put(t, at, value):
        window[t, at, :LANES] = value
        window[(t - 1) % (tiles + 1), at, LANES:] = value

    for p, copy in enumerate(copies):
        copy.wait()
        if p + ahead < pieces:
            copies[p + ahead].start()
        at = slice(p * part, (p + 1) * part)
        side = jnp.where(touches, side_ref[at, :], 0.0)
        cover_ref[tiles, EDGE + p * part : EDGE + (p + 1) * part, :] = side
        side = pltpu.roll(side, HALF, 1)
        before = side
        for t in range(tiles):
            value = loaded[at, t * LANES : (t + 1) * LANES].astype(F32)
            cover_ref[t, EDGE + p * part : EDGE + (p + 1) * part, :] = value
            here = pltpu.roll(value, HALF, 1)
            put(t, at, jnp.where(lane < HALF, before, here).astype(BF16))
            before = here
            for i in range(part // BS):
                cell = value[i * BS : (i + 1) * BS]
                cells_of[t, p * (part // BS) + i] = sum(cell[b : b + 8] for b in range(8, BS, 8)) + cell[:8]
        put(tiles, at, jnp.where(lane < HALF, before, side).astype(BF16))
    spot = iota((8, LANES), 1)
    sums = jnp.zeros((8, LANES), F32)
    for t in range(tiles):
        cell = fold([cells_of[t, i] for i in range(rows // BS)], (spot % per) * BS)
        sums = jnp.where(spot // per == t, cell, sums)
    sums_ref[...] = sums


def inner_kernel(window, band_ref, c_ref, cover_in, fine_ref, across, sums_ref):
    tiles = cover_in.shape[0] - 1
    rows = window.shape[1]
    cells = rows // BS
    per = LANES // BS
    spot = iota((cells, LANES), 1)
    pick = (spot % per) * BS

    def columns(t, count):
        part = window[t : t + count].reshape(count * rows, 2 * LANES)
        both = jnp.dot(part, band_ref[...], preferred_element_type=F32)
        for i in range(count):
            mine = both[i * rows : (i + 1) * rows]
            across[t + i, PAD + EDGE : PAD + EDGE + rows, :] = mine[:, :LANES] + mine[:, LANES:]

    def down(t):
        parts = []
        for a, n in chunks(0, rows, BS):
            low, high = max(a, 8), min(a + n, rows - 8)
            base = PAD + EDGE + low
            fine = row_blur(lambda k: across[t, base + k : base + k + high - low, :])
            fine_ref[t, EDGE + low : EDGE + high, :] = fine
            energy = cover_in[t, EDGE + low : EDGE + high, :] * fine
            parts.append(sum(energy[b : b + 8] for b in range(8, high - low, 8)) + energy[:8])
        if t < tiles:
            f = fold(parts, pick)
            sums_ref[...] = jnp.where(spot // per == t + tiles, f, sums_ref[...])

    sums_ref[...] = c_ref[...]
    groups = chunks(0, tiles + 1, 2)
    columns(*groups[0])
    for g, (start, count) in enumerate(groups):
        if g + 1 < len(groups):
            columns(*groups[g + 1])
        for t in range(start, start + count):
            down(t)


def outer_kernel(first_ref, second_ref, band_ref, across_ref, part_ref, cover_in, fine_in, cover_ref, fine_ref, sums_ref, across, window):
    tiles = cover_ref.shape[0] - 1
    ext = cover_ref.shape[1]
    rows = ext - 2 * EDGE
    even = lax.rem(lax.axis_index("row"), 2) == 0
    lane = iota((1, LANES), 1)
    cells = rows // BS
    per = LANES // BS
    spot = iota((cells, LANES), 1)
    pick = (spot % per) * BS
    both = 2 * EDGE
    touches = (lane < HALF) == (lax.axis_index("col") == 0)
    place = lax.axis_index("row")
    alone = (place == 0) | (place == lax.axis_size("row") - 1)

    def halo(t):
        if t < tiles:
            a, b = first_ref[t], second_ref[t]
        else:
            a = jnp.where(even, first_ref[t], first_ref[t + 1])
            b = jnp.where(even, second_ref[t + 1], second_ref[t])
            a, b = jnp.where(touches, a, 0.0), jnp.where(touches, b, 0.0)
        b = jnp.where(alone, 0.0, b)
        top = jnp.where(even, b, a)
        low = jnp.where(even, a, b)
        cover_ref[t, 0:EDGE, :] = top
        cover_ref[t, EDGE + rows :, :] = low
        return pltpu.roll(jnp.concatenate([top, low], axis=0), HALF, 1)

    before = halo(tiles)
    first = before
    for t in range(tiles + 1):
        here = halo(t) if t < tiles else first
        tile = jnp.where(lane < HALF, before, here).astype(BF16)
        window[t * both : (t + 1) * both, :LANES] = tile
        at = t - 1 if t else tiles
        window[at * both : (at + 1) * both, LANES:] = tile
        before = here
    twice = jnp.dot(window[...], band_ref[...], preferred_element_type=F32)
    once = twice[:, :LANES] + twice[:, LANES:]
    reach = 2 * PAD + 2 * EDGE
    total = jnp.zeros((cells, LANES), F32)
    for t in range(tiles + 1):
        across[t, 0:PAD, :] = jnp.zeros((PAD, LANES), F32)
        across[t, PAD : PAD + EDGE, :] = once[t * both : t * both + EDGE]
        across[t, PAD + EDGE : reach, :] = across_ref[t, PAD + EDGE : reach, :]
        low = reach
        across[t, low : low + PAD + EDGE, :] = across_ref[t, ext - PAD - EDGE : ext, :]
        across[t, low + PAD + EDGE : low + PAD + 2 * EDGE, :] = once[t * both + EDGE : (t + 1) * both]
        across[t, low + PAD + 2 * EDGE :, :] = jnp.zeros((PAD, LANES), F32)
        top = row_blur(lambda k: across[t, PAD + k : PAD + k + EDGE + 8, :])
        base = low + 8
        bot = row_blur(lambda k: across[t, base + k : base + k + EDGE + 8, :])
        fine_ref[t, 0 : EDGE + 8, :] = top
        fine_ref[t, EDGE + rows - 8 :, :] = bot
        if t < tiles:
            zero = jnp.zeros((8, LANES), F32)
            a = top[EDGE:] * cover_ref[t, EDGE : EDGE + 8, :]
            b = bot[:8] * cover_ref[t, EDGE + rows - 8 : EDGE + rows, :]
            total = jnp.where(spot // per == t + tiles, fold([a] + [zero] * (cells - 2) + [b], pick), total)
    sums_ref[...] = part_ref[...] + total


def spread_kernel(cover_ref, after_ref, blurred_ref, above_ref, below_ref):
    del after_ref
    tiles, ext = cover_ref.shape[0] - 1, cover_ref.shape[1]
    rows = ext - 2 * EDGE
    scale = 0.5 / 255.0
    row = iota((8, LANES), 0)
    for t in range(tiles + 1):
        for a, n in chunks(0, rows):
            blurred_ref[t, a : a + n, :] = row_blur(lambda k: cover_ref[t, EDGE + a + k : EDGE + a + k + n, :], scale)
        for i in range(rows // BS):
            top = EDGE + i * BS
            low = top + BS - 8
            above = jnp.zeros((8, LANES), F32)
            below = jnp.zeros((8, LANES), F32)
            for k in range(1, HALO + 1):
                tap = F32(TAPS[k] * scale)
                above = above + jnp.where(row < k, tap * cover_ref[t, top - k : top - k + 8, :], 0.0)
                below = below + jnp.where(row >= 8 - k, tap * cover_ref[t, low + k : low + k + 8, :], 0.0)
            above_ref[t, i] = above
            below_ref[t, i] = below


def first_dose_kernel(cover_ref, fine_ref, after_ref, dose_ref, blurred_ref, charge):
    del after_ref
    tiles, ext = cover_ref.shape[0] - 1, cover_ref.shape[1]
    rows = ext - 2 * EDGE
    for t in range(tiles + 1):
        for a, n in [(0, EDGE)] + [(EDGE + a, n) for a, n in chunks(0, rows)] + [(EDGE + rows, EDGE)]:
            dose = 2.0 - F32(0.5 / 255.0) * fine_ref[t, a : a + n, :]
            if t < tiles and EDGE <= a < EDGE + rows:
                dose_ref[t, a - EDGE : a - EDGE + n, :] = dose
            charge[t, a : a + n, :] = (dose - 0.5) * cover_ref[t, a : a + n, :]
        for a, n in chunks(0, rows):
            blurred_ref[t, a : a + n, :] = row_blur(
                lambda k: charge[t, EDGE + a + k : EDGE + a + k + n, :], 0.5 / 255.0
            )


def last_kernel(gathered_ref, left_ref, own_ref, right_ref, band_ref, dose_ref, charge_ref, blurred_ref, above_ref, below_ref, out_ref, c_all, f_all, ring_ref, last_ref, window, turned, ends, staged, sems):
    rows, cols = out_ref.shape
    tiles = cols // LANES
    n_rows, n_cols = c_all.shape
    cells = rows // BS
    col = lax.axis_index("col")
    row = lax.axis_index("row")
    lane8 = iota((cells, LANES), 1)
    lane = iota((1, LANES), 1)
    count = n_rows // cells
    for j in range(count):
        mine = gathered_ref[j * cells : (j + 1) * cells, :]
        other = gathered_ref[(count + j) * cells : (count + j + 1) * cells, :]
        here = col == bin(j).count("1") % 2
        low = jnp.where(here, mine, other)
        high = jnp.where(here, other, mine)
        at = pl.ds(pl.multiple_of((row ^ j) * cells, cells), cells)
        c_all[at, :] = jnp.where(lane8 < HALF, low, pltpu.roll(high, HALF, 1)) * F32(1.0 / (255.0 * BS * BS))
        f_all[at, :] = jnp.where(lane8 < HALF, pltpu.roll(low, HALF, 1), high) * F32(1.0 / (255.0 * 255.0 * BS * BS))
    right = right_ref[...]

    def both(x):
        part = dot(x, right)
        return jnp.concatenate([part[:, :n_cols], part[:, n_cols:]], axis=0)

    c = c_all[...]
    spread = both(c)
    ring_ref[...] = dot(own_ref[...], spread)
    coarse = dot(left_ref[...], spread)
    back = (1.5 - coarse) * c - 0.5 * f_all[...]
    last_ref[...] = dot(own_ref[...], both(back))

    ring = ring_ref.shape[0]

    def expand(ref, t):
        if t < tiles:
            pick = iota((ring, LANES), 1) // BS + (col * (cols // BS) + t * (LANES // BS))
        else:
            pick = jnp.where(iota((ring, LANES), 1) < HALF, (col + 1) * (cols // BS), col * (cols // BS) - 1)
        pick = jnp.clip(pick, 0, n_cols - 1)
        parts = [jnp.take_along_axis(ref[i : i + 8, :], pick[i : i + 8], axis=1) for i in range(0, ring, 8)]
        return jnp.concatenate(parts, axis=0)

    def charge(t):
        value = expand(ring_ref, t)
        for i in range(cells):
            here = value[1 + i : 2 + i, :]
            up = value[i : 1 + i, :] - here
            down = value[2 + i : 3 + i, :] - here
            at = i * BS
            some = charge_ref[t, at : at + BS, :] - here * blurred_ref[t, at : at + BS, :]
            some = jnp.concatenate(
                [some[:8] - up * above_ref[t, i], some[8 : BS - 8], some[BS - 8 :] - down * below_ref[t, i]], axis=0
            )
            turned[t % 2, at : at + BS, :] = pltpu.roll(some, HALF, 1)

    def put(t, at, value):
        for i, part in enumerate(halves(value)):
            if t < tiles:
                window[t, at, 2 * i * LANES : (2 * i + 1) * LANES] = part
            if t:
                window[t - 1, at, (2 * i + 1) * LANES : (2 * i + 2) * LANES] = part

    def fill(t):
        if t < tiles:
            charge(t)
        for a, n in chunks(0, rows):
            at = slice(a, a + n)
            before = turned[(t - 1) % 2, at, :] if t else ends[at, :]
            here = turned[t % 2, at, :] if t < tiles else ends[at, :]
            put(t, at, jnp.where(lane < HALF, before, here))

    def copy(g):
        span = slice(2 * g * LANES, 2 * (g + 1) * LANES)
        return pltpu.make_async_copy(staged.at[:, span], out_ref.at[:, span], sems.at[g])

    def finish(g):
        part = window[2 * g : 2 * g + 2].reshape(2 * rows, 4 * LANES)
        band = band_ref[...]
        both = jnp.dot(part, jnp.concatenate([band, band], axis=0), preferred_element_type=F32)
        for t in (2 * g, 2 * g + 1):
            fine = both[(t % 2) * rows : (t % 2 + 1) * rows]
            coarse = expand(ring_ref, t)[1 : 1 + cells] + expand(last_ref, t)[1 : 1 + cells]
            for i in range(cells):
                at = slice(i * BS, (i + 1) * BS)
                value = dose_ref[t, at, :] - fine[at, :LANES] - fine[at, LANES:] - coarse[i : i + 1, :]
                staged[at, t * LANES : (t + 1) * LANES] = value
        copy(g).start()

    def stage(body):
        pl.when(row >= 0)(body)

    def start():
        charge(tiles)
        ends[...] = turned[tiles % 2]
        for t in range(3):
            fill(t)

    stage(start)
    for g in range(tiles // 2):

        def step(g=g):
            if g:
                finish(g - 1)
            for t in range(2 * g + 1, 2 * g + 3):
                if t > 2:
                    fill(t)

        if g:
            stage(step)
    stage(lambda: finish(tiles // 2 - 1))
    for g in range(tiles // 2):
        copy(g).wait()


def shards(coverage, fog_rows, fog_cols):
    rows, cols = coverage.shape
    row_count = lax.axis_size("row")
    col_count = lax.axis_size("col")
    tiles = cols // LANES
    back_rows, back_cols = rows // BS, cols // BS
    n_rows, n_cols = back_rows * row_count, back_cols * col_count
    ext = rows + 2 * EDGE
    if col_count != 2 or n_cols != LANES or row_count & (row_count - 1):
        raise ValueError("unsupported mesh")

    def move(value, target):
        both = [(r, c) for r in range(row_count) for c in range(col_count)]
        flat = [(r * col_count + c, target(r, c)) for r, c in both]
        return lax.ppermute(value, ("row", "col"), [(i, r * col_count + c) for i, (r, c) in flat])

    def shape(*dims, dtype=F32):
        return jax.ShapeDtypeStruct(dims, dtype)

    def call(kernel, outs, ins, *args, scratch=(), mib=16, name=None, aliases={}, ops=1):
        return pl.pallas_call(
            kernel,
            out_shape=outs,
            in_specs=ins,
            out_specs=(VMEM,) * len(outs),
            scratch_shapes=list(scratch),
            input_output_aliases=aliases,
            compiler_params=pltpu.CompilerParams(vmem_limit_bytes=mib << 20),
            cost_estimate=pl.CostEstimate(flops=ops * rows * cols, bytes_accessed=ops * rows * cols, transcendentals=0),
            name=name,
        )(*args)

    wide = shape(tiles + 1, ext, LANES)
    own_tiles = shape(tiles + 1, rows, LANES)
    hbm = pl.BlockSpec(memory_space=pltpu.HBM)
    in_hbm = [pltpu.with_memory_space_constraint(x, pltpu.HBM) for x in (coverage, fog_rows, fog_cols)]
    edge, first_rows, second_rows = call(
        edges_kernel,
        (shape(rows, LANES), shape(tiles, EDGE, LANES), shape(tiles, EDGE, LANES)),
        [hbm],
        in_hbm[0],
        scratch=[
            pltpu.VMEM((rows, LANES), jnp.int32),
            pltpu.VMEM((2, EDGE, cols), jnp.int32),
            pltpu.SemaphoreType.DMA((3,)),
        ],
        mib=2,
        name="edges",
    )

    side = move(edge, lambda r, c: (r, 1 - c))
    corners = [side[None, :EDGE], side[None, rows - EDGE :]]

    first = move(jnp.concatenate([first_rows] + corners, axis=0), lambda r, c: (r ^ 1, c))
    second = move(
        jnp.concatenate([second_rows] + corners, axis=0),
        lambda r, c: (r, 1 - c) if r in (0, row_count - 1) else ((r + 1, c) if r % 2 else (r - 1, c)),
    )
    cover, window, c_sums, band, left, own, right = call(
        load_kernel,
        (
            wide,
            shape(tiles + 1, rows, 2 * LANES, dtype=BF16),
            shape(back_rows, LANES),
            shape(2 * LANES, 2 * LANES, dtype=BF16),
            shape(n_rows, 2 * n_rows),
            shape(16, 2 * n_rows),
            shape(n_cols, 2 * n_cols),
        ),
        [hbm] * 3 + [VMEM],
        *in_hbm,
        side,
        scratch=[
            pltpu.VMEM((rows, cols), jnp.int32),
            pltpu.VMEM((tiles, back_rows, 8, LANES), F32),
            pltpu.VMEM(fog_rows.shape, F32),
            pltpu.VMEM(fog_cols.shape, F32),
            pltpu.SemaphoreType.DMA((4 + 2,)),
        ],
        mib=8,
        name="load",
    )
    fine, across, part = call(
        inner_kernel,
        (wide, shape(tiles + 1, ext + 2 * PAD, LANES), shape(back_rows, LANES)),
        [VMEM] * 4,
        window,
        band,
        c_sums,
        cover,
        mib=8,
        name="inner",
    )
    cover, fine, sums = call(
        outer_kernel,
        (wide, wide, shape(back_rows, LANES)),
        [VMEM] * 7,
        first,
        second,
        band,
        across,
        part,
        cover,
        fine,
        scratch=[
            pltpu.VMEM((tiles + 1, 4 * PAD + 4 * EDGE, LANES), F32),
            pltpu.VMEM(((tiles + 1) * 2 * EDGE, 2 * LANES), BF16),
        ],
        aliases={5: 0, 6: 1},
        mib=8,
        name="outer",
    )

    few = shape(tiles + 1, back_rows, 8, LANES)

    def spread(after):
        return call(
            spread_kernel, (own_tiles, few, few), [VMEM] * 2, cover, after, mib=4, name="spread"
        )

    def first_dose(after):
        return call(
            first_dose_kernel,
            (shape(tiles, rows, LANES), own_tiles),
            [VMEM] * 3,
            cover,
            fine,
            after,
            scratch=[pltpu.VMEM((tiles + 1, ext, LANES), F32)],
            mib=8,
            name="dose",
        )

    pending = [spread, first_dose]
    done = []
    gathered = sums
    bit = 1
    while bit < row_count:
        other = move(gathered, lambda r, c: (r ^ bit, 1 - c))
        if bit > 1 and pending:
            results = pending.pop(0)(gathered)
            other, *results = lax.optimization_barrier((other, *results))
            done += results
        gathered = jnp.concatenate([gathered, other], axis=0)
        bit *= 2
    gathered = jnp.concatenate([gathered, move(gathered, lambda r, c: (r, 1 - c))], axis=0)
    for work in pending:
        done += work(gathered)
    blurred, above, below, dose, charge = done

    return pl.pallas_call(
        last_kernel,
        out_shape=shape(rows, cols),
        in_specs=[VMEM] * 10,
        out_specs=pl.BlockSpec(memory_space=pltpu.HBM),
        scratch_shapes=[
            pltpu.VMEM((n_rows, n_cols), F32),
            pltpu.VMEM((n_rows, n_cols), F32),
            pltpu.VMEM((16, n_cols), F32),
            pltpu.VMEM((16, n_cols), F32),
            pltpu.VMEM((tiles, rows, 4 * LANES), BF16),
            pltpu.VMEM((2, rows, LANES), F32),
            pltpu.VMEM((rows, LANES), F32),
            pltpu.VMEM((rows, cols), F32),
            pltpu.SemaphoreType.DMA((tiles // 2,)),
        ],
        compiler_params=pltpu.CompilerParams(vmem_limit_bytes=16 << 20),
        name="last",
    )(gathered, left, own, right, band, dose, charge, blurred, above, below)


def solution(mesh):
    in_specs = (P(("stripe", "row"), "col"), P(), P())
    out_specs = P(("stripe", "row"), "col")
    return jax.shard_map(shards, mesh=mesh, in_specs=in_specs, out_specs=out_specs, check_vma=False)
```

```python
import math

import jax
import jax.numpy as jnp
import numpy as np
from jax import lax
from jax.experimental import pallas as pl
from jax.experimental.pallas import tpu as pltpu
from jax.sharding import PartitionSpec as P

BS = 32
FB = 256
HALO = 4
BSIG = 16
REACH = 40
LANES = 128
HALF = LANES // 2
EDGE = 2 * HALO
PAD = 8
F32 = jnp.float32
BF16 = jnp.bfloat16
VMEM = pl.BlockSpec(memory_space=pltpu.VMEM)


def fine_taps():
    offsets = np.arange(-HALO, HALO + 1).astype(np.float32)
    raw = np.exp(np.float32(-0.5) * (offsets / np.float32(1.25)) ** 2).astype(np.float32)
    taps = (raw / raw.sum(dtype=np.float32)).astype(np.float32)
    return [float(taps[HALO + k]) for k in range(HALO + 1)]


TAPS = fine_taps()


def iota(shape, dim):
    return lax.broadcasted_iota(jnp.int32, shape, dim)


def tap_of(distance):
    value = jnp.zeros(distance.shape, F32)
    for k in range(HALO + 1):
        value = jnp.where(distance == k, F32(TAPS[k]), value)
    return value


def gauss(offsets):
    off = offsets.astype(F32)
    values = jnp.exp(-0.5 * (off / BSIG) ** 2) / (BSIG * math.sqrt(2.0 * math.pi))
    return jnp.where(jnp.abs(off) <= REACH, values, jnp.zeros_like(values))


def halves(x):
    upper = x.astype(BF16)
    return upper, (x - upper.astype(F32)).astype(BF16)


def dot(a, b):
    (ah, al), (bh, bl) = halves(a), halves(b)
    return jnp.dot(
        jnp.concatenate([ah, al, ah], axis=1),
        jnp.concatenate([bh, bh, bl], axis=0),
        preferred_element_type=F32,
    )


def full_dot(a, b, over=1):
    return lax.dot_general(
        a, b, (((over,), (0,)), ((), ())), precision=lax.Precision.HIGHEST, preferred_element_type=F32
    )


def prep(place, fog_rows, fog_cols, left_ref, own_ref, right_ref):
    n_rows = left_ref.shape[0]
    n_cols = right_ref.shape[0]
    side = FB // BS
    kr = fog_rows / jnp.sum(fog_rows, axis=1, keepdims=True)
    kc = fog_cols / jnp.sum(fog_cols, axis=1, keepdims=True)
    fr, fc = kr.shape[0], kc.shape[0]
    spread_r = (iota((fr, n_rows), 1) // side == iota((fr, n_rows), 0)).astype(F32)
    spread_c = (iota((fc, n_cols), 1) // side == iota((fc, n_cols), 0)).astype(F32)
    kr_cols = full_dot(kr, spread_r)

    def left(count, first):
        here = iota((count, n_rows), 0) + first
        weight = 0.3 * gauss(here - iota((count, n_rows), 1))
        cell = jnp.clip(iota((count, fr), 0) + first, 0, n_rows - 1) // side
        pick = (cell == iota((count, fr), 1)).astype(F32)
        return weight, full_dot(pick, kr_cols) * F32(0.2 / (side * side))

    left_ref[:, :n_rows], left_ref[:, n_rows:] = left(n_rows, 0)
    own_ref[:, :n_rows], own_ref[:, n_rows:] = left(own_ref.shape[0], place - 1)
    right_ref[:, :n_cols] = gauss(iota((n_cols, n_cols), 0) - iota((n_cols, n_cols), 1))
    right_ref[:, n_cols:] = full_dot(spread_c, full_dot(kc, spread_c, 0), 0)


def row_blur(load, scale=1.0):
    acc = F32(TAPS[0] * scale) * load(0)
    for k in range(1, HALO + 1):
        acc = acc + F32(TAPS[k] * scale) * (load(-k) + load(k))
    return acc


def eights(x):
    return sum((x[b : b + 8] for b in range(8, x.shape[0], 8)), x[:8])


def sublane_sums(x):
    half = x.shape[0] // 2
    x = x[:half] + x[half:]
    return x.reshape(half // 8, 8, LANES).sum(axis=1)


def chunks(start, stop, size=64):
    return [(a, min(size, stop - a)) for a in range(start, stop, size)]


def edges_kernel(cov_ref, edge_ref, first_ref, second_ref, tile, strips, sems):
    rows, cols = cov_ref.shape
    tiles = cols // LANES
    odd = lax.rem(lax.axis_index("row"), 2)
    over = pl.ds(pl.multiple_of((1 - lax.axis_index("col")) * (cols - LANES), LANES), LANES)
    copies = [pltpu.make_async_copy(cov_ref.at[:, over], tile, sems.at[0])]
    for i, start in enumerate((1 - odd, odd)):
        span = pl.ds(pl.multiple_of(start * (rows - EDGE), EDGE), EDGE)
        copies.append(pltpu.make_async_copy(cov_ref.at[span], strips.at[i], sems.at[1 + i]))
    for copy in copies:
        copy.start()
    for copy in copies:
        copy.wait()
    edge_ref[...] = tile[...].astype(F32)
    for t in range(tiles):
        first_ref[t] = strips[0, :, t * LANES : (t + 1) * LANES].astype(F32)
        second_ref[t] = strips[1, :, t * LANES : (t + 1) * LANES].astype(F32)


def load_kernel(cov_ref, fog_rows_ref, fog_cols_ref, side_ref, cover_ref, window, parts_ref, band_ref, fold_ref, left_ref, own_ref, right_ref, loaded, fog_r, fog_c, sems):
    rows, cols = cov_ref.shape
    tiles = cols // LANES
    pieces = sems.shape[0] - 2
    part = rows // pieces
    copies = [
        pltpu.make_async_copy(
            cov_ref.at[p * part : (p + 1) * part], loaded.at[p * part : (p + 1) * part], sems.at[p]
        )
        for p in range(pieces)
    ]
    fogs = [
        pltpu.make_async_copy(fog_rows_ref, fog_r, sems.at[pieces]),
        pltpu.make_async_copy(fog_cols_ref, fog_c, sems.at[pieces + 1]),
    ]
    ahead = 3
    for copy in fogs + copies[:ahead]:
        copy.start()
    tap = tap_of(jnp.abs(iota((2 * LANES, LANES), 0) - HALF - iota((2 * LANES, LANES), 1)))
    band_ref[:, :LANES], band_ref[:, LANES:] = halves(tap)
    for t in range(tiles):
        group = (iota((LANES, LANES), 0) + t * LANES) // BS
        fold_ref[t * LANES : (t + 1) * LANES, :] = (group == iota((LANES, LANES), 1)).astype(F32).astype(BF16)
    for copy in fogs:
        copy.wait()
    place = lax.axis_index("row") * (rows // BS)
    prep(place, fog_r[...], fog_c[...], left_ref, own_ref, right_ref)
    lane = iota((1, LANES), 1)
    touches = (lane < HALF) == (lax.axis_index("col") == 0)

    def put(t, at, value):
        window[t, at, :LANES] = value
        window[(t - 1) % (tiles + 1), at, LANES:] = value

    for p, copy in enumerate(copies):
        copy.wait()
        if p + ahead < pieces:
            copies[p + ahead].start()
        at = slice(p * part, (p + 1) * part)
        side = jnp.where(touches, side_ref[at, :], 0.0)
        cover_ref[tiles, EDGE + p * part : EDGE + (p + 1) * part, :] = side
        side = pltpu.roll(side, HALF, 1)
        before = side
        for t in range(tiles):
            value = loaded[at, t * LANES : (t + 1) * LANES].astype(F32)
            cover_ref[t, EDGE + p * part : EDGE + (p + 1) * part, :] = value
            here = pltpu.roll(value, HALF, 1)
            put(t, at, jnp.where(lane < HALF, before, here).astype(BF16))
            before = here
            some = jnp.concatenate([eights(value[i : i + BS]) for i in range(0, part, BS)], axis=0)
            span = slice(t * LANES, (t + 1) * LANES)
            for half, rest in zip(range(2), halves(some)):
                low = half * (rows // 4) + p * (part // 4)
                parts_ref[low : low + part // 4, span] = rest
        put(tiles, at, jnp.where(lane < HALF, before, side).astype(BF16))

def inner_kernel(window, band_ref, fold_ref, c_ref, cover_in, fine_ref, across, sums_ref, f_parts):
    tiles = cover_in.shape[0] - 1
    rows = window.shape[1]

    def columns(t, count):
        part = window[t : t + count].reshape(count * rows, 2 * LANES)
        both = jnp.dot(part, band_ref[...], preferred_element_type=F32)
        for i in range(count):
            mine = both[i * rows : (i + 1) * rows]
            across[t + i, PAD + EDGE : PAD + EDGE + rows, :] = mine[:, :LANES] + mine[:, LANES:]

    def down(t):
        parts = []
        for a, n in chunks(0, rows, BS):
            low, high = max(a, 8), min(a + n, rows - 8)
            base = PAD + EDGE + low
            fine = row_blur(lambda k: across[t, base + k : base + k + high - low, :])
            fine_ref[t, EDGE + low : EDGE + high, :] = fine
            parts.append(eights(cover_in[t, EDGE + low : EDGE + high, :] * fine))
        if t < tiles:
            span = slice(t * LANES, (t + 1) * LANES)
            for i in range(0, len(parts), 2):
                upper, lower = halves(jnp.concatenate(parts[i : i + 2], axis=0))
                f_parts[8 * i : 8 * i + 16, span] = upper
                f_parts[rows // 4 + 8 * i : rows // 4 + 8 * i + 16, span] = lower

    groups = chunks(0, tiles + 1, 2)
    columns(*groups[0])
    for g, (start, count) in enumerate(groups):
        if g + 1 < len(groups):
            columns(*groups[g + 1])
        for t in range(start, start + count):
            down(t)
    c = sublane_sums(jnp.dot(c_ref[...], fold_ref[...], preferred_element_type=F32))
    f = sublane_sums(jnp.dot(f_parts[...], fold_ref[...], preferred_element_type=F32))
    sums_ref[...] = c + pltpu.roll(f, HALF, 1)


def outer_kernel(first_ref, second_ref, band_ref, fold_ref, across_ref, part_ref, cover_in, fine_in, cover_ref, fine_ref, sums_ref, across, window, f_parts):
    tiles = cover_ref.shape[0] - 1
    ext = cover_ref.shape[1]
    rows = ext - 2 * EDGE
    even = lax.rem(lax.axis_index("row"), 2) == 0
    lane = iota((1, LANES), 1)
    cells = rows // BS
    both = 2 * EDGE
    touches = (lane < HALF) == (lax.axis_index("col") == 0)
    place = lax.axis_index("row")
    alone = (place == 0) | (place == lax.axis_size("row") - 1)

    def halo(t):
        if t < tiles:
            a, b = first_ref[t], second_ref[t]
        else:
            a = jnp.where(even, first_ref[t], first_ref[t + 1])
            b = jnp.where(even, second_ref[t + 1], second_ref[t])
            a, b = jnp.where(touches, a, 0.0), jnp.where(touches, b, 0.0)
        b = jnp.where(alone, 0.0, b)
        top = jnp.where(even, b, a)
        low = jnp.where(even, a, b)
        cover_ref[t, 0:EDGE, :] = top
        cover_ref[t, EDGE + rows :, :] = low
        return pltpu.roll(jnp.concatenate([top, low], axis=0), HALF, 1)

    before = halo(tiles)
    first = before
    for t in range(tiles + 1):
        here = halo(t) if t < tiles else first
        tile = jnp.where(lane < HALF, before, here).astype(BF16)
        window[t * both : (t + 1) * both, :LANES] = tile
        at = t - 1 if t else tiles
        window[at * both : (at + 1) * both, LANES:] = tile
        before = here
    twice = jnp.dot(window[...], band_ref[...], preferred_element_type=F32)
    once = twice[:, :LANES] + twice[:, LANES:]
    reach = 2 * PAD + 2 * EDGE
    for t in range(tiles + 1):
        across[t, 0:PAD, :] = jnp.zeros((PAD, LANES), F32)
        across[t, PAD : PAD + EDGE, :] = once[t * both : t * both + EDGE]
        across[t, PAD + EDGE : reach, :] = across_ref[t, PAD + EDGE : reach, :]
        low = reach
        across[t, low : low + PAD + EDGE, :] = across_ref[t, ext - PAD - EDGE : ext, :]
        across[t, low + PAD + EDGE : low + PAD + 2 * EDGE, :] = once[t * both + EDGE : (t + 1) * both]
        across[t, low + PAD + 2 * EDGE :, :] = jnp.zeros((PAD, LANES), F32)
        top = row_blur(lambda k: across[t, PAD + k : PAD + k + EDGE + 8, :])
        base = low + 8
        bot = row_blur(lambda k: across[t, base + k : base + k + EDGE + 8, :])
        fine_ref[t, 0 : EDGE + 8, :] = top
        fine_ref[t, EDGE + rows - 8 :, :] = bot
        if t < tiles:
            a = top[EDGE:] * cover_ref[t, EDGE : EDGE + 8, :]
            b = bot[:8] * cover_ref[t, EDGE + rows - 8 : EDGE + rows, :]
            span = slice(t * LANES, (t + 1) * LANES)
            f_parts[:16, span], f_parts[16:, span] = halves(jnp.concatenate([a, b], axis=0))
    f = sublane_sums(jnp.dot(f_parts[...], fold_ref[...], preferred_element_type=F32))
    row = iota((cells, LANES), 0)
    total = jnp.where(row == 0, f[0:1], jnp.where(row == cells - 1, f[1:2], 0.0))
    sums_ref[...] = part_ref[...] + pltpu.roll(total, HALF, 1)


def spread_kernel(cover_ref, after_ref, blurred_ref, above_ref, below_ref):
    del after_ref
    tiles, ext = cover_ref.shape[0] - 1, cover_ref.shape[1]
    rows = ext - 2 * EDGE
    scale = 0.5 / 255.0
    row = iota((8, LANES), 0)
    for t in range(tiles + 1):
        for a, n in chunks(0, rows):
            blurred_ref[t, a : a + n, :] = row_blur(lambda k: cover_ref[t, EDGE + a + k : EDGE + a + k + n, :], scale)
        for i in range(rows // BS):
            top = EDGE + i * BS
            low = top + BS - 8
            above = jnp.zeros((8, LANES), F32)
            below = jnp.zeros((8, LANES), F32)
            for k in range(1, HALO + 1):
                tap = F32(TAPS[k] * scale)
                above = above + jnp.where(row < k, tap * cover_ref[t, top - k : top - k + 8, :], 0.0)
                below = below + jnp.where(row >= 8 - k, tap * cover_ref[t, low + k : low + k + 8, :], 0.0)
            above_ref[t, i] = above
            below_ref[t, i] = below


def first_dose_kernel(cover_ref, fine_ref, after_ref, dose_ref, blurred_ref, charge):
    del after_ref
    tiles, ext = cover_ref.shape[0] - 1, cover_ref.shape[1]
    rows = ext - 2 * EDGE
    for t in range(tiles + 1):
        for a, n in [(0, EDGE)] + [(EDGE + a, n) for a, n in chunks(0, rows)] + [(EDGE + rows, EDGE)]:
            dose = 2.0 - F32(0.5 / 255.0) * fine_ref[t, a : a + n, :]
            if t < tiles and EDGE <= a < EDGE + rows:
                dose_ref[t, a - EDGE : a - EDGE + n, :] = dose
            charge[t, a : a + n, :] = (dose - 0.5) * cover_ref[t, a : a + n, :]
        for a, n in chunks(0, rows):
            blurred_ref[t, a : a + n, :] = row_blur(
                lambda k: charge[t, EDGE + a + k : EDGE + a + k + n, :], 0.5 / 255.0
            )


def last_kernel(gathered_ref, left_ref, own_ref, right_ref, band_ref, dose_ref, charge_ref, blurred_ref, above_ref, below_ref, out_ref, c_all, f_all, ring_ref, last_ref, window, turned, ends, staged, sems):
    rows, cols = out_ref.shape
    tiles = cols // LANES
    n_rows, n_cols = c_all.shape
    cells = rows // BS
    col = lax.axis_index("col")
    row = lax.axis_index("row")
    lane8 = iota((cells, LANES), 1)
    lane = iota((1, LANES), 1)
    count = n_rows // cells
    for j in range(count):
        mine = gathered_ref[j * cells : (j + 1) * cells, :]
        other = gathered_ref[(count + j) * cells : (count + j + 1) * cells, :]
        here = col == bin(j).count("1") % 2
        low = jnp.where(here, mine, other)
        high = jnp.where(here, other, mine)
        at = pl.ds(pl.multiple_of((row ^ j) * cells, cells), cells)
        c_all[at, :] = jnp.where(lane8 < HALF, low, pltpu.roll(high, HALF, 1)) * F32(1.0 / (255.0 * BS * BS))
        f_all[at, :] = jnp.where(lane8 < HALF, pltpu.roll(low, HALF, 1), high) * F32(1.0 / (255.0 * 255.0 * BS * BS))
    right = right_ref[...]

    def both(x):
        part = dot(x, right)
        return jnp.concatenate([part[:, :n_cols], part[:, n_cols:]], axis=0)

    c = c_all[...]
    spread = both(c)
    ring_ref[...] = dot(own_ref[...], spread)
    coarse = dot(left_ref[...], spread)
    back = (1.5 - coarse) * c - 0.5 * f_all[...]
    last_ref[...] = dot(own_ref[...], both(back))

    ring = ring_ref.shape[0]

    def expand(ref, t):
        if t < tiles:
            pick = iota((ring, LANES), 1) // BS + (col * (cols // BS) + t * (LANES // BS))
        else:
            pick = jnp.where(iota((ring, LANES), 1) < HALF, (col + 1) * (cols // BS), col * (cols // BS) - 1)
        pick = jnp.clip(pick, 0, n_cols - 1)
        parts = [jnp.take_along_axis(ref[i : i + 8, :], pick[i : i + 8], axis=1) for i in range(0, ring, 8)]
        return jnp.concatenate(parts, axis=0)

    def charge(t):
        value = expand(ring_ref, t)
        for i in range(cells):
            here = value[1 + i : 2 + i, :]
            up = value[i : 1 + i, :] - here
            down = value[2 + i : 3 + i, :] - here
            at = i * BS
            some = charge_ref[t, at : at + BS, :] - here * blurred_ref[t, at : at + BS, :]
            some = jnp.concatenate(
                [some[:8] - up * above_ref[t, i], some[8 : BS - 8], some[BS - 8 :] - down * below_ref[t, i]], axis=0
            )
            turned[t % 2, at : at + BS, :] = pltpu.roll(some, HALF, 1)

    def put(t, at, value):
        for i, part in enumerate(halves(value)):
            if t < tiles:
                window[t, at, 2 * i * LANES : (2 * i + 1) * LANES] = part
            if t:
                window[t - 1, at, (2 * i + 1) * LANES : (2 * i + 2) * LANES] = part

    def fill(t):
        if t < tiles:
            charge(t)
        for a, n in chunks(0, rows):
            at = slice(a, a + n)
            before = turned[(t - 1) % 2, at, :] if t else ends[at, :]
            here = turned[t % 2, at, :] if t < tiles else ends[at, :]
            put(t, at, jnp.where(lane < HALF, before, here))

    def copy(g):
        span = slice(2 * g * LANES, 2 * (g + 1) * LANES)
        return pltpu.make_async_copy(staged.at[:, span], out_ref.at[:, span], sems.at[g])

    def finish(g):
        part = window[2 * g : 2 * g + 2].reshape(2 * rows, 4 * LANES)
        band = band_ref[...]
        both = jnp.dot(part, jnp.concatenate([band, band], axis=0), preferred_element_type=F32)
        for t in (2 * g, 2 * g + 1):
            fine = both[(t % 2) * rows : (t % 2 + 1) * rows]
            coarse = expand(ring_ref, t)[1 : 1 + cells] + expand(last_ref, t)[1 : 1 + cells]
            for i in range(cells):
                at = slice(i * BS, (i + 1) * BS)
                value = dose_ref[t, at, :] - fine[at, :LANES] - fine[at, LANES:] - coarse[i : i + 1, :]
                staged[at, t * LANES : (t + 1) * LANES] = value
        copy(g).start()

    def stage(body):
        body()

    def start():
        charge(tiles)
        ends[...] = turned[tiles % 2]
        for t in range(3):
            fill(t)

    stage(start)
    for g in range(tiles // 2):

        def step(g=g):
            if g:
                finish(g - 1)
            for t in range(2 * g + 1, 2 * g + 3):
                if t > 2:
                    fill(t)

        if g:
            stage(step)
    stage(lambda: finish(tiles // 2 - 1))
    for g in range(tiles // 2):
        copy(g).wait()


def shards(coverage, fog_rows, fog_cols):
    rows, cols = coverage.shape
    row_count = lax.axis_size("row")
    col_count = lax.axis_size("col")
    tiles = cols // LANES
    back_rows, back_cols = rows // BS, cols // BS
    n_rows, n_cols = back_rows * row_count, back_cols * col_count
    ext = rows + 2 * EDGE
    if col_count != 2 or n_cols != LANES or row_count & (row_count - 1):
        raise ValueError("unsupported mesh")

    def move(value, target):
        both = [(r, c) for r in range(row_count) for c in range(col_count)]
        flat = [(r * col_count + c, target(r, c)) for r, c in both]
        return lax.ppermute(value, ("row", "col"), [(i, r * col_count + c) for i, (r, c) in flat])

    def shape(*dims, dtype=F32):
        return jax.ShapeDtypeStruct(dims, dtype)

    def call(kernel, outs, ins, *args, scratch=(), mib=16, name=None, aliases={}, ops=1):
        return pl.pallas_call(
            kernel,
            out_shape=outs,
            in_specs=ins,
            out_specs=(VMEM,) * len(outs),
            scratch_shapes=list(scratch),
            input_output_aliases=aliases,
            compiler_params=pltpu.CompilerParams(vmem_limit_bytes=mib << 20),
            cost_estimate=pl.CostEstimate(flops=ops * rows * cols, bytes_accessed=ops * rows * cols, transcendentals=0),
            name=name,
        )(*args)

    wide = shape(tiles + 1, ext, LANES)
    own_tiles = shape(tiles + 1, rows, LANES)
    hbm = pl.BlockSpec(memory_space=pltpu.HBM)
    in_hbm = [pltpu.with_memory_space_constraint(x, pltpu.HBM) for x in (coverage, fog_rows, fog_cols)]
    edge, first_rows, second_rows = call(
        edges_kernel,
        (shape(rows, LANES), shape(tiles, EDGE, LANES), shape(tiles, EDGE, LANES)),
        [hbm],
        in_hbm[0],
        scratch=[
            pltpu.VMEM((rows, LANES), jnp.int32),
            pltpu.VMEM((2, EDGE, cols), jnp.int32),
            pltpu.SemaphoreType.DMA((3,)),
        ],
        mib=2,
        name="edges",
    )

    side = move(edge, lambda r, c: (r, 1 - c))
    corners = [side[None, :EDGE], side[None, rows - EDGE :]]

    first = move(jnp.concatenate([first_rows] + corners, axis=0), lambda r, c: (r ^ 1, c))
    second = move(
        jnp.concatenate([second_rows] + corners, axis=0),
        lambda r, c: (r, 1 - c) if r in (0, row_count - 1) else ((r + 1, c) if r % 2 else (r - 1, c)),
    )
    cover, window, c_parts, band, fold, left, own, right = call(
        load_kernel,
        (
            wide,
            shape(tiles + 1, rows, 2 * LANES, dtype=BF16),
            shape(rows // 2, cols, dtype=BF16),
            shape(2 * LANES, 2 * LANES, dtype=BF16),
            shape(cols, LANES, dtype=BF16),
            shape(n_rows, 2 * n_rows),
            shape(16, 2 * n_rows),
            shape(n_cols, 2 * n_cols),
        ),
        [hbm] * 3 + [VMEM],
        *in_hbm,
        side,
        scratch=[
            pltpu.VMEM((rows, cols), jnp.int32),
            pltpu.VMEM(fog_rows.shape, F32),
            pltpu.VMEM(fog_cols.shape, F32),
            pltpu.SemaphoreType.DMA((4 + 2,)),
        ],
        mib=8,
        name="load",
    )
    fine, across, part = call(
        inner_kernel,
        (wide, shape(tiles + 1, ext + 2 * PAD, LANES), shape(back_rows, LANES)),
        [VMEM] * 5,
        window,
        band,
        fold,
        c_parts,
        cover,
        scratch=[pltpu.VMEM((rows // 2, cols), BF16)],
        mib=8,
        name="inner",
    )
    cover, fine, sums = call(
        outer_kernel,
        (wide, wide, shape(back_rows, LANES)),
        [VMEM] * 8,
        first,
        second,
        band,
        fold,
        across,
        part,
        cover,
        fine,
        scratch=[
            pltpu.VMEM((tiles + 1, 4 * PAD + 4 * EDGE, LANES), F32),
            pltpu.VMEM(((tiles + 1) * 2 * EDGE, 2 * LANES), BF16),
            pltpu.VMEM((32, cols), BF16),
        ],
        aliases={6: 0, 7: 1},
        mib=8,
        name="outer",
    )

    few = shape(tiles + 1, back_rows, 8, LANES)

    def spread(after):
        return call(
            spread_kernel, (own_tiles, few, few), [VMEM] * 2, cover, after, mib=4, name="spread"
        )

    def first_dose(after):
        return call(
            first_dose_kernel,
            (shape(tiles, rows, LANES), own_tiles),
            [VMEM] * 3,
            cover,
            fine,
            after,
            scratch=[pltpu.VMEM((tiles + 1, ext, LANES), F32)],
            mib=8,
            name="dose",
        )

    pending = [spread, first_dose]
    done = []
    gathered = sums
    bit = 1
    while bit < row_count:
        other = move(gathered, lambda r, c: (r ^ bit, 1 - c))
        if bit > 1 and pending:
            results = pending.pop(0)(gathered)
            other, *results = lax.optimization_barrier((other, *results))
            done += results
        gathered = jnp.concatenate([gathered, other], axis=0)
        bit *= 2
    gathered = jnp.concatenate([gathered, move(gathered, lambda r, c: (r, 1 - c))], axis=0)
    for work in pending:
        done += work(gathered)
    blurred, above, below, dose, charge = done

    return pl.pallas_call(
        last_kernel,
        out_shape=shape(rows, cols),
        in_specs=[VMEM] * 10,
        out_specs=pl.BlockSpec(memory_space=pltpu.HBM),
        scratch_shapes=[
            pltpu.VMEM((n_rows, n_cols), F32),
            pltpu.VMEM((n_rows, n_cols), F32),
            pltpu.VMEM((16, n_cols), F32),
            pltpu.VMEM((16, n_cols), F32),
            pltpu.VMEM((tiles, rows, 4 * LANES), BF16),
            pltpu.VMEM((2, rows, LANES), F32),
            pltpu.VMEM((rows, LANES), F32),
            pltpu.VMEM((rows, cols), F32),
            pltpu.SemaphoreType.DMA((tiles // 2,)),
        ],
        compiler_params=pltpu.CompilerParams(vmem_limit_bytes=16 << 20),
        name="last",
    )(gathered, left, own, right, band, dose, charge, blurred, above, below)


def solution(mesh):
    in_specs = (P(("stripe", "row"), "col"), P(), P())
    out_specs = P(("stripe", "row"), "col")
    return jax.shard_map(shards, mesh=mesh, in_specs=in_specs, out_specs=out_specs, check_vma=False)
```

```python
import math

import jax
import jax.numpy as jnp
import numpy as np
from jax import lax
from jax.experimental import pallas as pl
from jax.experimental.pallas import tpu as pltpu
from jax.sharding import PartitionSpec as P

BS = 32
FB = 256
HALO = 4
BSIG = 16
REACH = 40
LANES = 128
HALF = LANES // 2
EDGE = 2 * HALO
PAD = 8
F32 = jnp.float32
BF16 = jnp.bfloat16
VMEM = pl.BlockSpec(memory_space=pltpu.VMEM)


def fine_taps():
    offsets = np.arange(-HALO, HALO + 1).astype(np.float32)
    raw = np.exp(np.float32(-0.5) * (offsets / np.float32(1.25)) ** 2).astype(np.float32)
    taps = (raw / raw.sum(dtype=np.float32)).astype(np.float32)
    return [float(taps[HALO + k]) for k in range(HALO + 1)]


TAPS = fine_taps()


def iota(shape, dim):
    return lax.broadcasted_iota(jnp.int32, shape, dim)


def tap_of(distance):
    value = jnp.zeros(distance.shape, F32)
    for k in range(HALO + 1):
        value = jnp.where(distance == k, F32(TAPS[k]), value)
    return value


def gauss(offsets):
    off = offsets.astype(F32)
    values = jnp.exp(-0.5 * (off / BSIG) ** 2) / (BSIG * math.sqrt(2.0 * math.pi))
    return jnp.where(jnp.abs(off) <= REACH, values, jnp.zeros_like(values))


def halves(x):
    upper = x.astype(BF16)
    return upper, (x - upper.astype(F32)).astype(BF16)


def dot(a, b):
    (ah, al), (bh, bl) = halves(a), halves(b)
    return jnp.dot(
        jnp.concatenate([ah, al, ah], axis=1),
        jnp.concatenate([bh, bh, bl], axis=0),
        preferred_element_type=F32,
    )


def full_dot(a, b, over=1):
    return lax.dot_general(
        a, b, (((over,), (0,)), ((), ())), precision=lax.Precision.HIGHEST, preferred_element_type=F32
    )


def prep(place, fog_rows, fog_cols, left_ref, own_ref, right_ref):
    n_rows = left_ref.shape[0]
    n_cols = right_ref.shape[0]
    side = FB // BS
    kr = fog_rows / jnp.sum(fog_rows, axis=1, keepdims=True)
    kc = fog_cols / jnp.sum(fog_cols, axis=1, keepdims=True)
    fr, fc = kr.shape[0], kc.shape[0]
    spread_r = (iota((fr, n_rows), 1) // side == iota((fr, n_rows), 0)).astype(F32)
    spread_c = (iota((fc, n_cols), 1) // side == iota((fc, n_cols), 0)).astype(F32)
    kr_cols = full_dot(kr, spread_r)

    def left(count, first):
        here = iota((count, n_rows), 0) + first
        weight = 0.3 * gauss(here - iota((count, n_rows), 1))
        cell = jnp.clip(iota((count, fr), 0) + first, 0, n_rows - 1) // side
        pick = (cell == iota((count, fr), 1)).astype(F32)
        return weight, full_dot(pick, kr_cols) * F32(0.2 / (side * side))

    left_ref[:, :n_rows], left_ref[:, n_rows:] = left(n_rows, 0)
    own_ref[:, :n_rows], own_ref[:, n_rows:] = left(own_ref.shape[0], place - 1)
    right_ref[:, :n_cols] = gauss(iota((n_cols, n_cols), 0) - iota((n_cols, n_cols), 1))
    right_ref[:, n_cols:] = full_dot(spread_c, full_dot(kc, spread_c, 0), 0)


def row_blur(load, scale=1.0):
    acc = F32(TAPS[0] * scale) * load(0)
    for k in range(1, HALO + 1):
        acc = acc + F32(TAPS[k] * scale) * (load(-k) + load(k))
    return acc


def eights(x):
    return sum((x[b : b + 8] for b in range(8, x.shape[0], 8)), x[:8])


def sublane_sums(x):
    half = x.shape[0] // 2
    x = x[:half] + x[half:]
    return x.reshape(half // 8, 8, LANES).sum(axis=1)


def chunks(start, stop, size=64):
    return [(a, min(size, stop - a)) for a in range(start, stop, size)]


def edges_kernel(cov_ref, fog_rows_ref, fog_cols_ref, edge_ref, first_ref, second_ref, fog_r, fog_c, tile, strips, sems):
    rows, cols = cov_ref.shape
    tiles = cols // LANES
    odd = lax.rem(lax.axis_index("row"), 2)
    over = pl.ds(pl.multiple_of((1 - lax.axis_index("col")) * (cols - LANES), LANES), LANES)
    copies = [pltpu.make_async_copy(cov_ref.at[:, over], tile, sems.at[0])]
    for i, start in enumerate((1 - odd, odd)):
        span = pl.ds(pl.multiple_of(start * (rows - EDGE), EDGE), EDGE)
        copies.append(pltpu.make_async_copy(cov_ref.at[span], strips.at[i], sems.at[1 + i]))
    copies.append(pltpu.make_async_copy(fog_rows_ref, fog_r, sems.at[3]))
    copies.append(pltpu.make_async_copy(fog_cols_ref, fog_c, sems.at[4]))
    for copy in copies:
        copy.start()
    for copy in copies:
        copy.wait()
    edge_ref[:rows, :] = tile[...].astype(F32)
    for i, start in enumerate((1 - odd, odd)):
        span = pl.ds(pl.multiple_of(start * (rows - EDGE), EDGE), EDGE)
        edge_ref[rows + i * EDGE : rows + (i + 1) * EDGE, :] = tile[span, :].astype(F32)
    for t in range(tiles):
        first_ref[t] = strips[0, :, t * LANES : (t + 1) * LANES].astype(F32)
        second_ref[t] = strips[1, :, t * LANES : (t + 1) * LANES].astype(F32)


def prep_kernel(fog_rows_ref, fog_cols_ref, band_ref, fold_ref, left_ref, own_ref, right_ref):
    tap = tap_of(jnp.abs(iota((2 * LANES, LANES), 0) - HALF - iota((2 * LANES, LANES), 1)))
    band_ref[:, :LANES], band_ref[:, LANES:] = halves(tap)
    for t in range(0, fold_ref.shape[0], LANES):
        group = (iota((LANES, LANES), 0) + t) // BS
        fold_ref[t : t + LANES, :] = (group == iota((LANES, LANES), 1)).astype(F32).astype(BF16)
    place = lax.axis_index("row") * (left_ref.shape[0] // lax.axis_size("row"))
    prep(place, fog_rows_ref[...], fog_cols_ref[...], left_ref, own_ref, right_ref)


def block_kernel(cov_ref, side_ref, band_ref, fold_ref, cover_ref, fine_ref, across, sums_ref, window, parts):
    rows, cols = cov_ref.shape
    tiles = cols // LANES
    part = 2 * BS
    pieces = rows // part
    cells = rows // BS
    lane = iota((1, LANES), 1)
    touches = (lane < HALF) == (lax.axis_index("col") == 0)
    c_rows, f_rows = 8 * cells, 8 * (cells + 2)

    def keep(base, height, low, span, values):
        for half, value in zip(range(2), halves(jnp.concatenate(values, axis=0))):
            at = base + half * height + low
            parts[at : at + 8 * len(values), span] = value

    for p in range(pieces):
        first = p * part
        at = slice(EDGE + first, EDGE + first + part)

        def put(t, value):
            window[t, :, :LANES] = value
            window[(t - 1) % (tiles + 1), :, LANES:] = value

        side = jnp.where(touches, side_ref[first : first + part, :], 0.0)
        cover_ref[tiles, at, :] = side
        side = pltpu.roll(side, HALF, 1)
        before = side
        for t in range(tiles):
            span = slice(t * LANES, (t + 1) * LANES)
            value = cov_ref[first : first + part, span].astype(F32)
            cover_ref[t, at, :] = value
            here = pltpu.roll(value, HALF, 1)
            put(t, jnp.where(lane < HALF, before, here).astype(BF16))
            before = here
            keep(0, c_rows, 8 * (first // BS), span, [eights(value[i : i + BS]) for i in range(0, part, BS)])
        put(tiles, jnp.where(lane < HALF, before, side).astype(BF16))
        for t, count in chunks(0, tiles + 1, 6):
            some = window[t : t + count].reshape(count * part, 2 * LANES)
            both = jnp.dot(some, band_ref[...], preferred_element_type=F32)
            for i in range(count):
                mine = both[i * part : (i + 1) * part]
                across[t + i, PAD + EDGE + first : PAD + EDGE + first + part, :] = mine[:, :LANES] + mine[:, LANES:]
        ready = range(max(2 * p - 1, 0), 2 * p + 1 if p + 1 < pieces else cells)
        for t in range(tiles + 1):
            got = {}
            for i in ready:
                low, high = max(i * BS, 8), min((i + 1) * BS, rows - 8)
                base = PAD + EDGE + low
                fine = row_blur(lambda k: across[t, base + k : base + k + high - low, :])
                fine_ref[t, EDGE + low : EDGE + high, :] = fine
                if t < tiles:
                    got[i] = eights(cover_ref[t, EDGE + low : EDGE + high, :] * fine)
            if t < tiles:
                span = slice(t * LANES, (t + 1) * LANES)
                zero = jnp.zeros((8, LANES), F32)
                for i in got:
                    if i % 2 or i == 0:
                        pair = [got[i], got.get(i + 1, zero)] if i else [got[0], zero]
                        keep(2 * c_rows, f_rows, 8 * (i + 1) if i else 0, span, pair)
    def folded(some, step):
        return sum(
            jnp.dot(parts[some, a : a + step], fold_ref[a : a + step, :], preferred_element_type=F32)
            for a in range(0, cols, step)
        )

    c = sublane_sums(folded(slice(0, 2 * c_rows), cols))
    f = sublane_sums(folded(slice(2 * c_rows, 2 * c_rows + 2 * f_rows), 4 * LANES))
    sums_ref[...] = c + pltpu.roll(jnp.concatenate([f[:1], f[2 : cells + 1]], axis=0), HALF, 1)


def outer_kernel(first_ref, second_ref, band_ref, fold_ref, across_ref, part_ref, cover_in, fine_in, cover_ref, fine_ref, sums_ref, across, window, f_parts):
    tiles = cover_ref.shape[0] - 1
    ext = cover_ref.shape[1]
    rows = ext - 2 * EDGE
    even = lax.rem(lax.axis_index("row"), 2) == 0
    lane = iota((1, LANES), 1)
    cells = rows // BS
    both = 2 * EDGE
    touches = (lane < HALF) == (lax.axis_index("col") == 0)
    place = lax.axis_index("row")
    alone = (place == 0) | (place == lax.axis_size("row") - 1)

    def halo(t):
        a, b = first_ref[t], second_ref[t]
        if t == tiles:
            a, b = jnp.where(touches, a, 0.0), jnp.where(touches, b, 0.0)
        b = jnp.where(alone, 0.0, b)
        top = jnp.where(even, b, a)
        low = jnp.where(even, a, b)
        cover_ref[t, 0:EDGE, :] = top
        cover_ref[t, EDGE + rows :, :] = low
        return pltpu.roll(jnp.concatenate([top, low], axis=0), HALF, 1)

    before = halo(tiles)
    first = before
    for t in range(tiles + 1):
        here = halo(t) if t < tiles else first
        tile = jnp.where(lane < HALF, before, here).astype(BF16)
        window[t * both : (t + 1) * both, :LANES] = tile
        at = t - 1 if t else tiles
        window[at * both : (at + 1) * both, LANES:] = tile
        before = here
    twice = jnp.dot(window[...], band_ref[...], preferred_element_type=F32)
    once = twice[:, :LANES] + twice[:, LANES:]
    reach = 2 * PAD + 2 * EDGE
    for t in range(tiles + 1):
        across[t, 0:PAD, :] = jnp.zeros((PAD, LANES), F32)
        across[t, PAD : PAD + EDGE, :] = once[t * both : t * both + EDGE]
        across[t, PAD + EDGE : reach, :] = across_ref[t, PAD + EDGE : reach, :]
        low = reach
        across[t, low : low + PAD + EDGE, :] = across_ref[t, ext - PAD - EDGE : ext, :]
        across[t, low + PAD + EDGE : low + PAD + 2 * EDGE, :] = once[t * both + EDGE : (t + 1) * both]
        across[t, low + PAD + 2 * EDGE :, :] = jnp.zeros((PAD, LANES), F32)
        top = row_blur(lambda k: across[t, PAD + k : PAD + k + EDGE + 8, :])
        base = low + 8
        bot = row_blur(lambda k: across[t, base + k : base + k + EDGE + 8, :])
        fine_ref[t, 0 : EDGE + 8, :] = top
        fine_ref[t, EDGE + rows - 8 :, :] = bot
        if t < tiles:
            a = top[EDGE:] * cover_ref[t, EDGE : EDGE + 8, :]
            b = bot[:8] * cover_ref[t, EDGE + rows - 8 : EDGE + rows, :]
            span = slice(t * LANES, (t + 1) * LANES)
            f_parts[:16, span], f_parts[16:, span] = halves(jnp.concatenate([a, b], axis=0))
    f = sublane_sums(jnp.dot(f_parts[...], fold_ref[...], preferred_element_type=F32))
    row = iota((cells, LANES), 0)
    total = jnp.where(row == 0, f[0:1], jnp.where(row == cells - 1, f[1:2], 0.0))
    sums_ref[...] = part_ref[...] + pltpu.roll(total, HALF, 1)


def spread_kernel(cover_ref, after_ref, blurred_ref, above_ref, below_ref):
    del after_ref
    tiles, ext = cover_ref.shape[0] - 1, cover_ref.shape[1]
    rows = ext - 2 * EDGE
    scale = 0.5 / 255.0
    row = iota((8, LANES), 0)
    for t in range(tiles + 1):
        for a, n in chunks(0, rows):
            blurred_ref[t, a : a + n, :] = row_blur(lambda k: cover_ref[t, EDGE + a + k : EDGE + a + k + n, :], scale)
        for i in range(rows // BS):
            top = EDGE + i * BS
            low = top + BS - 8
            above = jnp.zeros((8, LANES), F32)
            below = jnp.zeros((8, LANES), F32)
            for k in range(1, HALO + 1):
                tap = F32(TAPS[k] * scale)
                above = above + jnp.where(row < k, tap * cover_ref[t, top - k : top - k + 8, :], 0.0)
                below = below + jnp.where(row >= 8 - k, tap * cover_ref[t, low + k : low + k + 8, :], 0.0)
            above_ref[t, i] = above
            below_ref[t, i] = below


def first_dose_kernel(cover_ref, fine_ref, after_ref, dose_ref, blurred_ref, charge):
    del after_ref
    tiles, ext = cover_ref.shape[0] - 1, cover_ref.shape[1]
    rows = ext - 2 * EDGE
    for t in range(tiles + 1):
        for a, n in [(0, EDGE)] + [(EDGE + a, n) for a, n in chunks(0, rows)] + [(EDGE + rows, EDGE)]:
            dose = 2.0 - F32(0.5 / 255.0) * fine_ref[t, a : a + n, :]
            if t < tiles and EDGE <= a < EDGE + rows:
                dose_ref[t, a - EDGE : a - EDGE + n, :] = dose
            charge[t, a : a + n, :] = (dose - 0.5) * cover_ref[t, a : a + n, :]
        for a, n in chunks(0, rows):
            blurred_ref[t, a : a + n, :] = row_blur(
                lambda k: charge[t, EDGE + a + k : EDGE + a + k + n, :], 0.5 / 255.0
            )


def last_kernel(gathered_ref, left_ref, own_ref, right_ref, band_ref, dose_ref, charge_ref, blurred_ref, above_ref, below_ref, out_ref, c_all, f_all, ring_ref, last_ref, window, turned, ends, staged, sems):
    rows, cols = out_ref.shape
    tiles = cols // LANES
    n_rows, n_cols = c_all.shape
    cells = rows // BS
    col = lax.axis_index("col")
    row = lax.axis_index("row")
    lane8 = iota((cells, LANES), 1)
    lane = iota((1, LANES), 1)
    count = n_rows // cells
    for j in range(count):
        mine = gathered_ref[j * cells : (j + 1) * cells, :]
        other = gathered_ref[(count + j) * cells : (count + j + 1) * cells, :]
        here = col == bin(j).count("1") % 2
        low = jnp.where(here, mine, other)
        high = jnp.where(here, other, mine)
        at = pl.ds(pl.multiple_of((row ^ j) * cells, cells), cells)
        c_all[at, :] = jnp.where(lane8 < HALF, low, pltpu.roll(high, HALF, 1)) * F32(1.0 / (255.0 * BS * BS))
        f_all[at, :] = jnp.where(lane8 < HALF, pltpu.roll(low, HALF, 1), high) * F32(1.0 / (255.0 * 255.0 * BS * BS))
    right = right_ref[...]

    def both(x):
        part = dot(x, right)
        return jnp.concatenate([part[:, :n_cols], part[:, n_cols:]], axis=0)

    c = c_all[...]
    spread = both(c)
    ring_ref[...] = dot(own_ref[...], spread)
    coarse = dot(left_ref[...], spread)
    back = (1.5 - coarse) * c - 0.5 * f_all[...]
    last_ref[...] = dot(own_ref[...], both(back))

    ring = ring_ref.shape[0]

    def expand(ref, t):
        if t < tiles:
            pick = iota((ring, LANES), 1) // BS + (col * (cols // BS) + t * (LANES // BS))
        else:
            pick = jnp.where(iota((ring, LANES), 1) < HALF, (col + 1) * (cols // BS), col * (cols // BS) - 1)
        pick = jnp.clip(pick, 0, n_cols - 1)
        parts = [jnp.take_along_axis(ref[i : i + 8, :], pick[i : i + 8], axis=1) for i in range(0, ring, 8)]
        return jnp.concatenate(parts, axis=0)

    def charge(t):
        value = expand(ring_ref, t)
        for i in range(cells):
            here = value[1 + i : 2 + i, :]
            up = value[i : 1 + i, :] - here
            down = value[2 + i : 3 + i, :] - here
            at = i * BS
            some = charge_ref[t, at : at + BS, :] - here * blurred_ref[t, at : at + BS, :]
            some = jnp.concatenate(
                [some[:8] - up * above_ref[t, i], some[8 : BS - 8], some[BS - 8 :] - down * below_ref[t, i]], axis=0
            )
            turned[t % 2, at : at + BS, :] = pltpu.roll(some, HALF, 1)

    def put(t, at, value):
        for i, part in enumerate(halves(value)):
            if t < tiles:
                window[t, at, 2 * i * LANES : (2 * i + 1) * LANES] = part
            if t:
                window[t - 1, at, (2 * i + 1) * LANES : (2 * i + 2) * LANES] = part

    def fill(t):
        if t < tiles:
            charge(t)
        for a, n in chunks(0, rows):
            at = slice(a, a + n)
            before = turned[(t - 1) % 2, at, :] if t else ends[at, :]
            here = turned[t % 2, at, :] if t < tiles else ends[at, :]
            put(t, at, jnp.where(lane < HALF, before, here))

    def copy(g):
        span = slice(2 * g * LANES, 2 * (g + 1) * LANES)
        return pltpu.make_async_copy(staged.at[:, span], out_ref.at[:, span], sems.at[g])

    def finish(g):
        part = window[2 * g : 2 * g + 2].reshape(2 * rows, 4 * LANES)
        band = band_ref[...]
        both = jnp.dot(part, jnp.concatenate([band, band], axis=0), preferred_element_type=F32)
        for t in (2 * g, 2 * g + 1):
            fine = both[(t % 2) * rows : (t % 2 + 1) * rows]
            coarse = expand(ring_ref, t)[1 : 1 + cells] + expand(last_ref, t)[1 : 1 + cells]
            for i in range(cells):
                at = slice(i * BS, (i + 1) * BS)
                value = dose_ref[t, at, :] - fine[at, :LANES] - fine[at, LANES:] - coarse[i : i + 1, :]
                staged[at, t * LANES : (t + 1) * LANES] = value
        copy(g).start()

    def stage(body):
        body()

    def start():
        charge(tiles)
        ends[...] = turned[tiles % 2]
        for t in range(3):
            fill(t)

    stage(start)
    for g in range(tiles // 2):

        def step(g=g):
            if g:
                finish(g - 1)
            for t in range(2 * g + 1, 2 * g + 3):
                if t > 2:
                    fill(t)

        if g:
            stage(step)
    stage(lambda: finish(tiles // 2 - 1))
    for g in range(tiles // 2):
        copy(g).wait()


def shards(coverage, fog_rows, fog_cols):
    rows, cols = coverage.shape
    row_count = lax.axis_size("row")
    col_count = lax.axis_size("col")
    tiles = cols // LANES
    back_rows, back_cols = rows // BS, cols // BS
    n_rows, n_cols = back_rows * row_count, back_cols * col_count
    ext = rows + 2 * EDGE
    if col_count != 2 or n_cols != LANES or row_count & (row_count - 1):
        raise ValueError("unsupported mesh")

    def move(value, target):
        both = [(r, c) for r in range(row_count) for c in range(col_count)]
        flat = [(r * col_count + c, target(r, c)) for r, c in both]
        return lax.ppermute(value, ("row", "col"), [(i, r * col_count + c) for i, (r, c) in flat])

    def shape(*dims, dtype=F32):
        return jax.ShapeDtypeStruct(dims, dtype)

    def call(kernel, outs, ins, *args, scratch=(), mib=16, name=None, aliases={}, ops=1):
        return pl.pallas_call(
            kernel,
            out_shape=outs,
            in_specs=ins,
            out_specs=(VMEM,) * len(outs),
            scratch_shapes=list(scratch),
            input_output_aliases=aliases,
            compiler_params=pltpu.CompilerParams(vmem_limit_bytes=mib << 20),
            cost_estimate=pl.CostEstimate(flops=ops * rows * cols, bytes_accessed=ops * rows * cols, transcendentals=0),
            name=name,
        )(*args)

    wide = shape(tiles + 1, ext, LANES)
    own_tiles = shape(tiles + 1, rows, LANES)
    hbm = pl.BlockSpec(memory_space=pltpu.HBM)
    edge, first_rows, second_rows, fog_r, fog_c = call(
        edges_kernel,
        (
            shape(ext, LANES),
            shape(tiles, EDGE, LANES),
            shape(tiles, EDGE, LANES),
            shape(*fog_rows.shape),
            shape(*fog_cols.shape),
        ),
        [hbm] * 3,
        *[pltpu.with_memory_space_constraint(x, pltpu.HBM) for x in (coverage, fog_rows, fog_cols)],
        scratch=[
            pltpu.VMEM((rows, LANES), jnp.int32),
            pltpu.VMEM((2, EDGE, cols), jnp.int32),
            pltpu.SemaphoreType.DMA((5,)),
        ],
        mib=2,
        name="edges",
    )

    side = move(edge, lambda r, c: (r, 1 - c))
    band, fold, left, own, right = call(
        prep_kernel,
        (
            shape(2 * LANES, 2 * LANES, dtype=BF16),
            shape(cols, LANES, dtype=BF16),
            shape(n_rows, 2 * n_rows),
            shape(16, 2 * n_rows),
            shape(n_cols, 2 * n_cols),
        ),
        [VMEM] * 2,
        fog_r,
        fog_c,
        mib=4,
        name="prep",
    )
    side, band = lax.optimization_barrier((side, band))
    corners = side[rows:].reshape(2, EDGE, LANES)

    first = move(jnp.concatenate([first_rows, corners[:1]], axis=0), lambda r, c: (r ^ 1, c))
    second = move(
        jnp.concatenate([second_rows, corners[1:]], axis=0),
        lambda r, c: (r, 1 - c) if r in (0, row_count - 1) else ((r + 1, c) if r % 2 else (r - 1, c)),
    )
    cover, fine, across, part = call(
        block_kernel,
        (
            wide,
            wide,
            shape(tiles + 1, ext + 2 * PAD, LANES),
            shape(back_rows, LANES),
        ),
        [VMEM] * 4,
        coverage,
        side,
        band,
        fold,
        scratch=[
            pltpu.VMEM((tiles + 1, 2 * BS, 2 * LANES), BF16),
            pltpu.VMEM((32 * (back_rows + 1), cols), BF16),
        ],
        mib=8,
        name="block",
    )
    cover, fine, sums = call(
        outer_kernel,
        (wide, wide, shape(back_rows, LANES)),
        [VMEM] * 8,
        first,
        second,
        band,
        fold,
        across,
        part,
        cover,
        fine,
        scratch=[
            pltpu.VMEM((tiles + 1, 4 * PAD + 4 * EDGE, LANES), F32),
            pltpu.VMEM(((tiles + 1) * 2 * EDGE, 2 * LANES), BF16),
            pltpu.VMEM((32, cols), BF16),
        ],
        aliases={6: 0, 7: 1},
        mib=8,
        name="outer",
    )

    few = shape(tiles + 1, back_rows, 8, LANES)

    def spread(after):
        return call(
            spread_kernel, (own_tiles, few, few), [VMEM] * 2, cover, after, mib=4, name="spread"
        )

    def first_dose(after):
        return call(
            first_dose_kernel,
            (shape(tiles, rows, LANES), own_tiles),
            [VMEM] * 3,
            cover,
            fine,
            after,
            scratch=[pltpu.VMEM((tiles + 1, ext, LANES), F32)],
            mib=8,
            name="dose",
        )

    pending = [spread, first_dose]
    done = []
    gathered = sums
    bit = 1
    while bit < row_count:
        other = move(gathered, lambda r, c: (r ^ bit, 1 - c))
        if bit > 1 and pending:
            results = pending.pop(0)(gathered)
            other, *results = lax.optimization_barrier((other, *results))
            done += results
        gathered = jnp.concatenate([gathered, other], axis=0)
        bit *= 2
    gathered = jnp.concatenate([gathered, move(gathered, lambda r, c: (r, 1 - c))], axis=0)
    for work in pending:
        done += work(gathered)
    blurred, above, below, dose, charge = done

    return pl.pallas_call(
        last_kernel,
        out_shape=shape(rows, cols),
        in_specs=[VMEM] * 10,
        out_specs=pl.BlockSpec(memory_space=pltpu.HBM),
        scratch_shapes=[
            pltpu.VMEM((n_rows, n_cols), F32),
            pltpu.VMEM((n_rows, n_cols), F32),
            pltpu.VMEM((16, n_cols), F32),
            pltpu.VMEM((16, n_cols), F32),
            pltpu.VMEM((tiles, rows, 4 * LANES), BF16),
            pltpu.VMEM((2, rows, LANES), F32),
            pltpu.VMEM((rows, LANES), F32),
            pltpu.VMEM((rows, cols), F32),
            pltpu.SemaphoreType.DMA((tiles // 2,)),
        ],
        compiler_params=pltpu.CompilerParams(vmem_limit_bytes=16 << 20),
        name="last",
    )(gathered, left, own, right, band, dose, charge, blurred, above, below)


def solution(mesh):
    in_specs = (P(("stripe", "row"), "col"), P(), P())
    out_specs = P(("stripe", "row"), "col")
    return jax.shard_map(shards, mesh=mesh, in_specs=in_specs, out_specs=out_specs, check_vma=False)
```

```python
import math

import jax
import jax.numpy as jnp
import numpy as np
from jax import lax
from jax.experimental import pallas as pl
from jax.experimental.pallas import tpu as pltpu
from jax.sharding import PartitionSpec as P

BS = 32
FB = 256
HALO = 4
BSIG = 16
REACH = 40
LANES = 128
HALF = LANES // 2
EDGE = 2 * HALO
PAD = 8
F32 = jnp.float32
BF16 = jnp.bfloat16
VMEM = pl.BlockSpec(memory_space=pltpu.VMEM)


def fine_taps():
    offsets = np.arange(-HALO, HALO + 1).astype(np.float32)
    raw = np.exp(np.float32(-0.5) * (offsets / np.float32(1.25)) ** 2).astype(np.float32)
    taps = (raw / raw.sum(dtype=np.float32)).astype(np.float32)
    return [float(taps[HALO + k]) for k in range(HALO + 1)]


TAPS = fine_taps()


def iota(shape, dim):
    return lax.broadcasted_iota(jnp.int32, shape, dim)


def tap_of(distance):
    value = jnp.zeros(distance.shape, F32)
    for k in range(HALO + 1):
        value = jnp.where(distance == k, F32(TAPS[k]), value)
    return value


def gauss(offsets):
    off = offsets.astype(F32)
    values = jnp.exp(-0.5 * (off / BSIG) ** 2) / (BSIG * math.sqrt(2.0 * math.pi))
    return jnp.where(jnp.abs(off) <= REACH, values, jnp.zeros_like(values))


def halves(x):
    upper = x.astype(BF16)
    return upper, (x - upper.astype(F32)).astype(BF16)


def dot(a, b):
    (ah, al), (bh, bl) = halves(a), halves(b)
    return jnp.dot(
        jnp.concatenate([ah, al, ah], axis=1),
        jnp.concatenate([bh, bh, bl], axis=0),
        preferred_element_type=F32,
    )


def full_dot(a, b, over=1):
    return lax.dot_general(
        a, b, (((over,), (0,)), ((), ())), precision=lax.Precision.HIGHEST, preferred_element_type=F32
    )


def prep(place, fog_rows, fog_cols, left_ref, own_ref, right_ref):
    n_rows = left_ref.shape[0]
    n_cols = right_ref.shape[0]
    side = FB // BS
    kr = fog_rows / jnp.sum(fog_rows, axis=1, keepdims=True)
    kc = fog_cols / jnp.sum(fog_cols, axis=1, keepdims=True)
    fr, fc = kr.shape[0], kc.shape[0]
    spread_r = (iota((fr, n_rows), 1) // side == iota((fr, n_rows), 0)).astype(F32)
    spread_c = (iota((fc, n_cols), 1) // side == iota((fc, n_cols), 0)).astype(F32)
    kr_cols = full_dot(kr, spread_r)

    def left(count, first):
        here = iota((count, n_rows), 0) + first
        weight = 0.3 * gauss(here - iota((count, n_rows), 1))
        cell = jnp.clip(iota((count, fr), 0) + first, 0, n_rows - 1) // side
        pick = (cell == iota((count, fr), 1)).astype(F32)
        return weight, full_dot(pick, kr_cols) * F32(0.2 / (side * side))

    left_ref[:, :n_rows], left_ref[:, n_rows:] = left(n_rows, 0)
    own_ref[:, :n_rows], own_ref[:, n_rows:] = left(own_ref.shape[0], place - 1)
    right_ref[:, :n_cols] = gauss(iota((n_cols, n_cols), 0) - iota((n_cols, n_cols), 1))
    right_ref[:, n_cols:] = full_dot(spread_c, full_dot(kc, spread_c, 0), 0)


def row_blur(load, scale=1.0):
    acc = F32(TAPS[0] * scale) * load(0)
    for k in range(1, HALO + 1):
        acc = acc + F32(TAPS[k] * scale) * (load(-k) + load(k))
    return acc


def eights(x):
    return sum((x[b : b + 8] for b in range(8, x.shape[0], 8)), x[:8])


def sublane_sums(x):
    half = x.shape[0] // 2
    x = x[:half] + x[half:]
    return x.reshape(half // 8, 8, LANES).sum(axis=1)


def chunks(start, stop, size=64):
    return [(a, min(size, stop - a)) for a in range(start, stop, size)]


def edges_kernel(cov_ref, fog_rows_ref, fog_cols_ref, edge_ref, first_ref, second_ref, fog_r, fog_c, tile, strips, sems):
    rows, cols = cov_ref.shape
    tiles = cols // LANES
    odd = lax.rem(lax.axis_index("row"), 2)
    over = pl.ds(pl.multiple_of((1 - lax.axis_index("col")) * (cols - LANES), LANES), LANES)
    copies = [pltpu.make_async_copy(cov_ref.at[:, over], tile, sems.at[0])]
    for i, start in enumerate((1 - odd, odd)):
        span = pl.ds(pl.multiple_of(start * (rows - EDGE), EDGE), EDGE)
        copies.append(pltpu.make_async_copy(cov_ref.at[span], strips.at[i], sems.at[1 + i]))
    copies.append(pltpu.make_async_copy(fog_rows_ref, fog_r, sems.at[3]))
    copies.append(pltpu.make_async_copy(fog_cols_ref, fog_c, sems.at[4]))
    for copy in copies:
        copy.start()
    for copy in copies:
        copy.wait()
    edge_ref[:rows, :] = tile[...].astype(F32)
    for i, start in enumerate((1 - odd, odd)):
        span = pl.ds(pl.multiple_of(start * (rows - EDGE), EDGE), EDGE)
        edge_ref[rows + i * EDGE : rows + (i + 1) * EDGE, :] = tile[span, :].astype(F32)
    for t in range(tiles):
        first_ref[t] = strips[0, :, t * LANES : (t + 1) * LANES].astype(F32)
        second_ref[t] = strips[1, :, t * LANES : (t + 1) * LANES].astype(F32)


def prep_kernel(fog_rows_ref, fog_cols_ref, band_ref, fold_ref, left_ref, own_ref, right_ref):
    tap = tap_of(jnp.abs(iota((2 * LANES, LANES), 0) - HALF - iota((2 * LANES, LANES), 1)))
    band_ref[:, :LANES], band_ref[:, LANES:] = halves(tap)
    for t in range(0, fold_ref.shape[0], LANES):
        group = (iota((LANES, LANES), 0) + t) // BS
        fold_ref[t : t + LANES, :] = (group == iota((LANES, LANES), 1)).astype(F32).astype(BF16)
    place = lax.axis_index("row") * (left_ref.shape[0] // lax.axis_size("row"))
    prep(place, fog_rows_ref[...], fog_cols_ref[...], left_ref, own_ref, right_ref)


def block_kernel(cov_ref, side_ref, band_ref, fold_ref, cover_ref, fine_ref, across, sums_ref, window, parts):
    rows, cols = cov_ref.shape
    tiles = cols // LANES
    part = 2 * BS
    pieces = rows // part
    cells = rows // BS
    lane = iota((1, LANES), 1)
    touches = (lane < HALF) == (lax.axis_index("col") == 0)
    c_rows, f_rows = 8 * cells, 8 * (cells + 2)

    def keep(base, height, low, span, values):
        for half, value in zip(range(2), halves(jnp.concatenate(values, axis=0))):
            at = base + half * height + low
            parts[at : at + 8 * len(values), span] = value

    for p in range(pieces):
        first = p * part
        at = slice(EDGE + first, EDGE + first + part)

        def put(t, value):
            window[t] = value
            if t == 0:
                window[tiles + 1] = value

        side = jnp.where(touches, side_ref[first : first + part, :], 0.0)
        cover_ref[tiles, at, :] = side
        side = pltpu.roll(side, HALF, 1)
        before = side
        for t in range(tiles):
            span = slice(t * LANES, (t + 1) * LANES)
            value = cov_ref[first : first + part, span].astype(F32)
            cover_ref[t, at, :] = value
            here = pltpu.roll(value, HALF, 1)
            put(t, jnp.where(lane < HALF, before, here).astype(BF16))
            before = here
            keep(0, c_rows, 8 * (first // BS), span, [eights(value[i : i + BS]) for i in range(0, part, BS)])
        put(tiles, jnp.where(lane < HALF, before, side).astype(BF16))
        for t, count in chunks(0, tiles + 1, 6):
            some = [jnp.concatenate([window[t + i], window[t + i + 1]], axis=1) for i in range(count)]
            both = jnp.dot(jnp.concatenate(some, axis=0), band_ref[...], preferred_element_type=F32)
            for i in range(count):
                mine = both[i * part : (i + 1) * part]
                across[t + i, PAD + EDGE + first : PAD + EDGE + first + part, :] = mine[:, :LANES] + mine[:, LANES:]
        ready = range(max(2 * p - 1, 0), 2 * p + 1 if p + 1 < pieces else cells)
        for t in range(tiles + 1):
            got = {}
            for i in ready:
                low, high = max(i * BS, 8), min((i + 1) * BS, rows - 8)
                base = PAD + EDGE + low
                fine = row_blur(lambda k: across[t, base + k : base + k + high - low, :])
                fine_ref[t, EDGE + low : EDGE + high, :] = fine
                if t < tiles:
                    got[i] = eights(cover_ref[t, EDGE + low : EDGE + high, :] * fine)
            if t < tiles:
                span = slice(t * LANES, (t + 1) * LANES)
                zero = jnp.zeros((8, LANES), F32)
                for i in got:
                    if i % 2 or i == 0:
                        pair = [got[i], got.get(i + 1, zero)] if i else [got[0], zero]
                        keep(2 * c_rows, f_rows, 8 * (i + 1) if i else 0, span, pair)
    def folded(some, step):
        return sum(
            jnp.dot(parts[some, a : a + step], fold_ref[a : a + step, :], preferred_element_type=F32)
            for a in range(0, cols, step)
        )

    c = sublane_sums(folded(slice(0, 2 * c_rows), cols))
    f = sublane_sums(folded(slice(2 * c_rows, 2 * c_rows + 2 * f_rows), 4 * LANES))
    sums_ref[...] = c + pltpu.roll(jnp.concatenate([f[:1], f[2 : cells + 1]], axis=0), HALF, 1)


def outer_kernel(first_ref, second_ref, band_ref, fold_ref, across_ref, part_ref, cover_in, fine_in, cover_ref, fine_ref, sums_ref, across, window, f_parts):
    tiles = cover_ref.shape[0] - 1
    ext = cover_ref.shape[1]
    rows = ext - 2 * EDGE
    even = lax.rem(lax.axis_index("row"), 2) == 0
    lane = iota((1, LANES), 1)
    cells = rows // BS
    both = 2 * EDGE
    touches = (lane < HALF) == (lax.axis_index("col") == 0)
    place = lax.axis_index("row")
    alone = (place == 0) | (place == lax.axis_size("row") - 1)

    def halo(t):
        a, b = first_ref[t], second_ref[t]
        if t == tiles:
            a, b = jnp.where(touches, a, 0.0), jnp.where(touches, b, 0.0)
        b = jnp.where(alone, 0.0, b)
        top = jnp.where(even, b, a)
        low = jnp.where(even, a, b)
        cover_ref[t, 0:EDGE, :] = top
        cover_ref[t, EDGE + rows :, :] = low
        return pltpu.roll(jnp.concatenate([top, low], axis=0), HALF, 1)

    before = halo(tiles)
    first = before
    for t in range(tiles + 1):
        here = halo(t) if t < tiles else first
        tile = jnp.where(lane < HALF, before, here).astype(BF16)
        window[t * both : (t + 1) * both, :LANES] = tile
        at = t - 1 if t else tiles
        window[at * both : (at + 1) * both, LANES:] = tile
        before = here
    twice = jnp.dot(window[...], band_ref[...], preferred_element_type=F32)
    once = twice[:, :LANES] + twice[:, LANES:]
    reach = 2 * PAD + 2 * EDGE
    for t in range(tiles + 1):
        across[t, 0:PAD, :] = jnp.zeros((PAD, LANES), F32)
        across[t, PAD : PAD + EDGE, :] = once[t * both : t * both + EDGE]
        across[t, PAD + EDGE : reach, :] = across_ref[t, PAD + EDGE : reach, :]
        low = reach
        across[t, low : low + PAD + EDGE, :] = across_ref[t, ext - PAD - EDGE : ext, :]
        across[t, low + PAD + EDGE : low + PAD + 2 * EDGE, :] = once[t * both + EDGE : (t + 1) * both]
        across[t, low + PAD + 2 * EDGE :, :] = jnp.zeros((PAD, LANES), F32)
        top = row_blur(lambda k: across[t, PAD + k : PAD + k + EDGE + 8, :])
        base = low + 8
        bot = row_blur(lambda k: across[t, base + k : base + k + EDGE + 8, :])
        fine_ref[t, 0 : EDGE + 8, :] = top
        fine_ref[t, EDGE + rows - 8 :, :] = bot
        if t < tiles:
            a = top[EDGE:] * cover_ref[t, EDGE : EDGE + 8, :]
            b = bot[:8] * cover_ref[t, EDGE + rows - 8 : EDGE + rows, :]
            span = slice(t * LANES, (t + 1) * LANES)
            f_parts[:16, span], f_parts[16:, span] = halves(jnp.concatenate([a, b], axis=0))
    f = sublane_sums(jnp.dot(f_parts[...], fold_ref[...], preferred_element_type=F32))
    row = iota((cells, LANES), 0)
    total = jnp.where(row == 0, f[0:1], jnp.where(row == cells - 1, f[1:2], 0.0))
    sums_ref[...] = part_ref[...] + pltpu.roll(total, HALF, 1)


def spread_kernel(cover_ref, after_ref, blurred_ref, above_ref, below_ref):
    del after_ref
    tiles, ext = cover_ref.shape[0] - 1, cover_ref.shape[1]
    rows = ext - 2 * EDGE
    scale = 0.5 / 255.0
    row = iota((8, LANES), 0)
    for t in range(tiles + 1):
        for a, n in chunks(0, rows):
            blurred_ref[t, a : a + n, :] = row_blur(lambda k: cover_ref[t, EDGE + a + k : EDGE + a + k + n, :], scale)
        for i in range(rows // BS):
            top = EDGE + i * BS
            low = top + BS - 8
            above = jnp.zeros((8, LANES), F32)
            below = jnp.zeros((8, LANES), F32)
            for k in range(1, HALO + 1):
                tap = F32(TAPS[k] * scale)
                above = above + jnp.where(row < k, tap * cover_ref[t, top - k : top - k + 8, :], 0.0)
                below = below + jnp.where(row >= 8 - k, tap * cover_ref[t, low + k : low + k + 8, :], 0.0)
            above_ref[t, i] = above
            below_ref[t, i] = below


def first_dose_kernel(cover_ref, fine_ref, after_ref, dose_ref, blurred_ref, charge):
    del after_ref
    tiles, ext = cover_ref.shape[0] - 1, cover_ref.shape[1]
    rows = ext - 2 * EDGE
    for t in range(tiles + 1):
        for a, n in [(0, EDGE)] + [(EDGE + a, n) for a, n in chunks(0, rows)] + [(EDGE + rows, EDGE)]:
            dose = 2.0 - F32(0.5 / 255.0) * fine_ref[t, a : a + n, :]
            if t < tiles and EDGE <= a < EDGE + rows:
                dose_ref[t, a - EDGE : a - EDGE + n, :] = dose
            charge[t, a : a + n, :] = (dose - 0.5) * cover_ref[t, a : a + n, :]
        for a, n in chunks(0, rows):
            blurred_ref[t, a : a + n, :] = row_blur(
                lambda k: charge[t, EDGE + a + k : EDGE + a + k + n, :], 0.5 / 255.0
            )


def last_kernel(gathered_ref, left_ref, own_ref, right_ref, band_ref, dose_ref, charge_ref, blurred_ref, above_ref, below_ref, out_ref, c_all, f_all, ring_ref, last_ref, window, turned, ends, staged, sems):
    rows, cols = out_ref.shape
    tiles = cols // LANES
    n_rows, n_cols = c_all.shape
    cells = rows // BS
    col = lax.axis_index("col")
    row = lax.axis_index("row")
    lane8 = iota((cells, LANES), 1)
    lane = iota((1, LANES), 1)
    count = n_rows // cells
    for j in range(count):
        mine = gathered_ref[j * cells : (j + 1) * cells, :]
        other = gathered_ref[(count + j) * cells : (count + j + 1) * cells, :]
        here = col == bin(j).count("1") % 2
        low = jnp.where(here, mine, other)
        high = jnp.where(here, other, mine)
        at = pl.ds(pl.multiple_of((row ^ j) * cells, cells), cells)
        c_all[at, :] = jnp.where(lane8 < HALF, low, pltpu.roll(high, HALF, 1)) * F32(1.0 / (255.0 * BS * BS))
        f_all[at, :] = jnp.where(lane8 < HALF, pltpu.roll(low, HALF, 1), high) * F32(1.0 / (255.0 * 255.0 * BS * BS))
    right = right_ref[...]

    def both(x):
        part = dot(x, right)
        return jnp.concatenate([part[:, :n_cols], part[:, n_cols:]], axis=0)

    c = c_all[...]
    spread = both(c)
    ring_ref[...] = dot(own_ref[...], spread)
    coarse = dot(left_ref[...], spread)
    back = (1.5 - coarse) * c - 0.5 * f_all[...]
    last_ref[...] = dot(own_ref[...], both(back))

    ring = ring_ref.shape[0]

    def expand(ref, t):
        if t < tiles:
            pick = iota((ring, LANES), 1) // BS + (col * (cols // BS) + t * (LANES // BS))
        else:
            pick = jnp.where(iota((ring, LANES), 1) < HALF, (col + 1) * (cols // BS), col * (cols // BS) - 1)
        pick = jnp.clip(pick, 0, n_cols - 1)
        parts = [jnp.take_along_axis(ref[i : i + 8, :], pick[i : i + 8], axis=1) for i in range(0, ring, 8)]
        return jnp.concatenate(parts, axis=0)

    def charge(t):
        value = expand(ring_ref, t)
        for i in range(cells):
            here = value[1 + i : 2 + i, :]
            up = value[i : 1 + i, :] - here
            down = value[2 + i : 3 + i, :] - here
            at = i * BS
            some = charge_ref[t, at : at + BS, :] - here * blurred_ref[t, at : at + BS, :]
            some = jnp.concatenate(
                [some[:8] - up * above_ref[t, i], some[8 : BS - 8], some[BS - 8 :] - down * below_ref[t, i]], axis=0
            )
            turned[t % 2, at : at + BS, :] = pltpu.roll(some, HALF, 1)

    def put(t, at, value):
        for i, part in enumerate(halves(value)):
            if t < tiles:
                window[t, at, 2 * i * LANES : (2 * i + 1) * LANES] = part
            if t:
                window[t - 1, at, (2 * i + 1) * LANES : (2 * i + 2) * LANES] = part

    def fill(t):
        if t < tiles:
            charge(t)
        for a, n in chunks(0, rows):
            at = slice(a, a + n)
            before = turned[(t - 1) % 2, at, :] if t else ends[at, :]
            here = turned[t % 2, at, :] if t < tiles else ends[at, :]
            put(t, at, jnp.where(lane < HALF, before, here))

    def copy(g):
        span = slice(2 * g * LANES, 2 * (g + 1) * LANES)
        return pltpu.make_async_copy(staged.at[:, span], out_ref.at[:, span], sems.at[g])

    def finish(g):
        part = window[2 * g : 2 * g + 2].reshape(2 * rows, 4 * LANES)
        band = band_ref[...]
        both = jnp.dot(part, jnp.concatenate([band, band], axis=0), preferred_element_type=F32)
        for t in (2 * g, 2 * g + 1):
            fine = both[(t % 2) * rows : (t % 2 + 1) * rows]
            coarse = expand(ring_ref, t)[1 : 1 + cells] + expand(last_ref, t)[1 : 1 + cells]
            for i in range(cells):
                at = slice(i * BS, (i + 1) * BS)
                value = dose_ref[t, at, :] - fine[at, :LANES] - fine[at, LANES:] - coarse[i : i + 1, :]
                staged[at, t * LANES : (t + 1) * LANES] = value
        copy(g).start()

    def stage(body):
        body()

    def start():
        charge(tiles)
        ends[...] = turned[tiles % 2]
        for t in range(3):
            fill(t)

    stage(start)
    for g in range(tiles // 2):

        def step(g=g):
            if g:
                finish(g - 1)
            for t in range(2 * g + 1, 2 * g + 3):
                if t > 2:
                    fill(t)

        if g:
            stage(step)
    stage(lambda: finish(tiles // 2 - 1))
    for g in range(tiles // 2):
        copy(g).wait()


def shards(coverage, fog_rows, fog_cols):
    rows, cols = coverage.shape
    row_count = lax.axis_size("row")
    col_count = lax.axis_size("col")
    tiles = cols // LANES
    back_rows, back_cols = rows // BS, cols // BS
    n_rows, n_cols = back_rows * row_count, back_cols * col_count
    ext = rows + 2 * EDGE
    if col_count != 2 or n_cols != LANES or row_count & (row_count - 1):
        raise ValueError("unsupported mesh")

    def move(value, target):
        both = [(r, c) for r in range(row_count) for c in range(col_count)]
        flat = [(r * col_count + c, target(r, c)) for r, c in both]
        return lax.ppermute(value, ("row", "col"), [(i, r * col_count + c) for i, (r, c) in flat])

    def shape(*dims, dtype=F32):
        return jax.ShapeDtypeStruct(dims, dtype)

    def call(kernel, outs, ins, *args, scratch=(), mib=16, name=None, aliases={}, ops=1):
        return pl.pallas_call(
            kernel,
            out_shape=outs,
            in_specs=ins,
            out_specs=(VMEM,) * len(outs),
            scratch_shapes=list(scratch),
            input_output_aliases=aliases,
            compiler_params=pltpu.CompilerParams(vmem_limit_bytes=mib << 20),
            cost_estimate=pl.CostEstimate(flops=ops * rows * cols, bytes_accessed=ops * rows * cols, transcendentals=0),
            name=name,
        )(*args)

    wide = shape(tiles + 1, ext, LANES)
    own_tiles = shape(tiles + 1, rows, LANES)
    hbm = pl.BlockSpec(memory_space=pltpu.HBM)
    edge, first_rows, second_rows, fog_r, fog_c = call(
        edges_kernel,
        (
            shape(ext, LANES),
            shape(tiles, EDGE, LANES),
            shape(tiles, EDGE, LANES),
            shape(*fog_rows.shape),
            shape(*fog_cols.shape),
        ),
        [hbm] * 3,
        *[pltpu.with_memory_space_constraint(x, pltpu.HBM) for x in (coverage, fog_rows, fog_cols)],
        scratch=[
            pltpu.VMEM((rows, LANES), jnp.int32),
            pltpu.VMEM((2, EDGE, cols), jnp.int32),
            pltpu.SemaphoreType.DMA((5,)),
        ],
        mib=2,
        name="edges",
    )

    side = move(edge, lambda r, c: (r, 1 - c))
    band, fold, left, own, right = call(
        prep_kernel,
        (
            shape(2 * LANES, 2 * LANES, dtype=BF16),
            shape(cols, LANES, dtype=BF16),
            shape(n_rows, 2 * n_rows),
            shape(16, 2 * n_rows),
            shape(n_cols, 2 * n_cols),
        ),
        [VMEM] * 2,
        fog_r,
        fog_c,
        mib=4,
        name="prep",
    )
    side, band = lax.optimization_barrier((side, band))
    corners = side[rows:].reshape(2, EDGE, LANES)

    first = move(jnp.concatenate([first_rows, corners[:1]], axis=0), lambda r, c: (r ^ 1, c))
    second = move(
        jnp.concatenate([second_rows, corners[1:]], axis=0),
        lambda r, c: (r, 1 - c) if r in (0, row_count - 1) else ((r + 1, c) if r % 2 else (r - 1, c)),
    )
    cover, fine, across, part = call(
        block_kernel,
        (
            wide,
            wide,
            shape(tiles + 1, ext + 2 * PAD, LANES),
            shape(back_rows, LANES),
        ),
        [VMEM] * 4,
        coverage,
        side,
        band,
        fold,
        scratch=[
            pltpu.VMEM((tiles + 2, 2 * BS, LANES), BF16),
            pltpu.VMEM((32 * (back_rows + 1), cols), BF16),
        ],
        mib=8,
        name="block",
    )
    cover, fine, sums = call(
        outer_kernel,
        (wide, wide, shape(back_rows, LANES)),
        [VMEM] * 8,
        first,
        second,
        band,
        fold,
        across,
        part,
        cover,
        fine,
        scratch=[
            pltpu.VMEM((tiles + 1, 4 * PAD + 4 * EDGE, LANES), F32),
            pltpu.VMEM(((tiles + 1) * 2 * EDGE, 2 * LANES), BF16),
            pltpu.VMEM((32, cols), BF16),
        ],
        aliases={6: 0, 7: 1},
        mib=8,
        name="outer",
    )

    few = shape(tiles + 1, back_rows, 8, LANES)

    def spread(after):
        return call(
            spread_kernel, (own_tiles, few, few), [VMEM] * 2, cover, after, mib=4, name="spread"
        )

    def first_dose(after):
        return call(
            first_dose_kernel,
            (shape(tiles, rows, LANES), own_tiles),
            [VMEM] * 3,
            cover,
            fine,
            after,
            scratch=[pltpu.VMEM((tiles + 1, ext, LANES), F32)],
            mib=8,
            name="dose",
        )

    pending = [spread, first_dose]
    done = []
    gathered = sums
    bit = 1
    while bit < row_count:
        other = move(gathered, lambda r, c: (r ^ bit, 1 - c))
        if pending:
            results = pending.pop(0)(gathered)
            other, *results = lax.optimization_barrier((other, *results))
            done += results
        gathered = jnp.concatenate([gathered, other], axis=0)
        bit *= 2
    gathered = jnp.concatenate([gathered, move(gathered, lambda r, c: (r, 1 - c))], axis=0)
    for work in pending:
        done += work(gathered)
    blurred, above, below, dose, charge = done

    return pl.pallas_call(
        last_kernel,
        out_shape=shape(rows, cols),
        in_specs=[VMEM] * 10,
        out_specs=pl.BlockSpec(memory_space=pltpu.HBM),
        scratch_shapes=[
            pltpu.VMEM((n_rows, n_cols), F32),
            pltpu.VMEM((n_rows, n_cols), F32),
            pltpu.VMEM((16, n_cols), F32),
            pltpu.VMEM((16, n_cols), F32),
            pltpu.VMEM((tiles, rows, 4 * LANES), BF16),
            pltpu.VMEM((2, rows, LANES), F32),
            pltpu.VMEM((rows, LANES), F32),
            pltpu.VMEM((rows, cols), F32),
            pltpu.SemaphoreType.DMA((tiles // 2,)),
        ],
        compiler_params=pltpu.CompilerParams(vmem_limit_bytes=16 << 20),
        name="last",
    )(gathered, left, own, right, band, dose, charge, blurred, above, below)


def solution(mesh):
    in_specs = (P(("stripe", "row"), "col"), P(), P())
    out_specs = P(("stripe", "row"), "col")
    return jax.shard_map(shards, mesh=mesh, in_specs=in_specs, out_specs=out_specs, check_vma=False)
```

```python
import math

import jax
import jax.numpy as jnp
import numpy as np
from jax import lax
from jax.experimental import pallas as pl
from jax.experimental.pallas import tpu as pltpu
from jax.sharding import PartitionSpec as P

BS = 32
FB = 256
HALO = 4
BSIG = 16
REACH = 40
LANES = 128
HALF = LANES // 2
EDGE = 2 * HALO
PAD = 8
F32 = jnp.float32
BF16 = jnp.bfloat16
VMEM = pl.BlockSpec(memory_space=pltpu.VMEM)


def fine_taps():
    offsets = np.arange(-HALO, HALO + 1).astype(np.float32)
    raw = np.exp(np.float32(-0.5) * (offsets / np.float32(1.25)) ** 2).astype(np.float32)
    taps = (raw / raw.sum(dtype=np.float32)).astype(np.float32)
    return [float(taps[HALO + k]) for k in range(HALO + 1)]


TAPS = fine_taps()


def iota(shape, dim):
    return lax.broadcasted_iota(jnp.int32, shape, dim)


def tap_of(distance):
    value = jnp.zeros(distance.shape, F32)
    for k in range(HALO + 1):
        value = jnp.where(distance == k, F32(TAPS[k]), value)
    return value


def gauss(offsets):
    off = offsets.astype(F32)
    values = jnp.exp(-0.5 * (off / BSIG) ** 2) / (BSIG * math.sqrt(2.0 * math.pi))
    return jnp.where(jnp.abs(off) <= REACH, values, jnp.zeros_like(values))


def halves(x):
    upper = x.astype(BF16)
    return upper, (x - upper.astype(F32)).astype(BF16)


def dot(a, b):
    (ah, al), (bh, bl) = halves(a), halves(b)
    return jnp.dot(
        jnp.concatenate([ah, al, ah], axis=1),
        jnp.concatenate([bh, bh, bl], axis=0),
        preferred_element_type=F32,
    )


def full_dot(a, b, over=1):
    return lax.dot_general(
        a, b, (((over,), (0,)), ((), ())), precision=lax.Precision.HIGHEST, preferred_element_type=F32
    )


def prep(place, fog_rows, fog_cols, left_ref, own_ref, right_ref):
    n_rows = left_ref.shape[0]
    n_cols = right_ref.shape[0]
    side = FB // BS
    kr = fog_rows / jnp.sum(fog_rows, axis=1, keepdims=True)
    kc = fog_cols / jnp.sum(fog_cols, axis=1, keepdims=True)
    fr, fc = kr.shape[0], kc.shape[0]
    spread_r = (iota((fr, n_rows), 1) // side == iota((fr, n_rows), 0)).astype(F32)
    spread_c = (iota((fc, n_cols), 1) // side == iota((fc, n_cols), 0)).astype(F32)
    kr_cols = full_dot(kr, spread_r)

    def left(count, first):
        here = iota((count, n_rows), 0) + first
        weight = 0.3 * gauss(here - iota((count, n_rows), 1))
        cell = jnp.clip(iota((count, fr), 0) + first, 0, n_rows - 1) // side
        pick = (cell == iota((count, fr), 1)).astype(F32)
        return weight, full_dot(pick, kr_cols) * F32(0.2 / (side * side))

    left_ref[:, :n_rows], left_ref[:, n_rows:] = left(n_rows, 0)
    own_ref[:, :n_rows], own_ref[:, n_rows:] = left(own_ref.shape[0], place - 1)
    right_ref[:, :n_cols] = gauss(iota((n_cols, n_cols), 0) - iota((n_cols, n_cols), 1))
    right_ref[:, n_cols:] = full_dot(spread_c, full_dot(kc, spread_c, 0), 0)


def row_blur(load, scale=1.0):
    acc = F32(TAPS[0] * scale) * load(0)
    for k in range(1, HALO + 1):
        acc = acc + F32(TAPS[k] * scale) * (load(-k) + load(k))
    return acc


def eights(x):
    return sum((x[b : b + 8] for b in range(8, x.shape[0], 8)), x[:8])


def sublane_sums(x):
    half = x.shape[0] // 2
    x = x[:half] + x[half:]
    return x.reshape(half // 8, 8, LANES).sum(axis=1)


def chunks(start, stop, size=64):
    return [(a, min(size, stop - a)) for a in range(start, stop, size)]


def edges_kernel(cov_ref, fog_rows_ref, fog_cols_ref, edge_ref, first_ref, second_ref, fog_r, fog_c, tile, strips, sems):
    rows, cols = cov_ref.shape
    tiles = cols // LANES
    odd = lax.rem(lax.axis_index("row"), 2)
    over = pl.ds(pl.multiple_of((1 - lax.axis_index("col")) * (cols - LANES), LANES), LANES)
    copies = [pltpu.make_async_copy(cov_ref.at[:, over], tile, sems.at[0])]
    for i, start in enumerate((1 - odd, odd)):
        span = pl.ds(pl.multiple_of(start * (rows - EDGE), EDGE), EDGE)
        copies.append(pltpu.make_async_copy(cov_ref.at[span], strips.at[i], sems.at[1 + i]))
    copies.append(pltpu.make_async_copy(fog_rows_ref, fog_r, sems.at[3]))
    copies.append(pltpu.make_async_copy(fog_cols_ref, fog_c, sems.at[4]))
    for copy in copies:
        copy.start()
    for copy in copies:
        copy.wait()
    edge_ref[:rows, :] = tile[...].astype(F32)
    for i, start in enumerate((1 - odd, odd)):
        span = pl.ds(pl.multiple_of(start * (rows - EDGE), EDGE), EDGE)
        edge_ref[rows + i * EDGE : rows + (i + 1) * EDGE, :] = tile[span, :].astype(F32)
    for t in range(tiles):
        first_ref[t] = strips[0, :, t * LANES : (t + 1) * LANES].astype(F32)
        second_ref[t] = strips[1, :, t * LANES : (t + 1) * LANES].astype(F32)


def prep_kernel(fog_rows_ref, fog_cols_ref, band_ref, fold_ref, left_ref, own_ref, right_ref):
    tap = tap_of(jnp.abs(iota((2 * LANES, LANES), 0) - HALF - iota((2 * LANES, LANES), 1)))
    band_ref[:, :LANES], band_ref[:, LANES:] = halves(tap)
    for t in range(0, fold_ref.shape[0], LANES):
        group = (iota((LANES, LANES), 0) + t) // BS
        fold_ref[t : t + LANES, :] = (group == iota((LANES, LANES), 1)).astype(F32).astype(BF16)
    place = lax.axis_index("row") * (left_ref.shape[0] // lax.axis_size("row"))
    prep(place, fog_rows_ref[...], fog_cols_ref[...], left_ref, own_ref, right_ref)


def block_kernel(cov_ref, side_ref, band_ref, fold_ref, cover_ref, fine_ref, across, sums_ref, window, parts):
    rows, cols = cov_ref.shape
    tiles = cols // LANES
    part = 2 * BS
    pieces = rows // part
    cells = rows // BS
    lane = iota((1, LANES), 1)
    touches = (lane < HALF) == (lax.axis_index("col") == 0)
    c_rows, f_rows = 8 * cells, 8 * (cells + 2)

    def keep(base, height, low, span, values):
        for half, value in zip(range(2), halves(jnp.concatenate(values, axis=0))):
            at = base + half * height + low
            parts[at : at + 8 * len(values), span] = value

    for p in range(pieces):
        first = p * part
        at = slice(EDGE + first, EDGE + first + part)

        def put(t, value):
            window[t] = value
            if t == 0:
                window[tiles + 1] = value

        side = jnp.where(touches, side_ref[first : first + part, :], 0.0)
        cover_ref[tiles, at, :] = side
        side = pltpu.roll(side, HALF, 1)
        before = side
        for t in range(tiles):
            span = slice(t * LANES, (t + 1) * LANES)
            value = cov_ref[first : first + part, span].astype(F32)
            cover_ref[t, at, :] = value
            here = pltpu.roll(value, HALF, 1)
            put(t, jnp.where(lane < HALF, before, here).astype(BF16))
            before = here
            keep(0, c_rows, 8 * (first // BS), span, [eights(value[i : i + BS]) for i in range(0, part, BS)])
        put(tiles, jnp.where(lane < HALF, before, side).astype(BF16))
        for t, count in chunks(0, tiles + 1, 6):
            some = [jnp.concatenate([window[t + i], window[t + i + 1]], axis=1) for i in range(count)]
            both = jnp.dot(jnp.concatenate(some, axis=0), band_ref[...], preferred_element_type=F32)
            for i in range(count):
                mine = both[i * part : (i + 1) * part]
                across[t + i, PAD + EDGE + first : PAD + EDGE + first + part, :] = mine[:, :LANES] + mine[:, LANES:]
        ready = range(max(2 * p - 1, 0), 2 * p + 1 if p + 1 < pieces else cells)
        for t in range(tiles + 1):
            got = {}
            for i in ready:
                low, high = max(i * BS, 8), min((i + 1) * BS, rows - 8)
                base = PAD + EDGE + low
                fine = row_blur(lambda k: across[t, base + k : base + k + high - low, :])
                fine_ref[t, EDGE + low : EDGE + high, :] = fine
                if t < tiles:
                    got[i] = eights(cover_ref[t, EDGE + low : EDGE + high, :] * fine)
            if t < tiles:
                span = slice(t * LANES, (t + 1) * LANES)
                zero = jnp.zeros((8, LANES), F32)
                for i in got:
                    if i % 2 or i == 0:
                        pair = [got[i], got.get(i + 1, zero)] if i else [got[0], zero]
                        keep(2 * c_rows, f_rows, 8 * (i + 1) if i else 0, span, pair)
    def folded(some, step):
        return sum(
            jnp.dot(parts[some, a : a + step], fold_ref[a : a + step, :], preferred_element_type=F32)
            for a in range(0, cols, step)
        )

    c = sublane_sums(folded(slice(0, 2 * c_rows), cols))
    f = sublane_sums(folded(slice(2 * c_rows, 2 * c_rows + 2 * f_rows), 4 * LANES))
    sums_ref[...] = c + pltpu.roll(jnp.concatenate([f[:1], f[2 : cells + 1]], axis=0), HALF, 1)


def outer_kernel(first_ref, second_ref, band_ref, fold_ref, across_ref, part_ref, cover_in, fine_in, cover_ref, fine_ref, sums_ref, across, window, f_parts):
    tiles = cover_ref.shape[0] - 1
    ext = cover_ref.shape[1]
    rows = ext - 2 * EDGE
    even = lax.rem(lax.axis_index("row"), 2) == 0
    lane = iota((1, LANES), 1)
    cells = rows // BS
    both = 2 * EDGE
    touches = (lane < HALF) == (lax.axis_index("col") == 0)
    place = lax.axis_index("row")
    alone = (place == 0) | (place == lax.axis_size("row") - 1)

    def halo(t):
        a, b = first_ref[t], second_ref[t]
        if t == tiles:
            a, b = jnp.where(touches, a, 0.0), jnp.where(touches, b, 0.0)
        b = jnp.where(alone, 0.0, b)
        top = jnp.where(even, b, a)
        low = jnp.where(even, a, b)
        cover_ref[t, 0:EDGE, :] = top
        cover_ref[t, EDGE + rows :, :] = low
        return pltpu.roll(jnp.concatenate([top, low], axis=0), HALF, 1)

    before = halo(tiles)
    first = before
    for t in range(tiles + 1):
        here = halo(t) if t < tiles else first
        tile = jnp.where(lane < HALF, before, here).astype(BF16)
        window[t * both : (t + 1) * both, :LANES] = tile
        at = t - 1 if t else tiles
        window[at * both : (at + 1) * both, LANES:] = tile
        before = here
    twice = jnp.dot(window[...], band_ref[...], preferred_element_type=F32)
    once = twice[:, :LANES] + twice[:, LANES:]
    reach = 2 * PAD + 2 * EDGE
    for t in range(tiles + 1):
        across[t, 0:PAD, :] = jnp.zeros((PAD, LANES), F32)
        across[t, PAD : PAD + EDGE, :] = once[t * both : t * both + EDGE]
        across[t, PAD + EDGE : reach, :] = across_ref[t, PAD + EDGE : reach, :]
        low = reach
        across[t, low : low + PAD + EDGE, :] = across_ref[t, ext - PAD - EDGE : ext, :]
        across[t, low + PAD + EDGE : low + PAD + 2 * EDGE, :] = once[t * both + EDGE : (t + 1) * both]
        across[t, low + PAD + 2 * EDGE :, :] = jnp.zeros((PAD, LANES), F32)
        top = row_blur(lambda k: across[t, PAD + k : PAD + k + EDGE + 8, :])
        base = low + 8
        bot = row_blur(lambda k: across[t, base + k : base + k + EDGE + 8, :])
        fine_ref[t, 0 : EDGE + 8, :] = top
        fine_ref[t, EDGE + rows - 8 :, :] = bot
        if t < tiles:
            a = top[EDGE:] * cover_ref[t, EDGE : EDGE + 8, :]
            b = bot[:8] * cover_ref[t, EDGE + rows - 8 : EDGE + rows, :]
            span = slice(t * LANES, (t + 1) * LANES)
            f_parts[:16, span], f_parts[16:, span] = halves(jnp.concatenate([a, b], axis=0))
    f = sublane_sums(jnp.dot(f_parts[...], fold_ref[...], preferred_element_type=F32))
    row = iota((cells, LANES), 0)
    total = jnp.where(row == 0, f[0:1], jnp.where(row == cells - 1, f[1:2], 0.0))
    sums_ref[...] = part_ref[...] + pltpu.roll(total, HALF, 1)


def spread_kernel(cover_ref, after_ref, blurred_ref, above_ref, below_ref):
    del after_ref
    tiles, ext = cover_ref.shape[0] - 1, cover_ref.shape[1]
    rows = ext - 2 * EDGE
    scale = 0.5 / 255.0
    row = iota((8, LANES), 0)
    for t in range(tiles + 1):
        for a, n in chunks(0, rows):
            blurred_ref[t, a : a + n, :] = row_blur(lambda k: cover_ref[t, EDGE + a + k : EDGE + a + k + n, :], scale)
        for i in range(rows // BS):
            top = EDGE + i * BS
            low = top + BS - 8
            above = jnp.zeros((8, LANES), F32)
            below = jnp.zeros((8, LANES), F32)
            for k in range(1, HALO + 1):
                tap = F32(TAPS[k] * scale)
                above = above + jnp.where(row < k, tap * cover_ref[t, top - k : top - k + 8, :], 0.0)
                below = below + jnp.where(row >= 8 - k, tap * cover_ref[t, low + k : low + k + 8, :], 0.0)
            above_ref[t, i] = above
            below_ref[t, i] = below


def first_dose_kernel(cover_ref, fine_ref, after_ref, dose_ref, blurred_ref, charge):
    del after_ref
    tiles, ext = cover_ref.shape[0] - 1, cover_ref.shape[1]
    rows = ext - 2 * EDGE
    for t in range(tiles + 1):
        for a, n in [(0, EDGE)] + [(EDGE + a, n) for a, n in chunks(0, rows)] + [(EDGE + rows, EDGE)]:
            dose = 2.0 - F32(0.5 / 255.0) * fine_ref[t, a : a + n, :]
            if t < tiles and EDGE <= a < EDGE + rows:
                dose_ref[t, a - EDGE : a - EDGE + n, :] = dose
            charge[t, a : a + n, :] = (dose - 0.5) * cover_ref[t, a : a + n, :]
        for a, n in chunks(0, rows):
            blurred_ref[t, a : a + n, :] = row_blur(
                lambda k: charge[t, EDGE + a + k : EDGE + a + k + n, :], 0.5 / 255.0
            )


def last_kernel(gathered_ref, left_ref, own_ref, right_ref, band_ref, dose_ref, charge_ref, blurred_ref, above_ref, below_ref, out_ref, c_all, f_all, ring_ref, last_ref, window, turned, ends, staged, sems):
    rows, cols = out_ref.shape
    tiles = cols // LANES
    n_rows, n_cols = c_all.shape
    cells = rows // BS
    col = lax.axis_index("col")
    row = lax.axis_index("row")
    lane8 = iota((cells, LANES), 1)
    lane = iota((1, LANES), 1)
    count = n_rows // cells
    for j in range(count):
        far = sum(count // 2 >> i for i in range(count.bit_length() - 1) if j >> i & 1)
        mine = gathered_ref[j * cells : (j + 1) * cells, :]
        other = gathered_ref[(count + j) * cells : (count + j + 1) * cells, :]
        here = col == bin(j).count("1") % 2
        low = jnp.where(here, mine, other)
        high = jnp.where(here, other, mine)
        at = pl.ds(pl.multiple_of((row ^ far) * cells, cells), cells)
        c_all[at, :] = jnp.where(lane8 < HALF, low, pltpu.roll(high, HALF, 1)) * F32(1.0 / (255.0 * BS * BS))
        f_all[at, :] = jnp.where(lane8 < HALF, pltpu.roll(low, HALF, 1), high) * F32(1.0 / (255.0 * 255.0 * BS * BS))
    right = right_ref[...]

    def both(x):
        part = dot(x, right)
        return jnp.concatenate([part[:, :n_cols], part[:, n_cols:]], axis=0)

    c = c_all[...]
    spread = both(c)
    ring_ref[...] = dot(own_ref[...], spread)
    coarse = dot(left_ref[...], spread)
    back = (1.5 - coarse) * c - 0.5 * f_all[...]
    last_ref[...] = dot(own_ref[...], both(back))

    ring = ring_ref.shape[0]

    def expand(ref, t):
        if t < tiles:
            pick = iota((ring, LANES), 1) // BS + (col * (cols // BS) + t * (LANES // BS))
        else:
            pick = jnp.where(iota((ring, LANES), 1) < HALF, (col + 1) * (cols // BS), col * (cols // BS) - 1)
        pick = jnp.clip(pick, 0, n_cols - 1)
        parts = [jnp.take_along_axis(ref[i : i + 8, :], pick[i : i + 8], axis=1) for i in range(0, ring, 8)]
        return jnp.concatenate(parts, axis=0)

    def charge(t):
        value = expand(ring_ref, t)
        for i in range(cells):
            here = value[1 + i : 2 + i, :]
            up = value[i : 1 + i, :] - here
            down = value[2 + i : 3 + i, :] - here
            at = i * BS
            some = charge_ref[t, at : at + BS, :] - here * blurred_ref[t, at : at + BS, :]
            some = jnp.concatenate(
                [some[:8] - up * above_ref[t, i], some[8 : BS - 8], some[BS - 8 :] - down * below_ref[t, i]], axis=0
            )
            turned[t % 2, at : at + BS, :] = pltpu.roll(some, HALF, 1)

    def put(t, at, value):
        for i, part in enumerate(halves(value)):
            if t < tiles:
                window[t, at, 2 * i * LANES : (2 * i + 1) * LANES] = part
            if t:
                window[t - 1, at, (2 * i + 1) * LANES : (2 * i + 2) * LANES] = part

    def fill(t):
        if t < tiles:
            charge(t)
        for a, n in chunks(0, rows):
            at = slice(a, a + n)
            before = turned[(t - 1) % 2, at, :] if t else ends[at, :]
            here = turned[t % 2, at, :] if t < tiles else ends[at, :]
            put(t, at, jnp.where(lane < HALF, before, here))

    def copy(g):
        span = slice(2 * g * LANES, 2 * (g + 1) * LANES)
        return pltpu.make_async_copy(staged.at[:, span], out_ref.at[:, span], sems.at[g])

    def finish(g):
        part = window[2 * g : 2 * g + 2].reshape(2 * rows, 4 * LANES)
        band = band_ref[...]
        both = jnp.dot(part, jnp.concatenate([band, band], axis=0), preferred_element_type=F32)
        for t in (2 * g, 2 * g + 1):
            fine = both[(t % 2) * rows : (t % 2 + 1) * rows]
            coarse = expand(ring_ref, t)[1 : 1 + cells] + expand(last_ref, t)[1 : 1 + cells]
            for i in range(cells):
                at = slice(i * BS, (i + 1) * BS)
                value = dose_ref[t, at, :] - fine[at, :LANES] - fine[at, LANES:] - coarse[i : i + 1, :]
                staged[at, t * LANES : (t + 1) * LANES] = value
        copy(g).start()

    def stage(body):
        body()

    def start():
        charge(tiles)
        ends[...] = turned[tiles % 2]
        for t in range(3):
            fill(t)

    stage(start)
    for g in range(tiles // 2):

        def step(g=g):
            if g:
                finish(g - 1)
            for t in range(2 * g + 1, 2 * g + 3):
                if t > 2:
                    fill(t)

        if g:
            stage(step)
    stage(lambda: finish(tiles // 2 - 1))
    for g in range(tiles // 2):
        copy(g).wait()


def shards(coverage, fog_rows, fog_cols):
    rows, cols = coverage.shape
    row_count = lax.axis_size("row")
    col_count = lax.axis_size("col")
    tiles = cols // LANES
    back_rows, back_cols = rows // BS, cols // BS
    n_rows, n_cols = back_rows * row_count, back_cols * col_count
    ext = rows + 2 * EDGE
    if col_count != 2 or n_cols != LANES or row_count & (row_count - 1):
        raise ValueError("unsupported mesh")

    def move(value, target):
        both = [(r, c) for r in range(row_count) for c in range(col_count)]
        flat = [(r * col_count + c, target(r, c)) for r, c in both]
        return lax.ppermute(value, ("row", "col"), [(i, r * col_count + c) for i, (r, c) in flat])

    def shape(*dims, dtype=F32):
        return jax.ShapeDtypeStruct(dims, dtype)

    def call(kernel, outs, ins, *args, scratch=(), mib=16, name=None, aliases={}, ops=1):
        return pl.pallas_call(
            kernel,
            out_shape=outs,
            in_specs=ins,
            out_specs=(VMEM,) * len(outs),
            scratch_shapes=list(scratch),
            input_output_aliases=aliases,
            compiler_params=pltpu.CompilerParams(vmem_limit_bytes=mib << 20),
            cost_estimate=pl.CostEstimate(flops=ops * rows * cols, bytes_accessed=ops * rows * cols, transcendentals=0),
            name=name,
        )(*args)

    wide = shape(tiles + 1, ext, LANES)
    own_tiles = shape(tiles + 1, rows, LANES)
    hbm = pl.BlockSpec(memory_space=pltpu.HBM)
    edge, first_rows, second_rows, fog_r, fog_c = call(
        edges_kernel,
        (
            shape(ext, LANES),
            shape(tiles, EDGE, LANES),
            shape(tiles, EDGE, LANES),
            shape(*fog_rows.shape),
            shape(*fog_cols.shape),
        ),
        [hbm] * 3,
        *[pltpu.with_memory_space_constraint(x, pltpu.HBM) for x in (coverage, fog_rows, fog_cols)],
        scratch=[
            pltpu.VMEM((rows, LANES), jnp.int32),
            pltpu.VMEM((2, EDGE, cols), jnp.int32),
            pltpu.SemaphoreType.DMA((5,)),
        ],
        mib=2,
        name="edges",
    )

    side = move(edge, lambda r, c: (r, 1 - c))
    band, fold, left, own, right = call(
        prep_kernel,
        (
            shape(2 * LANES, 2 * LANES, dtype=BF16),
            shape(cols, LANES, dtype=BF16),
            shape(n_rows, 2 * n_rows),
            shape(16, 2 * n_rows),
            shape(n_cols, 2 * n_cols),
        ),
        [VMEM] * 2,
        fog_r,
        fog_c,
        mib=4,
        name="prep",
    )
    side, band = lax.optimization_barrier((side, band))
    corners = side[rows:].reshape(2, EDGE, LANES)

    first = move(jnp.concatenate([first_rows, corners[:1]], axis=0), lambda r, c: (r ^ 1, c))
    second = move(
        jnp.concatenate([second_rows, corners[1:]], axis=0),
        lambda r, c: (r, 1 - c) if r in (0, row_count - 1) else ((r + 1, c) if r % 2 else (r - 1, c)),
    )
    cover, fine, across, part = call(
        block_kernel,
        (
            wide,
            wide,
            shape(tiles + 1, ext + 2 * PAD, LANES),
            shape(back_rows, LANES),
        ),
        [VMEM] * 4,
        coverage,
        side,
        band,
        fold,
        scratch=[
            pltpu.VMEM((tiles + 2, 2 * BS, LANES), BF16),
            pltpu.VMEM((32 * (back_rows + 1), cols), BF16),
        ],
        mib=8,
        name="block",
    )
    cover, fine, sums = call(
        outer_kernel,
        (wide, wide, shape(back_rows, LANES)),
        [VMEM] * 8,
        first,
        second,
        band,
        fold,
        across,
        part,
        cover,
        fine,
        scratch=[
            pltpu.VMEM((tiles + 1, 4 * PAD + 4 * EDGE, LANES), F32),
            pltpu.VMEM(((tiles + 1) * 2 * EDGE, 2 * LANES), BF16),
            pltpu.VMEM((32, cols), BF16),
        ],
        aliases={6: 0, 7: 1},
        mib=8,
        name="outer",
    )

    few = shape(tiles + 1, back_rows, 8, LANES)

    def spread(after):
        return call(
            spread_kernel, (own_tiles, few, few), [VMEM] * 2, cover, after, mib=4, name="spread"
        )

    def first_dose(after):
        return call(
            first_dose_kernel,
            (shape(tiles, rows, LANES), own_tiles),
            [VMEM] * 3,
            cover,
            fine,
            after,
            scratch=[pltpu.VMEM((tiles + 1, ext, LANES), F32)],
            mib=8,
            name="dose",
        )

    pending = [spread, first_dose]
    done = []
    gathered = sums
    bit = row_count // 2
    while bit:
        other = move(gathered, lambda r, c: (r ^ bit, 1 - c))
        if pending:
            results = pending.pop(0)(gathered)
            other, *results = lax.optimization_barrier((other, *results))
            done += results
        gathered = jnp.concatenate([gathered, other], axis=0)
        bit //= 2
    gathered = jnp.concatenate([gathered, move(gathered, lambda r, c: (r, 1 - c))], axis=0)
    for work in pending:
        done += work(gathered)
    blurred, above, below, dose, charge = done

    return pl.pallas_call(
        last_kernel,
        out_shape=shape(rows, cols),
        in_specs=[VMEM] * 10,
        out_specs=pl.BlockSpec(memory_space=pltpu.HBM),
        scratch_shapes=[
            pltpu.VMEM((n_rows, n_cols), F32),
            pltpu.VMEM((n_rows, n_cols), F32),
            pltpu.VMEM((16, n_cols), F32),
            pltpu.VMEM((16, n_cols), F32),
            pltpu.VMEM((tiles, rows, 4 * LANES), BF16),
            pltpu.VMEM((2, rows, LANES), F32),
            pltpu.VMEM((rows, LANES), F32),
            pltpu.VMEM((rows, cols), F32),
            pltpu.SemaphoreType.DMA((tiles // 2,)),
        ],
        compiler_params=pltpu.CompilerParams(vmem_limit_bytes=16 << 20),
        name="last",
    )(gathered, left, own, right, band, dose, charge, blurred, above, below)


def solution(mesh):
    in_specs = (P(("stripe", "row"), "col"), P(), P())
    out_specs = P(("stripe", "row"), "col")
    return jax.shard_map(shards, mesh=mesh, in_specs=in_specs, out_specs=out_specs, check_vma=False)
```

```python
import math

import jax
import jax.numpy as jnp
import numpy as np
from jax import lax
from jax.experimental import pallas as pl
from jax.experimental.pallas import tpu as pltpu
from jax.sharding import PartitionSpec as P

BS = 32
FB = 256
HALO = 4
BSIG = 16
REACH = 40
LANES = 128
HALF = LANES // 2
EDGE = 2 * HALO
PAD = 8
F32 = jnp.float32
BF16 = jnp.bfloat16
VMEM = pl.BlockSpec(memory_space=pltpu.VMEM)


def fine_taps():
    offsets = np.arange(-HALO, HALO + 1).astype(np.float32)
    raw = np.exp(np.float32(-0.5) * (offsets / np.float32(1.25)) ** 2).astype(np.float32)
    taps = (raw / raw.sum(dtype=np.float32)).astype(np.float32)
    return [float(taps[HALO + k]) for k in range(HALO + 1)]


TAPS = fine_taps()


def iota(shape, dim):
    return lax.broadcasted_iota(jnp.int32, shape, dim)


def tap_of(distance):
    value = jnp.zeros(distance.shape, F32)
    for k in range(HALO + 1):
        value = jnp.where(distance == k, F32(TAPS[k]), value)
    return value


def gauss(offsets):
    off = offsets.astype(F32)
    values = jnp.exp(-0.5 * (off / BSIG) ** 2) / (BSIG * math.sqrt(2.0 * math.pi))
    return jnp.where(jnp.abs(off) <= REACH, values, jnp.zeros_like(values))


def halves(x):
    upper = x.astype(BF16)
    return upper, (x - upper.astype(F32)).astype(BF16)


def dot(a, b):
    (ah, al), (bh, bl) = halves(a), halves(b)
    return jnp.dot(
        jnp.concatenate([ah, al, ah], axis=1),
        jnp.concatenate([bh, bh, bl], axis=0),
        preferred_element_type=F32,
    )


def full_dot(a, b, over=1):
    return lax.dot_general(
        a, b, (((over,), (0,)), ((), ())), precision=lax.Precision.HIGHEST, preferred_element_type=F32
    )


def prep(place, fog_rows, fog_cols, left_ref, own_ref, right_ref):
    n_rows = left_ref.shape[0]
    n_cols = right_ref.shape[0]
    side = FB // BS
    kr = fog_rows / jnp.sum(fog_rows, axis=1, keepdims=True)
    kc = fog_cols / jnp.sum(fog_cols, axis=1, keepdims=True)
    fr, fc = kr.shape[0], kc.shape[0]
    spread_r = (iota((fr, n_rows), 1) // side == iota((fr, n_rows), 0)).astype(F32)
    spread_c = (iota((fc, n_cols), 1) // side == iota((fc, n_cols), 0)).astype(F32)
    kr_cols = full_dot(kr, spread_r)

    def left(count, first):
        here = iota((count, n_rows), 0) + first
        weight = 0.3 * gauss(here - iota((count, n_rows), 1))
        cell = jnp.clip(iota((count, fr), 0) + first, 0, n_rows - 1) // side
        pick = (cell == iota((count, fr), 1)).astype(F32)
        return weight, full_dot(pick, kr_cols) * F32(0.2 / (side * side))

    left_ref[:, :n_rows], left_ref[:, n_rows:] = left(n_rows, 0)
    own_ref[:, :n_rows], own_ref[:, n_rows:] = left(own_ref.shape[0], place - 1)
    right_ref[:, :n_cols] = gauss(iota((n_cols, n_cols), 0) - iota((n_cols, n_cols), 1))
    right_ref[:, n_cols:] = full_dot(spread_c, full_dot(kc, spread_c, 0), 0)


def row_blur(load, scale=1.0):
    acc = F32(TAPS[0] * scale) * load(0)
    for k in range(1, HALO + 1):
        acc = acc + F32(TAPS[k] * scale) * (load(-k) + load(k))
    return acc


def eights(x):
    return sum((x[b : b + 8] for b in range(8, x.shape[0], 8)), x[:8])


def sublane_sums(x):
    half = x.shape[0] // 2
    x = x[:half] + x[half:]
    return x.reshape(half // 8, 8, LANES).sum(axis=1)


def chunks(start, stop, size=64):
    return [(a, min(size, stop - a)) for a in range(start, stop, size)]


def edges_kernel(cov_ref, fog_rows_ref, fog_cols_ref, edge_ref, first_ref, second_ref, fog_r, fog_c, tile, strips, sems):
    rows, cols = cov_ref.shape
    tiles = cols // LANES
    odd = lax.rem(lax.axis_index("row"), 2)
    over = pl.ds(pl.multiple_of((1 - lax.axis_index("col")) * (cols - LANES), LANES), LANES)
    copies = [pltpu.make_async_copy(cov_ref.at[:, over], tile, sems.at[0])]
    for i, start in enumerate((1 - odd, odd)):
        span = pl.ds(pl.multiple_of(start * (rows - EDGE), EDGE), EDGE)
        copies.append(pltpu.make_async_copy(cov_ref.at[span], strips.at[i], sems.at[1 + i]))
    copies.append(pltpu.make_async_copy(fog_rows_ref, fog_r, sems.at[3]))
    copies.append(pltpu.make_async_copy(fog_cols_ref, fog_c, sems.at[4]))
    for copy in copies:
        copy.start()
    for copy in copies:
        copy.wait()
    edge_ref[:rows, :] = tile[...].astype(F32)
    for i, start in enumerate((1 - odd, odd)):
        span = pl.ds(pl.multiple_of(start * (rows - EDGE), EDGE), EDGE)
        edge_ref[rows + i * EDGE : rows + (i + 1) * EDGE, :] = tile[span, :].astype(F32)
    for t in range(tiles):
        first_ref[t] = strips[0, :, t * LANES : (t + 1) * LANES].astype(F32)
        second_ref[t] = strips[1, :, t * LANES : (t + 1) * LANES].astype(F32)


def prep_kernel(fog_rows_ref, fog_cols_ref, band_ref, fold_ref, left_ref, own_ref, right_ref):
    tap = tap_of(jnp.abs(iota((2 * LANES, LANES), 0) - HALF - iota((2 * LANES, LANES), 1)))
    band_ref[:, :LANES], band_ref[:, LANES:] = halves(tap)
    for t in range(0, fold_ref.shape[0], LANES):
        group = (iota((LANES, LANES), 0) + t) // BS
        fold_ref[t : t + LANES, :] = (group == iota((LANES, LANES), 1)).astype(F32).astype(BF16)
    place = lax.axis_index("row") * (left_ref.shape[0] // lax.axis_size("row"))
    prep(place, fog_rows_ref[...], fog_cols_ref[...], left_ref, own_ref, right_ref)


def block_kernel(cov_ref, side_ref, band_ref, fold_ref, cover_ref, fine_ref, across, sums_ref, window, parts):
    rows, cols = cov_ref.shape
    tiles = cols // LANES
    part = 2 * BS
    pieces = rows // part
    cells = rows // BS
    lane = iota((1, LANES), 1)
    touches = (lane < HALF) == (lax.axis_index("col") == 0)
    c_rows, f_rows = 8 * cells, 8 * (cells + 2)

    def keep(base, height, low, span, values):
        for half, value in zip(range(2), halves(jnp.concatenate(values, axis=0))):
            at = base + half * height + low
            parts[at : at + 8 * len(values), span] = value

    for p in range(pieces):
        first = p * part
        at = slice(EDGE + first, EDGE + first + part)

        def put(t, value):
            window[t] = value
            if t == 0:
                window[tiles + 1] = value

        side = jnp.where(touches, side_ref[first : first + part, :], 0.0)
        cover_ref[tiles, at, :] = side
        side = pltpu.roll(side, HALF, 1)
        before = side
        for t in range(tiles):
            span = slice(t * LANES, (t + 1) * LANES)
            value = cov_ref[first : first + part, span].astype(F32)
            cover_ref[t, at, :] = value
            here = pltpu.roll(value, HALF, 1)
            put(t, jnp.where(lane < HALF, before, here).astype(BF16))
            before = here
            keep(0, c_rows, 8 * (first // BS), span, [eights(value[i : i + BS]) for i in range(0, part, BS)])
        put(tiles, jnp.where(lane < HALF, before, side).astype(BF16))
        for t, count in chunks(0, tiles + 1, 6):
            some = [jnp.concatenate([window[t + i], window[t + i + 1]], axis=1) for i in range(count)]
            both = jnp.dot(jnp.concatenate(some, axis=0), band_ref[...], preferred_element_type=F32)
            for i in range(count):
                mine = both[i * part : (i + 1) * part]
                across[t + i, PAD + EDGE + first : PAD + EDGE + first + part, :] = mine[:, :LANES] + mine[:, LANES:]
        ready = range(max(2 * p - 1, 0), 2 * p + 1 if p + 1 < pieces else cells)
        for t in range(tiles + 1):
            got = {}
            for i in ready:
                low, high = max(i * BS, 8), min((i + 1) * BS, rows - 8)
                base = PAD + EDGE + low
                fine = row_blur(lambda k: across[t, base + k : base + k + high - low, :])
                fine_ref[t, EDGE + low : EDGE + high, :] = fine
                if t < tiles:
                    got[i] = eights(cover_ref[t, EDGE + low : EDGE + high, :] * fine)
            if t < tiles:
                span = slice(t * LANES, (t + 1) * LANES)
                zero = jnp.zeros((8, LANES), F32)
                for i in got:
                    if i % 2 or i == 0:
                        pair = [got[i], got.get(i + 1, zero)] if i else [got[0], zero]
                        keep(2 * c_rows, f_rows, 8 * (i + 1) if i else 0, span, pair)
    def folded(some, step):
        return sum(
            jnp.dot(parts[some, a : a + step], fold_ref[a : a + step, :], preferred_element_type=F32)
            for a in range(0, cols, step)
        )

    c = sublane_sums(folded(slice(0, 2 * c_rows), cols))
    f = sublane_sums(folded(slice(2 * c_rows, 2 * c_rows + 2 * f_rows), 4 * LANES))
    sums_ref[...] = c + pltpu.roll(jnp.concatenate([f[:1], f[2 : cells + 1]], axis=0), HALF, 1)


def outer_kernel(first_ref, second_ref, band_ref, fold_ref, across_ref, part_ref, cover_in, fine_in, cover_ref, fine_ref, sums_ref, across, window, f_parts):
    tiles = cover_ref.shape[0] - 1
    ext = cover_ref.shape[1]
    rows = ext - 2 * EDGE
    even = lax.rem(lax.axis_index("row"), 2) == 0
    lane = iota((1, LANES), 1)
    cells = rows // BS
    both = 2 * EDGE
    touches = (lane < HALF) == (lax.axis_index("col") == 0)
    place = lax.axis_index("row")
    alone = (place == 0) | (place == lax.axis_size("row") - 1)

    def halo(t):
        a, b = first_ref[t], second_ref[t]
        if t == tiles:
            a, b = jnp.where(touches, a, 0.0), jnp.where(touches, b, 0.0)
        b = jnp.where(alone, 0.0, b)
        top = jnp.where(even, b, a)
        low = jnp.where(even, a, b)
        cover_ref[t, 0:EDGE, :] = top
        cover_ref[t, EDGE + rows :, :] = low
        return pltpu.roll(jnp.concatenate([top, low], axis=0), HALF, 1)

    before = halo(tiles)
    first = before
    for t in range(tiles + 1):
        here = halo(t) if t < tiles else first
        tile = jnp.where(lane < HALF, before, here).astype(BF16)
        window[t * both : (t + 1) * both, :LANES] = tile
        at = t - 1 if t else tiles
        window[at * both : (at + 1) * both, LANES:] = tile
        before = here
    twice = jnp.dot(window[...], band_ref[...], preferred_element_type=F32)
    once = twice[:, :LANES] + twice[:, LANES:]
    reach = 2 * PAD + 2 * EDGE
    for t in range(tiles + 1):
        across[t, 0:PAD, :] = jnp.zeros((PAD, LANES), F32)
        across[t, PAD : PAD + EDGE, :] = once[t * both : t * both + EDGE]
        across[t, PAD + EDGE : reach, :] = across_ref[t, PAD + EDGE : reach, :]
        low = reach
        across[t, low : low + PAD + EDGE, :] = across_ref[t, ext - PAD - EDGE : ext, :]
        across[t, low + PAD + EDGE : low + PAD + 2 * EDGE, :] = once[t * both + EDGE : (t + 1) * both]
        across[t, low + PAD + 2 * EDGE :, :] = jnp.zeros((PAD, LANES), F32)
        top = row_blur(lambda k: across[t, PAD + k : PAD + k + EDGE + 8, :])
        base = low + 8
        bot = row_blur(lambda k: across[t, base + k : base + k + EDGE + 8, :])
        fine_ref[t, 0 : EDGE + 8, :] = top
        fine_ref[t, EDGE + rows - 8 :, :] = bot
        if t < tiles:
            a = top[EDGE:] * cover_ref[t, EDGE : EDGE + 8, :]
            b = bot[:8] * cover_ref[t, EDGE + rows - 8 : EDGE + rows, :]
            span = slice(t * LANES, (t + 1) * LANES)
            f_parts[:16, span], f_parts[16:, span] = halves(jnp.concatenate([a, b], axis=0))
    f = sublane_sums(jnp.dot(f_parts[...], fold_ref[...], preferred_element_type=F32))
    row = iota((cells, LANES), 0)
    total = jnp.where(row == 0, f[0:1], jnp.where(row == cells - 1, f[1:2], 0.0))
    sums_ref[...] = part_ref[...] + pltpu.roll(total, HALF, 1)


def spread_kernel(cover_ref, after_ref, blurred_ref, above_ref, below_ref):
    del after_ref
    tiles, ext = cover_ref.shape[0] - 1, cover_ref.shape[1]
    rows = ext - 2 * EDGE
    scale = 0.5 / 255.0
    row = iota((8, LANES), 0)
    for t in range(tiles + 1):
        for a, n in chunks(0, rows):
            blurred_ref[t, a : a + n, :] = row_blur(lambda k: cover_ref[t, EDGE + a + k : EDGE + a + k + n, :], scale)
        for i in range(rows // BS):
            top = EDGE + i * BS
            low = top + BS - 8
            above = jnp.zeros((8, LANES), F32)
            below = jnp.zeros((8, LANES), F32)
            for k in range(1, HALO + 1):
                tap = F32(TAPS[k] * scale)
                above = above + jnp.where(row < k, tap * cover_ref[t, top - k : top - k + 8, :], 0.0)
                below = below + jnp.where(row >= 8 - k, tap * cover_ref[t, low + k : low + k + 8, :], 0.0)
            above_ref[t, i] = above
            below_ref[t, i] = below


def first_dose_kernel(cover_ref, fine_ref, after_ref, dose_ref, blurred_ref, charge):
    del after_ref
    tiles, ext = cover_ref.shape[0] - 1, cover_ref.shape[1]
    rows = ext - 2 * EDGE
    for t in range(tiles + 1):
        for a, n in [(0, EDGE)] + [(EDGE + a, n) for a, n in chunks(0, rows)] + [(EDGE + rows, EDGE)]:
            dose = 2.0 - F32(0.5 / 255.0) * fine_ref[t, a : a + n, :]
            if t < tiles and EDGE <= a < EDGE + rows:
                dose_ref[t, a - EDGE : a - EDGE + n, :] = dose
            charge[t, a : a + n, :] = (dose - 0.5) * cover_ref[t, a : a + n, :]
        for a, n in chunks(0, rows):
            blurred_ref[t, a : a + n, :] = row_blur(
                lambda k: charge[t, EDGE + a + k : EDGE + a + k + n, :], 0.5 / 255.0
            )


def last_kernel(gathered_ref, left_ref, own_ref, right_ref, band_ref, dose_ref, charge_ref, blurred_ref, above_ref, below_ref, out_ref, c_all, f_all, ring_ref, last_ref, window, turned, ends, staged, sems):
    rows, cols = out_ref.shape
    tiles = cols // LANES
    n_rows, n_cols = c_all.shape
    cells = rows // BS
    col = lax.axis_index("col")
    row = lax.axis_index("row")
    lane8 = iota((cells, LANES), 1)
    lane = iota((1, LANES), 1)
    count = n_rows // cells
    for j in range(count):
        mine = gathered_ref[j * cells : (j + 1) * cells, :]
        other = gathered_ref[(count + j) * cells : (count + j + 1) * cells, :]
        here = col == bin(j).count("1") % 2
        low = jnp.where(here, mine, other)
        high = jnp.where(here, other, mine)
        at = pl.ds(pl.multiple_of((row ^ j) * cells, cells), cells)
        c_all[at, :] = jnp.where(lane8 < HALF, low, pltpu.roll(high, HALF, 1)) * F32(1.0 / (255.0 * BS * BS))
        f_all[at, :] = jnp.where(lane8 < HALF, pltpu.roll(low, HALF, 1), high) * F32(1.0 / (255.0 * 255.0 * BS * BS))
    right = right_ref[...]

    def both(x):
        part = dot(x, right)
        return jnp.concatenate([part[:, :n_cols], part[:, n_cols:]], axis=0)

    c = c_all[...]
    spread = both(c)
    ring_ref[...] = dot(own_ref[...], spread)
    coarse = dot(left_ref[...], spread)
    back = (1.5 - coarse) * c - 0.5 * f_all[...]
    last_ref[...] = dot(own_ref[...], both(back))

    ring = ring_ref.shape[0]

    def expand(ref, t):
        if t < tiles:
            pick = iota((ring, LANES), 1) // BS + (col * (cols // BS) + t * (LANES // BS))
        else:
            pick = jnp.where(iota((ring, LANES), 1) < HALF, (col + 1) * (cols // BS), col * (cols // BS) - 1)
        pick = jnp.clip(pick, 0, n_cols - 1)
        parts = [jnp.take_along_axis(ref[i : i + 8, :], pick[i : i + 8], axis=1) for i in range(0, ring, 8)]
        return jnp.concatenate(parts, axis=0)

    def charge(t):
        value = expand(ring_ref, t)
        for i in range(cells):
            here = value[1 + i : 2 + i, :]
            up = value[i : 1 + i, :] - here
            down = value[2 + i : 3 + i, :] - here
            at = i * BS
            some = charge_ref[t, at : at + BS, :] - here * blurred_ref[t, at : at + BS, :]
            some = jnp.concatenate(
                [some[:8] - up * above_ref[t, i], some[8 : BS - 8], some[BS - 8 :] - down * below_ref[t, i]], axis=0
            )
            turned[t % 2, at : at + BS, :] = pltpu.roll(some, HALF, 1)

    def put(t, at, value):
        for i, part in enumerate(halves(value)):
            if t < tiles:
                window[t, at, 2 * i * LANES : (2 * i + 1) * LANES] = part
            if t:
                window[t - 1, at, (2 * i + 1) * LANES : (2 * i + 2) * LANES] = part

    def fill(t):
        if t < tiles:
            charge(t)
        for a, n in chunks(0, rows):
            at = slice(a, a + n)
            before = turned[(t - 1) % 2, at, :] if t else ends[at, :]
            here = turned[t % 2, at, :] if t < tiles else ends[at, :]
            put(t, at, jnp.where(lane < HALF, before, here))

    def copy(g):
        span = slice(2 * g * LANES, 2 * (g + 1) * LANES)
        return pltpu.make_async_copy(staged.at[:, span], out_ref.at[:, span], sems.at[g])

    def finish(g):
        part = window[4 * g : 4 * g + 4].reshape(4 * rows, 4 * LANES)
        band = band_ref[...]
        both = jnp.dot(part, jnp.concatenate([band, band], axis=0), preferred_element_type=F32)
        for t in range(4 * g, 4 * g + 4):
            fine = both[(t % 4) * rows : (t % 4 + 1) * rows]
            coarse = expand(ring_ref, t)[1 : 1 + cells] + expand(last_ref, t)[1 : 1 + cells]
            for i in range(cells):
                at = slice(i * BS, (i + 1) * BS)
                value = dose_ref[t, at, :] - fine[at, :LANES] - fine[at, LANES:] - coarse[i : i + 1, :]
                staged[at, t * LANES : (t + 1) * LANES] = value
            if t % 2:
                copy(t // 2).start()

    def stage(body):
        body()

    def start():
        charge(tiles)
        ends[...] = turned[tiles % 2]
        for t in range(3):
            fill(t)

    stage(start)
    for t in range(3, 5):
        fill(t)
    for g in range(tiles // 4):
        for t in range(4 * g + 5, min(4 * g + 9, tiles + 1)):
            fill(t)
        finish(g)
    for g in range(tiles // 2):
        copy(g).wait()


def shards(coverage, fog_rows, fog_cols):
    rows, cols = coverage.shape
    row_count = lax.axis_size("row")
    col_count = lax.axis_size("col")
    tiles = cols // LANES
    back_rows, back_cols = rows // BS, cols // BS
    n_rows, n_cols = back_rows * row_count, back_cols * col_count
    ext = rows + 2 * EDGE
    if col_count != 2 or n_cols != LANES or row_count & (row_count - 1):
        raise ValueError("unsupported mesh")

    def move(value, target):
        both = [(r, c) for r in range(row_count) for c in range(col_count)]
        flat = [(r * col_count + c, target(r, c)) for r, c in both]
        return lax.ppermute(value, ("row", "col"), [(i, r * col_count + c) for i, (r, c) in flat])

    def shape(*dims, dtype=F32):
        return jax.ShapeDtypeStruct(dims, dtype)

    def call(kernel, outs, ins, *args, scratch=(), mib=16, name=None, aliases={}, ops=1):
        return pl.pallas_call(
            kernel,
            out_shape=outs,
            in_specs=ins,
            out_specs=(VMEM,) * len(outs),
            scratch_shapes=list(scratch),
            input_output_aliases=aliases,
            compiler_params=pltpu.CompilerParams(vmem_limit_bytes=mib << 20),
            cost_estimate=pl.CostEstimate(flops=ops * rows * cols, bytes_accessed=ops * rows * cols, transcendentals=0),
            name=name,
        )(*args)

    wide = shape(tiles + 1, ext, LANES)
    own_tiles = shape(tiles + 1, rows, LANES)
    hbm = pl.BlockSpec(memory_space=pltpu.HBM)
    edge, first_rows, second_rows, fog_r, fog_c = call(
        edges_kernel,
        (
            shape(ext, LANES),
            shape(tiles, EDGE, LANES),
            shape(tiles, EDGE, LANES),
            shape(*fog_rows.shape),
            shape(*fog_cols.shape),
        ),
        [hbm] * 3,
        *[pltpu.with_memory_space_constraint(x, pltpu.HBM) for x in (coverage, fog_rows, fog_cols)],
        scratch=[
            pltpu.VMEM((rows, LANES), jnp.int32),
            pltpu.VMEM((2, EDGE, cols), jnp.int32),
            pltpu.SemaphoreType.DMA((5,)),
        ],
        mib=2,
        name="edges",
    )

    side = move(edge, lambda r, c: (r, 1 - c))
    band, fold, left, own, right = call(
        prep_kernel,
        (
            shape(2 * LANES, 2 * LANES, dtype=BF16),
            shape(cols, LANES, dtype=BF16),
            shape(n_rows, 2 * n_rows),
            shape(16, 2 * n_rows),
            shape(n_cols, 2 * n_cols),
        ),
        [VMEM] * 2,
        fog_r,
        fog_c,
        mib=4,
        name="prep",
    )
    side, band = lax.optimization_barrier((side, band))
    corners = side[rows:].reshape(2, EDGE, LANES)

    first = move(jnp.concatenate([first_rows, corners[:1]], axis=0), lambda r, c: (r ^ 1, c))
    second = move(
        jnp.concatenate([second_rows, corners[1:]], axis=0),
        lambda r, c: (r, 1 - c) if r in (0, row_count - 1) else ((r + 1, c) if r % 2 else (r - 1, c)),
    )
    cover, fine, across, part = call(
        block_kernel,
        (
            wide,
            wide,
            shape(tiles + 1, ext + 2 * PAD, LANES),
            shape(back_rows, LANES),
        ),
        [VMEM] * 4,
        coverage,
        side,
        band,
        fold,
        scratch=[
            pltpu.VMEM((tiles + 2, 2 * BS, LANES), BF16),
            pltpu.VMEM((32 * (back_rows + 1), cols), BF16),
        ],
        mib=8,
        name="block",
    )
    cover, fine, sums = call(
        outer_kernel,
        (wide, wide, shape(back_rows, LANES)),
        [VMEM] * 8,
        first,
        second,
        band,
        fold,
        across,
        part,
        cover,
        fine,
        scratch=[
            pltpu.VMEM((tiles + 1, 4 * PAD + 4 * EDGE, LANES), F32),
            pltpu.VMEM(((tiles + 1) * 2 * EDGE, 2 * LANES), BF16),
            pltpu.VMEM((32, cols), BF16),
        ],
        aliases={6: 0, 7: 1},
        mib=8,
        name="outer",
    )

    few = shape(tiles + 1, back_rows, 8, LANES)

    def spread(after):
        return call(
            spread_kernel, (own_tiles, few, few), [VMEM] * 2, cover, after, mib=4, name="spread"
        )

    def first_dose(after):
        return call(
            first_dose_kernel,
            (shape(tiles, rows, LANES), own_tiles),
            [VMEM] * 3,
            cover,
            fine,
            after,
            scratch=[pltpu.VMEM((tiles + 1, ext, LANES), F32)],
            mib=8,
            name="dose",
        )

    pending = [spread, first_dose]
    done = []
    gathered = sums
    bit = 1
    while bit < row_count:
        other = move(gathered, lambda r, c: (r ^ bit, 1 - c))
        if pending:
            results = pending.pop(0)(gathered)
            other, *results = lax.optimization_barrier((other, *results))
            done += results
        gathered = jnp.concatenate([gathered, other], axis=0)
        bit *= 2
    gathered = jnp.concatenate([gathered, move(gathered, lambda r, c: (r, 1 - c))], axis=0)
    for work in pending:
        done += work(gathered)
    blurred, above, below, dose, charge = done

    return pl.pallas_call(
        last_kernel,
        out_shape=shape(rows, cols),
        in_specs=[VMEM] * 10,
        out_specs=pl.BlockSpec(memory_space=pltpu.HBM),
        scratch_shapes=[
            pltpu.VMEM((n_rows, n_cols), F32),
            pltpu.VMEM((n_rows, n_cols), F32),
            pltpu.VMEM((16, n_cols), F32),
            pltpu.VMEM((16, n_cols), F32),
            pltpu.VMEM((tiles, rows, 4 * LANES), BF16),
            pltpu.VMEM((2, rows, LANES), F32),
            pltpu.VMEM((rows, LANES), F32),
            pltpu.VMEM((rows, cols), F32),
            pltpu.SemaphoreType.DMA((tiles // 2,)),
        ],
        compiler_params=pltpu.CompilerParams(vmem_limit_bytes=16 << 20),
        name="last",
    )(gathered, left, own, right, band, dose, charge, blurred, above, below)


def solution(mesh):
    in_specs = (P(("stripe", "row"), "col"), P(), P())
    out_specs = P(("stripe", "row"), "col")
    return jax.shard_map(shards, mesh=mesh, in_specs=in_specs, out_specs=out_specs, check_vma=False)
```
